32 devices in a mesh: dp: 8 (over z, x), tensor: 4 (over y, core).
Axes of the slice: x: 2, y: 2, z: 4, core: 2. Of those that a mesh axis runs over, the one named last changes fastest.
Arguments:
- tokens: bfloat16 [2560, 2048], P(('dp', 'tensor')), may hold values from -6 to 6
- segment_ids: int32 [2560], replicated, may hold values from 0 to 39, as said below
- key_mask: int32 [2560], replicated, may hold values 0 or 1
- attn_gain: float32 [2048], P(('dp', 'tensor')), may hold values from 0.1 to 1.9
- w_query: bfloat16 [2048, 2048], P('dp', 'tensor'), may hold values from -0.125 to 0.125
- w_key: bfloat16 [2048, 256], P('dp', 'tensor'), may hold values from -0.125 to 0.125
- w_value: bfloat16 [2048, 256], P('dp', 'tensor'), may hold values from -0.125 to 0.125
- w_out: bfloat16 [2048, 2048], P('tensor', 'dp'), may hold values from -0.75 to 0.75
- mlp_gain: float32 [2048], P(('dp', 'tensor')), may hold values from 0.1 to 1.9
- w_gate: bfloat16 [2048, 5632], P('dp', 'tensor'), may hold values from -0.125 to 0.125
- w_up: bfloat16 [2048, 5632], P('dp', 'tensor'), may hold values from -0.125 to 0.125
- w_down: bfloat16 [5632, 2048], P('tensor', 'dp'), may hold values from -0.078125 to 0.078125
- cotangent: bfloat16 [2560, 2048], P(('dp', 'tensor')), may hold values from -6 to 6
Outputs:
- layer_out: bfloat16 [2560, 2048], P(('dp', 'tensor'))
- input_grad: float32 [2560, 2048], P(('dp', 'tensor'))
- grad_attn_gain: float32 [2048], P(('dp', 'tensor'))
- grad_query: float32 [2048, 2048], P('dp', 'tensor')
- grad_key: float32 [2048, 256], P('dp', 'tensor')
- grad_value: float32 [2048, 256], P('dp', 'tensor')
- grad_out: float32 [2048, 2048], P('tensor', 'dp')
- grad_mlp_gain: float32 [2048], P(('dp', 'tensor'))
- grad_gate: float32 [2048, 5632], P('dp', 'tensor')
- grad_up: float32 [2048, 5632], P('dp', 'tensor')
- grad_down: float32 [5632, 2048], P('tensor', 'dp')
The draws below stay inside these ranges and needn't reach their ends.
Inputs may be any that keep to these rules, and one draw needn't show every extreme that they name: `segment_ids`: segment ids never fall from one token to the next; equal ids form one document; documents start only at positions that are multiples of 16, and there are exactly 40 of them; one document holds exactly 1600 tokens and starts at 0 or at a position of at most 64.
All inputs are finite; a program needn't handle non-finite values.
Results may differ from the reference program's by a relative error of at most 0.019.
Values may be sent and summed in bfloat16 or wider, within the bound.
A program may use at most 192 MiB of HBM per device.

```python
import jax
import jax.numpy as jnp
from jax import lax

D = 2048
HEADS = 32
KV_HEADS = 4
HEAD_DIM = 64
FF = 5632
TOKENS = 2560


def draw_segment_ids(key, part):
    base_key = jax.random.fold_in(key, 7919)
    class_key = jax.random.fold_in(base_key, 11)
    order_key = jax.random.fold_in(base_key, 23)
    start_key = jax.random.fold_in(base_key, 37)
    candidates = TOKENS // 16
    starts_wanted = TOKENS // 64
    long_span = 5 * candidates // 8
    long_start = jax.random.randint(start_key, (), 0, max(1, candidates // 32), dtype=jnp.int32)
    slot_index = jnp.arange(candidates, dtype=jnp.int32)
    class_rows = jax.random.randint(class_key, (candidates,), 0, 4, dtype=jnp.int32)
    order_values = jax.random.permutation(order_key, candidates).astype(jnp.int32)
    inside = (slot_index > long_start) & (slot_index < long_start + long_span)
    needed = (slot_index == 0) | (slot_index == long_start) | (slot_index == long_start + long_span)
    priority = jnp.where(needed, 8, jnp.where(inside, 0, 6 - class_rows))
    scores = priority * candidates + order_values
    ranked = jnp.argsort(-scores, stable=True).astype(jnp.int32)
    chosen = ranked[:starts_wanted]
    marks = jnp.zeros((candidates,), jnp.int32).at[chosen].set(1)
    starts = jnp.zeros((candidates, 16), jnp.int32).at[:, 0].set(marks).reshape(TOKENS)
    return (jnp.cumsum(starts) - 1).astype(jnp.int32)


def place_ends(values, key, smallest, largest):
    dims = values.shape
    index_at = [jax.random.randint(jax.random.fold_in(key, axis), (), 0, dims[axis]) for axis in range(len(dims))]
    values = values.at[tuple(index_at)].set(smallest)
    longest = dims.index(max(dims))
    index_at[longest] = (index_at[longest] + 1) % dims[longest]
    return values.at[tuple(index_at)].set(largest)


def levels(own_key, extent, split, low, top_value):
    factor_of = 1.0
    for position, blocks in split:
        draws = jax.random.uniform(jax.random.fold_in(jax.random.fold_in(own_key, 6), position), (blocks,), jnp.float32, low / len(split), top_value / len(split))
        factor_of = factor_of * jnp.repeat(jnp.exp(draws), extent[position] // blocks).reshape((-1,) + (1,) * (len(extent) - 1 - position))
    return factor_of


def gaussian(key, extent, scale, reach, cuts=(), held_as=jnp.bfloat16):
    entries = scale * jax.random.normal(key, extent, jnp.float32)
    if cuts:
        entries = entries * levels(key, extent, cuts, -0.22, 0.18)
    return jnp.clip(entries, -reach, reach).astype(held_as)


def setup_inputs(seed: int = 0) -> dict:
    seeds = jax.random.split(jax.random.key(seed), 14)
    return {
        "tokens": gaussian(seeds[0], (TOKENS, D), 1.0, 6.0, ((0, 32),)),
        "segment_ids": draw_segment_ids(jax.random.fold_in(seeds[13], 71), 0),
        "key_mask": place_ends((jax.random.randint(seeds[2], (TOKENS,), 0, 8) < 7).astype(jnp.int32), jax.random.fold_in(seeds[2], 1), 0, 1),
        "attn_gain": jnp.clip(1.0 + 0.18 * jax.random.normal(seeds[3], (D,), jnp.float32), 0.1, 1.9),
        "w_query": gaussian(seeds[4], (D, HEADS * HEAD_DIM), D ** -0.5, 0.125, ((0, 8), (1, 4))),
        "w_key": gaussian(seeds[5], (D, KV_HEADS * HEAD_DIM), D ** -0.5, 0.125, ((0, 8), (1, 4))),
        "w_value": gaussian(seeds[6], (D, KV_HEADS * HEAD_DIM), D ** -0.5, 0.125, ((0, 8), (1, 4))),
        "w_out": gaussian(seeds[7], (HEADS * HEAD_DIM, D), (HEADS * HEAD_DIM // 32) ** -0.5, 0.75, ((0, 4), (1, 8))),
        "mlp_gain": jnp.clip(1.0 + 0.18 * jax.random.normal(seeds[8], (D,), jnp.float32), 0.1, 1.9),
        "w_gate": gaussian(seeds[9], (D, FF), D ** -0.5, 0.125, ((0, 8), (1, 4))),
        "w_up": gaussian(seeds[10], (D, FF), D ** -0.5, 0.125, ((0, 8), (1, 4))),
        "w_down": gaussian(seeds[11], (FF, D), FF ** -0.5, 0.078125, ((0, 4), (1, 8))),
        "cotangent": gaussian(seeds[12], (TOKENS, D), 1.0, 6.0, ((0, 32),)),
    }


EPS = 1e-05
NEG = -1e+30
THETA = 10000.0
HIGHEST = lax.Precision.HIGHEST

@jax.custom_vjp
def low(v):
    return lax.optimization_barrier(v.astype(jnp.bfloat16)).astype(jnp.float32)

@jax.custom_vjp
def low_back(v):
    return v

def low_keep(v):
    return (low(v), None)

def low_pass(kept, grad):
    return (grad,)

def back_keep(v):
    return (v, None)

def back_low(kept, grad):
    return (low(grad),)
low.defvjp(low_keep, low_pass)
low_back.defvjp(back_keep, back_low)

def normalize(values, scaling):
    return values * lax.rsqrt(lax.optimization_barrier(jnp.mean(values * values, axis=-1, keepdims=True)) + EPS) * scaling

def angles(positions, half_dim):
    frequency = THETA ** (-jnp.arange(half_dim, dtype=jnp.float32) / half_dim)
    turned = positions.astype(jnp.float32)[:, None] * frequency[None, :]
    return (jnp.cos(turned), jnp.sin(turned))

def rotate(values, cosine_table, sine_table):
    half_dim = values.shape[-1] // 2
    front_half = values[..., :half_dim]
    back_half = values[..., half_dim:]
    cosine_rows = cosine_table[:, None, :]
    sine_rows = sine_table[:, None, :]
    return jnp.concatenate([front_half * cosine_rows - back_half * sine_rows, back_half * cosine_rows + front_half * sine_rows], axis=-1)

def product(left_rows, right_rows):
    return jnp.dot(left_rows, right_rows, precision=HIGHEST)

def attend(queries, key_rows, value_rows, segment_ids, key_mask):
    group_size = HEADS // KV_HEADS
    block_len = min(128, TOKENS)
    score_scale = HEAD_DIM ** (-0.5)
    query_blocks = queries.reshape(TOKENS // block_len, block_len, KV_HEADS, group_size, HEAD_DIM)
    key_index = jnp.arange(TOKENS, dtype=jnp.int32)

    def one_block(operands):
        query_block, block_start = operands
        query_index = block_start + jnp.arange(block_len, dtype=jnp.int32)
        query_segment = lax.dynamic_slice(segment_ids, (block_start,), (block_len,))
        raw_scores = jnp.einsum('qkgd,skd->kgqs', query_block, key_rows, precision=HIGHEST) * score_scale
        scores = low_back(raw_scores)
        allowed = (query_segment[:, None] == segment_ids[None, :]) & (key_index[None, :] <= query_index[:, None]) & ((key_mask[None, :] == 1) | (key_index[None, :] == query_index[:, None]))
        scores = jnp.where(allowed, scores, NEG)
        weights = low(jax.nn.softmax(scores, axis=-1))
        mixed_rows = jnp.einsum('kgqs,skd->qkgd', weights, value_rows, precision=HIGHEST)
        return mixed_rows.reshape(block_len, HEADS * HEAD_DIM)
    starts = jnp.arange(TOKENS // block_len, dtype=jnp.int32) * block_len
    outputs = lax.map(jax.checkpoint(one_block), (query_blocks, starts))
    return outputs.reshape(TOKENS, HEADS * HEAD_DIM)

def layer_forward(tokens, attn_gain, w_query, w_key, w_value, w_out, mlp_gain, w_gate, w_up, w_down, segment_ids, key_mask, cosine_table, sine_table):
    token_count = tokens.shape[0]
    normed = low(normalize(tokens, attn_gain))
    queries = low_back(product(normed, w_query)).reshape(token_count, HEADS, HEAD_DIM)
    key_rows = low_back(product(normed, w_key)).reshape(token_count, KV_HEADS, HEAD_DIM)
    value_rows = low(low_back(product(normed, w_value))).reshape(token_count, KV_HEADS, HEAD_DIM)
    queries = low(rotate(queries, cosine_table, sine_table))
    key_rows = low(rotate(key_rows, cosine_table, sine_table))
    mixed_rows = low(low_back(attend(queries, key_rows, value_rows, segment_ids, key_mask)))
    middle = tokens + low_back(product(mixed_rows, w_out))
    normed_two = low(normalize(middle, mlp_gain))
    gate_proj = low_back(product(normed_two, w_gate))
    upward = low_back(product(normed_two, w_up))
    hidden = low(jax.nn.silu(gate_proj) * upward)
    return middle + low_back(product(hidden, w_down))

def reference(tokens, segment_ids, key_mask, attn_gain, w_query, w_key, w_value, w_out, mlp_gain, w_gate, w_up, w_down, cotangent):
    cosine_table, sine_table = angles(jnp.arange(TOKENS, dtype=jnp.int32), HEAD_DIM // 2)

    def forward(tokens_f, attn_f, query_f, key_f, value_f, out_f, mlp_f, gate_f, up_f, down_f):
        return layer_forward(tokens_f, attn_f, query_f, key_f, value_f, out_f, mlp_f, gate_f, up_f, down_f, segment_ids, key_mask, cosine_table, sine_table)
    result, pullback = jax.vjp(forward, tokens.astype(jnp.float32), attn_gain.astype(jnp.float32), w_query.astype(jnp.float32), w_key.astype(jnp.float32), w_value.astype(jnp.float32), w_out.astype(jnp.float32), mlp_gain.astype(jnp.float32), w_gate.astype(jnp.float32), w_up.astype(jnp.float32), w_down.astype(jnp.float32))
    grads = pullback(cotangent.astype(jnp.float32))
    return (result.astype(jnp.bfloat16), grads[0], grads[1], grads[2], grads[3], grads[4], grads[5], grads[6], grads[7], grads[8], grads[9])
```

```python
import functools

import jax
import jax.numpy as jnp
from jax import lax
from jax.experimental import pallas as pl
from jax.experimental.pallas import tpu as pltpu
from jax.sharding import PartitionSpec as P

EPS = 1e-05
NEG = -1e30
THETA = 10000.0
BF = jnp.bfloat16
F32 = jnp.float32
MESH = pl.DeviceIdType.MESH
ANY = pl.BlockSpec(memory_space=pl.ANY)
VM = pl.BlockSpec(memory_space=pltpu.VMEM)


def sem_count():
    return 128 + 8 * lax.axis_size("dp")


class Sems:
    def __init__(self, send, recv):
        self.send, self.recv, self.used = send, recv, 0

    def take(self, count):
        base = self.used
        self.used += count
        assert self.used <= sem_count()
        return base


class Place:
    def __init__(self, chain):
        self.n_dp = lax.axis_size("dp")
        self.n_t = lax.axis_size("tensor")
        self.chain = chain
        self.groups = self.n_dp // chain
        self.d = lax.axis_index("dp")
        self.s = lax.axis_index("tensor")
        self.z = self.d // self.groups
        self.t = self.d % self.groups
        self.y = self.s // 2
        self.c = self.s % 2
        self.sy = (1 - self.y) * 2 + self.c
        self.sc = self.y * 2 + 1 - self.c
        self.so = (1 - self.y) * 2 + 1 - self.c
        self.above = self.at(z=jnp.minimum(self.z + 1, chain - 1))
        self.below = self.at(z=jnp.maximum(self.z - 1, 0))

    def at(self, z=None, t=None, s=None):
        z = self.z if z is None else z
        t = self.t if t is None else t
        s = self.s if s is None else s
        return {"dp": z * self.groups + t, "tensor": s}


def when(pred, act):
    if pred is None:
        act()
    else:
        pl.when(pred)(act)


class Copies:
    def __init__(self, sems):
        self.sems = sems
        self.sent = []

    def go(self, i, src, dst, where, pred=None):
        copy = pltpu.make_async_remote_copy(
            src_ref=src,
            dst_ref=dst,
            send_sem=self.sems.send.at[i],
            recv_sem=self.sems.recv.at[i],
            device_id=where,
            device_id_type=MESH,
        )
        when(pred, copy.start)
        self.sent.append((copy, pred))

    def keep(self, i, src, dst):
        copy = pltpu.make_async_copy(src, dst, self.sems.send.at[i])
        copy.start()
        return copy

    def arrive(self, i, dst, where, pred=None):
        copy = pltpu.make_async_remote_copy(
            src_ref=dst,
            dst_ref=dst,
            send_sem=self.sems.send.at[i],
            recv_sem=self.sems.recv.at[i],
            device_id=where,
            device_id_type=MESH,
        )
        when(pred, copy.wait_recv)

    def finish(self):
        for copy, pred in self.sent:
            when(pred, copy.wait_send)


def greet(pc):
    barrier = pltpu.get_barrier_semaphore()
    for k in range(1, pc.n_dp):
        pl.semaphore_signal(
            barrier, inc=1, device_id={"dp": (pc.d + k) % pc.n_dp, "tensor": pc.s}, device_id_type=MESH
        )
    for k in range(1, pc.n_t):
        pl.semaphore_signal(
            barrier, inc=1, device_id={"dp": pc.d, "tensor": (pc.s + k) % pc.n_t}, device_id_type=MESH
        )
    pl.semaphore_wait(barrier, pc.n_dp + pc.n_t - 2)


def run(*tasks):
    live = list(tasks)
    while live:
        left = []
        for task in live:
            try:
                next(task)
                left.append(task)
            except StopIteration:
                pass
        live = left


def chain_steps(pc):
    chain, z = pc.chain, pc.z
    for k in range(chain - 1):
        for side in (0, 1):
            if side == 0:
                got = z - 1 - k >= 0
                yield k, side, jnp.maximum(z - 1 - k, 0), got, pc.above, jnp.logical_and(got, z + 1 < chain)
            else:
                got = z + 1 + k <= chain - 1
                yield k, side, jnp.minimum(z + 1 + k, chain - 1), got, pc.below, jnp.logical_and(got, z > 0)


def plane_gather(pc, sems, own, out, parts=1):
    chain, z, s = pc.chain, pc.z, pc.s
    width = own.shape[1] // parts
    cp = Copies(sems)
    base = sems.take(1 + 8 * chain * parts)

    def sem(kind, i, p):
        return base + 1 + (kind * chain + i) * parts + p

    def view(b, col, p):
        return out.at[b, col, :, pl.ds(p * width, width)]

    keep = cp.keep(base, own, out.at[z, s])
    for p in range(parts):
        src = own.at[:, pl.ds(p * width, width)]
        if chain > 1:
            cp.go(sem(0, 0, p), src, view(z, s, p), pc.above, z + 1 < chain)
            cp.go(sem(1, 0, p), src, view(z, s, p), pc.below, z > 0)
        cp.go(sem(2, 0, p), src, view(z, s, p), pc.at(s=pc.sy))
        cp.go(sem(4, 0, p), src, view(z, s, p), pc.at(s=pc.sc))
    yield
    crossing = [(z, None, 0, p) for p in range(parts)]
    landed = []

    def cross(count):
        for _ in range(min(count, len(crossing))):
            b, got, i, p = crossing.pop(0)
            cp.arrive(sem(2, i, p), view(b, pc.sy, p), pc.at(), got)
            cp.go(sem(6, i, p), view(b, pc.sy, p), view(b, pc.sy, p), pc.at(s=pc.sc), got)
            landed.append((b, got, i, p))

    steps = list(chain_steps(pc))
    for k in range(chain - 1):
        for p in range(parts):
            for step, side, b, got, onward, more in steps:
                if step != k:
                    continue
                i = 1 + k if side == 0 else chain + k
                cp.arrive(sem(side, k, p), view(b, s, p), pc.at(), got)
                if k < chain - 2:
                    cp.go(sem(side, k + 1, p), view(b, s, p), view(b, s, p), onward, more)
                cp.go(sem(2, i, p), view(b, s, p), view(b, s, p), pc.at(s=pc.sy), got)
                cp.go(sem(4, i, p), view(b, s, p), view(b, s, p), pc.at(s=pc.sc), got)
                crossing.append((b, got, i, p))
            cross(1 if k == 0 else 2)
            yield
    while crossing:
        cross(2)
        yield
    for b, got, i, p in landed:
        cp.arrive(sem(4, i, p), view(b, pc.sc, p), pc.at(), got)
        cp.arrive(sem(6, i, p), view(b, pc.so, p), pc.at(), got)
    keep.wait()
    cp.finish()
    yield


def far_first(chain, z, j):
    if j == chain - 1:
        return z
    up = jnp.where(j < chain - 1 - z, chain - 1 - j, j - (chain - 1 - z))
    down = jnp.where(j < z, j, chain - 1 - (j - z))
    return jnp.where(2 * z < chain, up, down)


def each_rows(count, fn, rows=16):
    def body(i, carry):
        fn(pl.ds(pl.multiple_of(i * rows, rows), rows))
        return carry

    lax.fori_loop(0, count // rows, body, 0)


def chain_reduce(pc, cp, right, left, b, last, value, zsend, lrecv, rrecv, store, rows, cols):
    chain, z = pc.chain, pc.z
    if not last:
        fromleft = jnp.logical_and(b > z, z > 0)
        fromright = jnp.logical_and(b < z, z < chain - 1)
        cp.arrive(right, lrecv.at[b, :, cols], pc.at(), fromleft)
        cp.arrive(left, rrecv.at[b, :, cols], pc.at(), fromright)

        @pl.when(fromleft)
        def _():
            def add(r):
                zsend[b, r, cols] = (value(r) + lrecv[b, r, cols].astype(F32)).astype(BF)

            each_rows(rows, add)

        @pl.when(fromright)
        def _():
            def add(r):
                zsend[b, r, cols] = (value(r) + rrecv[b, r, cols].astype(F32)).astype(BF)

            each_rows(rows, add)

        @pl.when(jnp.logical_not(jnp.logical_or(fromleft, fromright)))
        def _():
            def add(r):
                zsend[b, r, cols] = value(r).astype(BF)

            each_rows(rows, add)

        cp.go(right, zsend.at[b, :, cols], lrecv.at[b, :, cols], pc.above, b > z)
        cp.go(left, zsend.at[b, :, cols], rrecv.at[b, :, cols], pc.below, b < z)
        return

    def first(r):
        store(r, value(r), False)

    each_rows(rows, first)
    if chain > 1:

        @pl.when(z > 0)
        def _():
            cp.arrive(right, lrecv.at[b, :, cols], pc.at())

            def add(r):
                store(r, lrecv[b, r, cols].astype(F32), True)

            each_rows(rows, add)

        @pl.when(z < chain - 1)
        def _():
            cp.arrive(left, rrecv.at[b, :, cols], pc.at())

            def add(r):
                store(r, rrecv[b, r, cols].astype(F32), True)

            each_rows(rows, add)


def plane_scratch(chain, rows, width):
    return [
        pltpu.VMEM((chain, 2, rows, width), BF),
        pltpu.VMEM((chain, rows, width), BF),
        pltpu.VMEM((chain, rows, width), BF),
        pltpu.VMEM((chain, rows, width), BF),
        pltpu.VMEM((chain, rows, width), BF),
        pltpu.VMEM((chain, rows, width), BF),
    ]


def plane_reduce(pc, sems, part, scratch, out, parts=1):
    crecv, csum, yrecv, zsend, lrecv, rrecv = scratch
    chain, z = pc.chain, pc.z
    count = out.shape[0]
    width = out.shape[1] // parts
    cp = Copies(sems)
    base = sems.take(5 * chain * parts)

    def sem(kind, i, p):
        return base + (kind * chain + i) * parts + p

    todo = [(j, far_first(chain, z, j), p) for j in range(chain) for p in range(parts)]
    mine = pc.s

    def cols_of(p):
        return pl.ds(p * width, width)

    for j, b, p in todo:
        for over in (1, 0):
            col = pc.so if over else pc.sc
            cp.go(
                sem(over, j, p),
                part.at[b, col, :, cols_of(p)],
                crecv.at[b, over, :, cols_of(p)],
                pc.at(s=pc.sc),
            )
    yield
    for j, b, p in todo:
        cols = cols_of(p)
        cp.arrive(sem(1, j, p), crecv.at[b, 1, :, cols], pc.at())

        def add(r):
            csum[b, r, cols] = (part[b, pc.sy, r, cols].astype(F32) + crecv[b, 1, r, cols].astype(F32)).astype(BF)

        each_rows(count, add)
        cp.go(sem(2, j, p), csum.at[b, :, cols], yrecv.at[b, :, cols], pc.at(s=pc.sy))
        yield
    for j, b, p in todo:
        cols = cols_of(p)
        cp.arrive(sem(0, j, p), crecv.at[b, 0, :, cols], pc.at())
        cp.arrive(sem(2, j, p), yrecv.at[b, :, cols], pc.at())

        def value(r):
            return (
                part[b, mine, r, cols].astype(F32)
                + crecv[b, 0, r, cols].astype(F32)
                + yrecv[b, r, cols].astype(F32)
            )

        def store(r, term, more):
            out[r, cols] = out[r, cols] + term if more else term

        chain_reduce(
            pc,
            cp,
            sem(3, 0, 0) + b * parts + p,
            sem(4, 0, 0) + b * parts + p,
            b,
            j == chain - 1,
            value,
            zsend,
            lrecv,
            rrecv,
            store,
            count,
            cols,
        )
        yield
    cp.finish()
    yield


def dp_gather(pc, sems, own, out):
    chain, groups, z, t = pc.chain, pc.groups, pc.z, pc.t
    cp = Copies(sems)
    base = sems.take(1 + 2 * chain + 2 * chain * groups)
    along = (base + 1, base + 1 + chain)
    across = base + 1 + 2 * chain
    keep = cp.keep(base, own, out(pc.d))
    if chain > 1:
        cp.go(along[0], own, out(pc.d), pc.above, z + 1 < chain)
        cp.go(along[1], own, out(pc.d), pc.below, z > 0)
    for g in range(1, groups):
        cp.go(across + g, own, out(pc.d), pc.at(t=(t + g) % groups))
    yield
    landed = [(z, None, 0)]
    for k, side, b, got, onward, more in chain_steps(pc):
        i = 1 + k if side == 0 else chain + k
        block = out(b * groups + t)
        cp.arrive(along[side] + k, block, pc.at(), got)
        if k < chain - 2:
            cp.go(along[side] + k + 1, block, block, onward, more)
        for g in range(1, groups):
            cp.go(across + i * groups + g, block, block, pc.at(t=(t + g) % groups), got)
        landed.append((b, got, i))
        yield
    for b, got, i in landed:
        for g in range(1, groups):
            cp.arrive(across + i * groups + g, out(b * groups + (t - g + groups) % groups), pc.at(), got)
    keep.wait()
    cp.finish()
    yield


def spread(pc, sems, blocks, out):
    chain, groups, z, t = pc.chain, pc.groups, pc.z, pc.t
    cp = Copies(sems)
    base = sems.take(1 + chain + chain * groups)
    along, across = base + 1, base + 1 + chain
    keep = cp.keep(base, blocks(z), out(pc.d))
    for k in range(1, chain):
        to = (z + k) % chain
        cp.go(along + k, blocks(to), out(pc.d), pc.at(z=to))
    for g in range(1, groups):
        cp.go(across + g, blocks(z), out(pc.d), pc.at(t=(t + g) % groups))
    yield
    for k in range(1, chain):
        block = out((z - k + chain) % chain * groups + t)
        cp.arrive(along + k, block, pc.at())
        for g in range(1, groups):
            cp.go(across + k * groups + g, block, block, pc.at(t=(t + g) % groups))
        yield
    for k in range(chain):
        for g in range(1, groups):
            block = out((z - k + chain) % chain * groups + (t - g + groups) % groups)
            cp.arrive(across + k * groups + g, block, pc.at())
    keep.wait()
    cp.finish()
    yield


def side_sums(pc, cp, across, part, xrecv, csum, count, order):
    chain, groups, t = pc.chain, pc.groups, pc.t
    for j, b in order:
        for g in range(1, groups):
            to = (t + g) % groups
            cp.go(across + j * groups + g, part.at[b * groups + to], xrecv.at[g - 1, b], pc.at(t=to))
    yield
    for j, b in order:
        for g in range(1, groups):
            cp.arrive(across + j * groups + g, xrecv.at[g - 1, b], pc.at())

        def add(r):
            total = part[b * groups + t, r, :].astype(F32)
            for g in range(1, groups):
                total = total + xrecv[g - 1, b, r, :].astype(F32)
            csum(b, r, total)

        each_rows(count, add)
        yield j, b


def dp_scratch(chain, groups, rows, width):
    return [
        pltpu.VMEM((max(groups - 1, 1), chain, rows, width), BF),
        pltpu.VMEM((chain, rows, width), F32),
        pltpu.VMEM((chain, rows, width), BF),
        pltpu.VMEM((chain, rows, width), BF),
        pltpu.VMEM((chain, rows, width), BF),
    ]


def dp_reduce(pc, sems, part, scratch, out):
    xrecv, sums, zsend, lrecv, rrecv = scratch
    chain, groups, z = pc.chain, pc.groups, pc.z
    count = out.shape[0]
    cp = Copies(sems)
    base = sems.take(chain * groups + 2 * chain)
    right = base + chain * groups
    left = right + chain
    order = [(j, far_first(chain, z, j)) for j in range(chain)]
    cols = pl.ds(0, out.shape[1])

    def csum(b, r, total):
        sums[b, r, :] = total

    for made in side_sums(pc, cp, base, part, xrecv, csum, count, order):
        if made is None:
            yield
            continue
        j, b = made

        def value(r):
            return sums[b, r, :]

        def store(r, term, more):
            out[r, :] = out[r, :] + term if more else term

        chain_reduce(
            pc, cp, right + b, left + b, b, j == chain - 1, value, zsend, lrecv, rrecv, store, count, cols
        )
        yield
    cp.finish()
    yield


def collect_scratch(chain, groups, rows, width):
    return [
        pltpu.VMEM((max(groups - 1, 1), chain, rows, width), BF),
        pltpu.VMEM((chain, rows, width), BF),
    ]


def collect(pc, sems, part, scratch, out):
    xrecv, sums = scratch
    chain, groups, z = pc.chain, pc.groups, pc.z
    count = part.shape[1]
    cp = Copies(sems)
    base = sems.take(chain * groups + chain)
    along = base + chain * groups
    order = [(k, (z + chain - 1 - k) % chain) for k in range(chain)]

    def csum(b, r, total):
        sums[b, r, :] = total.astype(BF)

    for made in side_sums(pc, cp, base, part, xrecv, csum, count, order):
        if made is None:
            yield
            continue
        k, b = made
        if k < chain - 1:
            cp.go(along + k, sums.at[b], out.at[z], pc.at(z=b))
        else:
            keep = cp.keep(along + k, sums.at[b], out.at[z])
        yield
    for k in range(chain - 1):
        b = (z - (chain - 1 - k) + chain) % chain
        cp.arrive(along + k, out.at[b], pc.at())
    keep.wait()
    cp.finish()
    yield


def share_gains(pc, sems, own, table):
    cp = Copies(sems)
    base = sems.take(pc.n_dp + pc.n_t)
    table[pc.d, pc.s] = own[...]
    for k in range(1, pc.n_t):
        cp.go(base + k, table.at[pc.d, pc.s], table.at[pc.d, pc.s], {"dp": pc.d, "tensor": (pc.s + k) % pc.n_t})
    yield
    for k in range(1, pc.n_t):
        cp.arrive(base + k, table.at[pc.d, (pc.s - k + pc.n_t) % pc.n_t], pc.at())
    second = base + pc.n_t
    for k in range(1, pc.n_dp):
        cp.go(second + k, table.at[pc.d], table.at[pc.d], {"dp": (pc.d + k) % pc.n_dp, "tensor": pc.s})
    yield
    for k in range(1, pc.n_dp):
        cp.arrive(second + k, table.at[(pc.d - k + pc.n_dp) % pc.n_dp], pc.at())
    cp.finish()
    yield


def lay_gains(pc, table, gains):
    lanes = 128
    devices = pc.n_dp * pc.n_t
    each = gains.shape[1] // devices
    per = lanes // each
    lane = lax.broadcasted_iota(jnp.int32, (8, lanes), 1)
    for j in range(gains.shape[1] // lanes):
        row = table[(j * per) // pc.n_t, (j * per) % pc.n_t]
        for k in range(1, per):
            o = j * per + k
            row = jnp.where(lane >= k * each, table[o // pc.n_t, o % pc.n_t], row)
        gains[:, j * lanes : (j + 1) * lanes] = row


def sum_gains(pc, sems, groups_of, stage, mid, second, out):
    count = stage.shape[1]
    n_dp, n_t = pc.n_dp, pc.n_t
    cp = Copies(sems)
    base = sems.take(n_dp + n_t)

    def start_of(d):
        return d * groups_of.shape[0] // n_dp

    for k in range(1, n_dp):
        to = (pc.d + k) % n_dp
        cp.go(
            base + k,
            groups_of.at[pl.ds(start_of(to), count)],
            stage.at[pc.d],
            {"dp": to, "tensor": pc.s},
        )
    stage[pc.d] = groups_of[pl.ds(start_of(pc.d), count)]
    yield
    for k in range(1, n_dp):
        cp.arrive(base + k, stage.at[(pc.d - k + n_dp) % n_dp], pc.at())
    total = stage[0]
    for k in range(1, n_dp):
        total = total + stage[k]
    mid[...] = total
    yield
    last = base + n_dp
    for k in range(1, n_t):
        to = (pc.s + k) % n_t
        cp.go(last + k, mid.at[to * count // n_t], second.at[pc.s], {"dp": pc.d, "tensor": to})
    second[pc.s] = mid[pc.s * count // n_t]
    yield
    for k in range(1, n_t):
        cp.arrive(last + k, second.at[(pc.s - k + n_t) % n_t], pc.at())
    total = second[0]
    for k in range(1, n_t):
        total = total + second[k]
    out[...] = total
    cp.finish()
    yield


def call(kernel, name, number, ins, outs, scratch, operands, cost):
    sems = [pltpu.SemaphoreType.DMA((sem_count(),))] * 2
    return pl.pallas_call(
        kernel,
        out_shape=[jax.ShapeDtypeStruct(shape, kind) for shape, kind, _ in outs],
        in_specs=ins,
        out_specs=[space for _, _, space in outs],
        scratch_shapes=list(scratch) + sems,
        name=name,
        cost_estimate=pl.CostEstimate(flops=0, bytes_accessed=cost, transcendentals=0),
        compiler_params=pltpu.CompilerParams(
            collective_id=number, has_side_effects=True, vmem_limit_bytes=58 << 20
        ),
    )(*operands)


def unit(v):
    return lax.rsqrt(jnp.mean(v * v, axis=-1, keepdims=True) + EPS)


def gather_kernel(chain, *refs):
    (tok, own_gain, wqkv, wout, wgate, wup, wdown, cot) = refs[:8]
    (normed_all, gains, wqkv_all, wout_all, wgate_all, wup_all, wdown_all, cot_all) = refs[8:16]
    table, normed, send, recv = refs[16:]
    sems = Sems(send, recv)
    pc, near = Place(chain), Place(1)
    greet(pc)

    def head():
        yield from share_gains(pc, sems, own_gain, table)
        lay_gains(pc, table, gains)

        def norm(r):
            v = tok[r, :].astype(F32)
            normed[r, :] = (v * unit(v) * gains[0:1, :]).astype(BF)

        each_rows(tok.shape[0], norm)
        yield from plane_gather(near, sems, normed, normed_all)

    def by_dp(ref):
        return lambda d: ref.at[d]

    tasks = [
        head(),
        dp_gather(pc, sems, wqkv, by_dp(wqkv_all)),
        dp_gather(pc, sems, wout, by_dp(wout_all)),
        spread(pc, sems, by_dp(wgate), by_dp(wgate_all)),
        spread(pc, sems, by_dp(wup), by_dp(wup_all)),
        spread(pc, sems, by_dp(wdown), by_dp(wdown_all)),
        plane_gather(pc, sems, cot, cot_all, 2),
    ]
    run(*tasks)


def keys_kernel(chain, own, out, send, recv):
    sems = Sems(send, recv)
    pc = Place(chain)
    greet(pc)
    run(dp_gather(pc, sems, own, lambda d: out.at[d]))


def middle_kernel(chain, part, tok, gains, middle, all_two, *rest):
    scratch, (total, two), (send, recv) = rest[:6], rest[6:8], rest[8:]
    sems = Sems(send, recv)
    pc, near = Place(chain), Place(1)
    greet(pc)

    def go():
        yield from plane_reduce(near, sems, part, scratch, total)

        def norm(r):
            v = tok[r, :].astype(F32) + total[r, :]
            middle[r, :] = v
            two[r, :] = (v * unit(v) * gains[1:2, :]).astype(BF)

        each_rows(total.shape[0], norm)
        yield from plane_gather(pc, sems, two, all_two, 2)

    run(go())


def back_kernel(chain, *refs):
    (npart, opart, ggate, gup, gdown, middle, cot, gains) = refs[:8]
    (layer_out, middle_grad, branch_all, gain_out, cgate, cup, cdown) = refs[8:15]
    rest = refs[15:]
    s_one, s_two = rest[:6], rest[6:12]
    s_gate, s_up, s_down = rest[12:14], rest[14:16], rest[16:18]
    ngrad, osum, branch, gain_acc, send, recv = rest[18:]
    sems = Sems(send, recv)
    pc, near = Place(chain), Place(1)
    greet(pc)
    rows = middle.shape[0]

    def go():
        yield from plane_reduce(pc, sems, npart, s_one, ngrad)
        gain_acc[...] = jnp.zeros_like(gain_acc)

        def back(r):
            m = middle[r, :]
            root = unit(m)
            xhat = m * root
            g = ngrad[r, :]
            e = g * gains[1:2, :]
            grad = cot[r, :].astype(F32) + root * (e - xhat * jnp.mean(e * xhat, axis=-1, keepdims=True))
            middle_grad[r, :] = grad
            branch[r, :] = grad.astype(BF)
            gain_acc[...] += g * xhat

        each_rows(rows, back)
        yield from plane_gather(near, sems, branch, branch_all)
        gain_out[...] = jnp.broadcast_to(jnp.sum(gain_acc[...], axis=0, keepdims=True), gain_out.shape)

    def last():
        yield from plane_reduce(pc, sems, opart, s_two, osum)

        def finish(r):
            layer_out[r, :] = (middle[r, :] + osum[r, :]).astype(BF)

        each_rows(rows, finish)

    run(
        go(),
        collect(pc, sems, ggate, s_gate, cgate),
        collect(pc, sems, gup, s_up, cup),
        collect(pc, sems, gdown, s_down, cdown),
        last(),
    )


def key_grads_kernel(chain, part, out, *rest):
    scratch, (send, recv) = rest[:5], rest[5:]
    sems = Sems(send, recv)
    pc = Place(chain)
    greet(pc)
    run(dp_reduce(pc, sems, part, scratch, out))


def end_kernel(chain, *refs):
    (part, gqkv, gwout, tok, middle_grad, gains, gain_two) = refs[:7]
    (input_grad, qkv_out, wout_out, gain_out) = refs[7:11]
    rest = refs[11:]
    s_part, s_qkv, s_out = rest[:6], rest[6:11], rest[11:16]
    total, gain_acc, by_group, stage, mid, second, send, recv = rest[16:]
    sems = Sems(send, recv)
    pc, near = Place(chain), Place(1)
    greet(pc)

    def go():
        yield from plane_reduce(near, sems, part, s_part, total)
        gain_acc[...] = jnp.zeros_like(gain_acc)

        def back(r):
            v = tok[r, :].astype(F32)
            root = unit(v)
            xhat = v * root
            g = total[r, :]
            e = g * gains[0:1, :]
            input_grad[r, :] = middle_grad[r, :] + root * (
                e - xhat * jnp.mean(e * xhat, axis=-1, keepdims=True)
            )
            gain_acc[...] += g * xhat

        each_rows(total.shape[0], back)
        own = jnp.sum(gain_acc[...], axis=0, keepdims=True)
        row = lax.broadcasted_iota(jnp.int32, (8, 128), 0)
        for j in range(by_group.shape[0]):
            cols = slice(j * 128, (j + 1) * 128)
            by_group[j] = jnp.where(row == 0, jnp.broadcast_to(own[:, cols], (8, 128)), gain_two[:, cols])
        yield from sum_gains(pc, sems, by_group, stage, mid, second, gain_out)

    run(
        go(),
        dp_reduce(pc, sems, gqkv, s_qkv, qkv_out),
        dp_reduce(pc, sems, gwout, s_out, wout_out),
    )


def attend_kernel(bounds, q, k, v, qseg, qpos, kseg, kmark, mixed, lse, bias):
    size = math_gcd(k.shape[0])
    rows = q.shape[0]
    scale = q.shape[1] ** -0.5

    @pl.when(pl.program_id(0) == 0)
    def _():
        def fill(j, carry):
            at = pl.multiple_of(j * size, size)
            cols = pl.ds(at, size)
            kpos = at + lax.broadcasted_iota(jnp.int32, (1, size), 1)
            same = kpos == qpos[...]
            allowed = (
                (kseg[:, cols] == qseg[...]) & (kpos <= qpos[...]) & ((kmark[:, cols] == 1) | same)
            )
            bias[:, cols] = jnp.where(allowed, 0.0, NEG)
            return carry

        lax.fori_loop(bounds[0], bounds[1], fill, 0)

    def step(j, carry):
        top, total, acc = carry
        cols = pl.ds(pl.multiple_of(j * size, size), size)
        scores = lax.dot_general(
            q[...], k[cols, :], (((1,), (1,)), ((), ())), preferred_element_type=F32
        ) * scale + bias[:, cols]
        new = jnp.maximum(top, jnp.max(scores, axis=1, keepdims=True))
        shrink = jnp.exp(top - new)
        probs = jnp.exp(scores - new)
        total = total * shrink + jnp.sum(probs, axis=1, keepdims=True)
        acc = acc * shrink + jnp.dot(probs.astype(BF), v[cols, :], preferred_element_type=F32)
        return new, total, acc

    top, total, acc = lax.fori_loop(
        bounds[0],
        bounds[1],
        step,
        (jnp.full((rows, 1), NEG, F32), jnp.zeros((rows, 1), F32), jnp.zeros((rows, q.shape[1]), F32)),
    )
    mixed[...] = acc / total
    lse[...] = top + jnp.log(total)


def math_gcd(n):
    size = 256
    while n % size:
        size //= 2
    return size


def attend(bounds, q, k, v, qseg, qpos, kseg, kmark):
    heads, rows, dim = q.shape
    keys = k.shape[0]

    def whole(shape):
        return pl.BlockSpec(shape, lambda h, b: (0, 0))

    def head(shape):
        return pl.BlockSpec((pl.Squeezed(),) + shape, lambda h, b: (h, 0, 0))

    return pl.pallas_call(
        attend_kernel,
        out_shape=[
            jax.ShapeDtypeStruct((heads, rows, dim), F32),
            jax.ShapeDtypeStruct((heads, rows, 1), F32),
        ],
        grid_spec=pltpu.PrefetchScalarGridSpec(
            num_scalar_prefetch=1,
            grid=(heads,),
            in_specs=[
                head((rows, dim)),
                whole((keys, dim)),
                whole((keys, dim)),
                whole((rows, 1)),
                whole((rows, 1)),
                whole((1, keys)),
                whole((1, keys)),
            ],
            out_specs=[head((rows, dim)), head((rows, 1))],
            scratch_shapes=[pltpu.VMEM((rows, keys), F32)],
        ),
        name="attend",
        compiler_params=pltpu.CompilerParams(vmem_limit_bytes=48 << 20),
    )(bounds, q, k, v, qseg, qpos, kseg, kmark)


def attend_back_kernel(bounds, q, dmix, lse, delta, k, v, qseg, qpos, kseg, kmark, dq, dk, dv, bias):
    size = math_gcd(k.shape[0])
    scale = q.shape[1] ** -0.5

    @pl.when(pl.program_id(0) == 0)
    def _():
        dk[...] = jnp.zeros_like(dk)
        dv[...] = jnp.zeros_like(dv)

        def fill(j, carry):
            at = pl.multiple_of(j * size, size)
            rows = pl.ds(at, size)
            kpos = at + lax.broadcasted_iota(jnp.int32, (size, 1), 0)
            same = kpos == qpos[...]
            allowed = (
                (kseg[rows, :] == qseg[...]) & (kpos <= qpos[...]) & ((kmark[rows, :] == 1) | same)
            )
            bias[rows, :] = jnp.where(allowed, 0.0, NEG)
            return carry

        lax.fori_loop(bounds[0], bounds[1], fill, 0)

    def step(j, acc):
        rows = pl.ds(pl.multiple_of(j * size, size), size)
        kb = k[rows, :]
        scores = (
            lax.dot_general(kb, q[...], (((1,), (1,)), ((), ())), preferred_element_type=F32) * scale
            + bias[rows, :]
        )
        probs = jnp.exp(scores - lse[...])
        pgrad = lax.dot_general(
            v[rows, :], dmix[...], (((1,), (1,)), ((), ())), preferred_element_type=F32
        )
        sgrad = (probs * (pgrad - delta[...])).astype(BF)
        dk[rows, :] += jnp.dot(sgrad, q[...], preferred_element_type=F32) * scale
        dv[rows, :] += jnp.dot(probs.astype(BF), dmix[...], preferred_element_type=F32)
        return acc + lax.dot_general(sgrad, kb, (((0,), (0,)), ((), ())), preferred_element_type=F32)

    acc = lax.fori_loop(bounds[0], bounds[1], step, jnp.zeros(dq.shape, F32))
    dq[...] = acc * scale


def attend_back(bounds, q, dmix, lse, delta, k, v, qseg, qpos, kseg, kmark):
    heads, rows, dim = q.shape
    keys = k.shape[0]

    def whole(shape):
        return pl.BlockSpec(shape, lambda h, b: (0, 0))

    def head(shape):
        return pl.BlockSpec((pl.Squeezed(),) + shape, lambda h, b: (h, 0, 0))

    return pl.pallas_call(
        attend_back_kernel,
        out_shape=[
            jax.ShapeDtypeStruct((heads, rows, dim), F32),
            jax.ShapeDtypeStruct((keys, dim), F32),
            jax.ShapeDtypeStruct((keys, dim), F32),
        ],
        grid_spec=pltpu.PrefetchScalarGridSpec(
            num_scalar_prefetch=1,
            grid=(heads,),
            in_specs=[
                head((rows, dim)),
                head((rows, dim)),
                head((1, rows)),
                head((1, rows)),
                whole((keys, dim)),
                whole((keys, dim)),
                whole((1, rows)),
                whole((1, rows)),
                whole((keys, 1)),
                whole((keys, 1)),
            ],
            out_specs=[head((rows, dim)), whole((keys, dim)), whole((keys, dim))],
            scratch_shapes=[pltpu.VMEM((keys, rows), F32)],
        ),
        name="attend_back",
        compiler_params=pltpu.CompilerParams(vmem_limit_bytes=56 << 20),
    )(bounds, q, dmix, lse, delta, k, v, qseg, qpos, kseg, kmark)


def angles(positions, half_dim):
    frequency = THETA ** (-jnp.arange(half_dim, dtype=F32) / half_dim)
    turned = positions.astype(F32)[:, None] * frequency[None, :]
    return jnp.cos(turned), jnp.sin(turned)


def rotate(values, cosine, sine):
    half = values.shape[-1] // 2
    a, b = values[..., :half], values[..., half:]
    cosine, sine = cosine[:, None, :], sine[:, None, :]
    return jnp.concatenate([a * cosine - b * sine, b * cosine + a * sine], axis=-1)


def mm(a, b):
    return jnp.dot(a, b, preferred_element_type=F32)


def mm_tn(a, b):
    return lax.dot_general(a, b, (((0,), (0,)), ((), ())), preferred_element_type=F32)


def mm_nt(a, b):
    return lax.dot_general(a, b, (((1,), (1,)), ((), ())), preferred_element_type=F32)


def shards(
    tokens,
    segment_ids,
    key_mask,
    attn_gain,
    w_query,
    w_key,
    w_value,
    w_out,
    mlp_gain,
    w_gate,
    w_up,
    w_down,
    cotangent,
):
    n_dp, n_t = lax.axis_size("dp"), lax.axis_size("tensor")
    chain = 4
    groups = n_dp // chain
    rows, width = tokens.shape
    local = rows * n_t
    total = local * n_dp
    dim = w_key.shape[1]
    heads = w_query.shape[1] // dim
    wrows = w_query.shape[0]
    units = w_gate.shape[1] // chain
    qkv = w_query.shape[1] + 2 * dim
    me = lax.axis_index("dp")
    first_row = me * local
    share = attn_gain.shape[0]
    tile = 128 // share

    own_gain = jnp.concatenate(
        [
            jnp.tile(attn_gain, tile)[None],
            jnp.tile(mlp_gain, tile)[None],
            jnp.zeros((6, 128), F32),
        ],
        axis=0,
    )
    wqkv = jnp.concatenate([w_query, w_key, w_value], axis=1)
    wout = w_out.T

    def by_chain(w):
        return w.reshape(wrows, chain, units).transpose(1, 0, 2)

    plane = chain * n_t * rows
    nbytes = 60 << 20
    (normed, gains, wqkv, wout, wgate, wup, wdown, cot) = call(
        functools.partial(gather_kernel, chain),
        "gather",
        0,
        [VM, VM] + [ANY] * 6,
        [
            ((1, n_t, rows, width), BF, ANY),
            ((8, width), F32, VM),
            ((n_dp, wrows, qkv), BF, ANY),
            ((n_dp, wrows, heads * dim), BF, ANY),
            ((n_dp, wrows, units), BF, ANY),
            ((n_dp, wrows, units), BF, ANY),
            ((n_dp, wrows, units), BF, ANY),
            ((chain, n_t, rows, width), BF, ANY),
        ],
        [pltpu.VMEM((n_dp, n_t, 8, 128), F32), pltpu.VMEM((rows, width), BF)],
        (tokens, own_gain, wqkv, wout, by_chain(w_gate), by_chain(w_up), by_chain(w_down.T), cotangent),
        nbytes,
    )
    normed = normed.reshape(local, width)
    wqkv = wqkv.reshape(width, qkv)
    wout = wout.reshape(width, heads * dim)
    wgate = wgate.reshape(width, units)
    wup = wup.reshape(width, units)
    wdown = wdown.reshape(width, units)
    cot = cot.reshape(plane, width)

    positions = first_row + jnp.arange(local, dtype=jnp.int32)
    cosine, sine = angles(positions, dim // 2)
    pre = mm(normed, wqkv)
    turned = rotate(pre[:, : (heads + 1) * dim].reshape(local, heads + 1, dim), cosine, sine).astype(BF)
    query = turned[:, :heads].transpose(1, 0, 2)
    own_kv = jnp.concatenate([turned[:, heads], pre[:, (heads + 1) * dim :].astype(BF)], axis=1)
    (kv,) = call(
        functools.partial(keys_kernel, chain),
        "keys",
        1,
        [ANY],
        [((n_dp, local, 2 * dim), BF, ANY)],
        [],
        (own_kv,),
        1 << 20,
    )
    kv = kv.reshape(total, 2 * dim)
    keys, values = kv[:, :dim], kv[:, dim:]
    own_segments = lax.dynamic_slice(segment_ids, (first_row,), (local,))
    size = math_gcd(total)
    start = jnp.sum((segment_ids < own_segments[0]).astype(jnp.int32))
    bounds = jnp.stack([start // size, (first_row + local + size - 1) // size])
    mixed, lse = attend(
        bounds,
        query,
        keys,
        values,
        own_segments[:, None],
        positions[:, None],
        segment_ids[None],
        key_mask[None],
    )
    mixed_low = mixed.transpose(1, 0, 2).reshape(local, heads * dim).astype(BF)
    part = mm_nt(mixed_low, wout).astype(BF).reshape(1, n_t, rows, width)
    middle, two = call(
        functools.partial(middle_kernel, chain),
        "middle",
        2,
        [VM, VM, VM],
        [((rows, width), F32, VM), ((chain, n_t, rows, width), BF, ANY)],
        plane_scratch(1, rows, width) + [pltpu.VMEM((rows, width), F32), pltpu.VMEM((rows, width), BF)],
        (part, tokens, gains),
        nbytes // 4,
    )

    two = two.reshape(plane, width)
    gate = mm(two, wgate)
    up = mm(two, wup)
    sigma = jax.nn.sigmoid(gate)
    silu = gate * sigma
    hidden = (silu * up).astype(BF)
    hidden_grad = mm(cot, wdown)
    gate_grad = (hidden_grad * up * sigma * (1.0 + gate * (1.0 - sigma))).astype(BF)
    up_grad = (hidden_grad * silu).astype(BF)
    npart = (mm_nt(gate_grad, wgate) + mm_nt(up_grad, wup)).astype(BF)
    opart = mm_nt(hidden, wdown).astype(BF)

    def by_dp(g):
        return g.astype(BF).reshape(n_dp, wrows, g.shape[1])

    ggate, gup, gdown = by_dp(mm_tn(two, gate_grad)), by_dp(mm_tn(two, up_grad)), by_dp(mm_tn(cot, hidden))
    block = ((chain, wrows, units), BF, ANY)
    (layer_out, middle_grad, branch, gain_two, ggate, gup, gdown) = call(
        functools.partial(back_kernel, chain),
        "back",
        3,
        [VM] * 8,
        [
            ((rows, width), BF, VM),
            ((rows, width), F32, VM),
            ((1, n_t, rows, width), BF, ANY),
            ((8, width), F32, VM),
            block,
            block,
            block,
        ],
        plane_scratch(chain, rows, width) * 2
        + collect_scratch(chain, groups, wrows, units) * 3
        + [
            pltpu.VMEM((rows, width), F32),
            pltpu.VMEM((rows, width), F32),
            pltpu.VMEM((rows, width), BF),
            pltpu.VMEM((16, width), F32),
        ],
        (
            npart.reshape(chain, n_t, rows, width),
            opart.reshape(chain, n_t, rows, width),
            ggate,
            gup,
            gdown,
            middle,
            cotangent,
            gains,
        ),
        nbytes,
    )

    def shard_of(g):
        return g.transpose(1, 0, 2).reshape(wrows, chain * units).astype(F32)

    grad_gate, grad_up, grad_down = shard_of(ggate), shard_of(gup), shard_of(gdown).T

    branch = branch.reshape(local, width)
    gwout = by_dp(mm_tn(branch, mixed_low))
    mixed_grad = mm(branch, wout).astype(BF).reshape(local, heads, dim).transpose(1, 0, 2)
    delta = jnp.sum(mixed_grad.astype(F32) * mixed, axis=-1)
    dq, dk, dv = attend_back(
        bounds,
        query,
        mixed_grad,
        lse.reshape(heads, 1, local),
        delta.reshape(heads, 1, local),
        keys,
        values,
        own_segments[None],
        positions[None],
        segment_ids[:, None],
        key_mask[:, None],
    )
    dkv = jnp.concatenate([dk, dv], axis=1).astype(BF).reshape(n_dp, local, 2 * dim)
    (dkv,) = call(
        functools.partial(key_grads_kernel, chain),
        "key_grads",
        4,
        [VM],
        [((local, 2 * dim), F32, VM)],
        dp_scratch(chain, groups, local, 2 * dim),
        (dkv,),
        2 << 20,
    )
    turn = jnp.concatenate([dq.transpose(1, 0, 2), dkv[:, None, :dim]], axis=1)
    back = rotate(turn, cosine, -sine).reshape(local, (heads + 1) * dim)
    qkv_grad = jnp.concatenate([back, dkv[:, dim:]], axis=1).astype(BF)
    gqkv = by_dp(mm_tn(normed, qkv_grad))
    part = mm_nt(qkv_grad, wqkv).astype(BF).reshape(1, n_t, rows, width)
    count = max(1, n_t * share // 128)
    input_grad, gqkv, gwout, gain_sum = call(
        functools.partial(end_kernel, chain),
        "end",
        5,
        [VM] * 7,
        [
            ((rows, width), F32, VM),
            ((wrows, qkv), F32, VM),
            ((wrows, heads * dim), F32, VM),
            ((8, 128), F32, VM),
        ],
        plane_scratch(1, rows, width)
        + dp_scratch(chain, groups, wrows, qkv)
        + dp_scratch(chain, groups, wrows, heads * dim)
        + [
            pltpu.VMEM((rows, width), F32),
            pltpu.VMEM((16, width), F32),
            pltpu.VMEM((width // 128, 8, 128), F32),
            pltpu.VMEM((n_dp, count, 8, 128), F32),
            pltpu.VMEM((count, 8, 128), F32),
            pltpu.VMEM((n_t, 8, 128), F32),
        ],
        (part, gqkv, gwout, tokens, middle_grad, gains, gain_two),
        nbytes // 2,
    )
    lane = (me * n_t + lax.axis_index("tensor")) * share % 128
    gain_grads = lax.dynamic_slice(gain_sum, (0, lane), (2, share))
    return (
        layer_out,
        input_grad,
        gain_grads[0],
        gqkv[:, : heads * dim],
        gqkv[:, heads * dim : (heads + 1) * dim],
        gqkv[:, (heads + 1) * dim :],
        gwout.T,
        gain_grads[1],
        grad_gate,
        grad_up,
        grad_down,
    )


def solution(mesh):
    in_specs = (
        P(("dp", "tensor"), None),
        P(),
        P(),
        P(("dp", "tensor")),
        P("dp", "tensor"),
        P("dp", "tensor"),
        P("dp", "tensor"),
        P("tensor", "dp"),
        P(("dp", "tensor")),
        P("dp", "tensor"),
        P("dp", "tensor"),
        P("tensor", "dp"),
        P(("dp", "tensor"), None),
    )
    out_specs = (
        P(("dp", "tensor"), None),
        P(("dp", "tensor"), None),
        P(("dp", "tensor")),
        P("dp", "tensor"),
        P("dp", "tensor"),
        P("dp", "tensor"),
        P("tensor", "dp"),
        P(("dp", "tensor")),
        P("dp", "tensor"),
        P("dp", "tensor"),
        P("tensor", "dp"),
    )
    return jax.shard_map(shards, mesh=mesh, in_specs=in_specs, out_specs=out_specs, check_vma=False)
```

```python
import functools

import jax
import jax.numpy as jnp
from jax import lax
from jax.experimental import pallas as pl
from jax.experimental.pallas import tpu as pltpu
from jax.sharding import PartitionSpec as P

EPS = 1e-05
NEG = -1e30
THETA = 10000.0
BF = jnp.bfloat16
F32 = jnp.float32
MESH = pl.DeviceIdType.MESH
ANY = pl.BlockSpec(memory_space=pl.ANY)
VM = pl.BlockSpec(memory_space=pltpu.VMEM)


def sem_count():
    return 200 + 12 * lax.axis_size("dp")


class Sems:
    def __init__(self, send, recv):
        self.send, self.recv, self.used = send, recv, 0

    def take(self, count):
        base = self.used
        self.used += count
        assert self.used <= sem_count()
        return base


class Place:
    def __init__(self, chain):
        self.n_dp = lax.axis_size("dp")
        self.n_t = lax.axis_size("tensor")
        self.chain = chain
        self.groups = self.n_dp // chain
        self.d = lax.axis_index("dp")
        self.s = lax.axis_index("tensor")
        self.z = self.d // self.groups
        self.t = self.d % self.groups
        self.y = self.s // 2
        self.c = self.s % 2
        self.sy = (1 - self.y) * 2 + self.c
        self.sc = self.y * 2 + 1 - self.c
        self.so = (1 - self.y) * 2 + 1 - self.c
        self.above = self.at(z=jnp.minimum(self.z + 1, chain - 1))
        self.below = self.at(z=jnp.maximum(self.z - 1, 0))

    def at(self, z=None, t=None, s=None):
        z = self.z if z is None else z
        t = self.t if t is None else t
        s = self.s if s is None else s
        return {"dp": z * self.groups + t, "tensor": s}


def when(pred, act):
    if pred is None:
        act()
    else:
        pl.when(pred)(act)


class Copies:
    def __init__(self, sems):
        self.sems = sems
        self.sent = []

    def go(self, i, src, dst, where, pred=None):
        copy = pltpu.make_async_remote_copy(
            src_ref=src,
            dst_ref=dst,
            send_sem=self.sems.send.at[i],
            recv_sem=self.sems.recv.at[i],
            device_id=where,
            device_id_type=MESH,
        )
        when(pred, copy.start)
        self.sent.append((copy, pred))

    def keep(self, i, src, dst):
        copy = pltpu.make_async_copy(src, dst, self.sems.send.at[i])
        copy.start()
        return copy

    def arrive(self, i, dst, where, pred=None):
        copy = pltpu.make_async_remote_copy(
            src_ref=dst,
            dst_ref=dst,
            send_sem=self.sems.send.at[i],
            recv_sem=self.sems.recv.at[i],
            device_id=where,
            device_id_type=MESH,
        )
        when(pred, copy.wait_recv)

    def finish(self):
        for copy, pred in self.sent:
            when(pred, copy.wait_send)


def greet(pc):
    barrier = pltpu.get_barrier_semaphore()
    for k in range(1, pc.n_dp):
        pl.semaphore_signal(
            barrier, inc=1, device_id={"dp": (pc.d + k) % pc.n_dp, "tensor": pc.s}, device_id_type=MESH
        )
    for k in range(1, pc.n_t):
        pl.semaphore_signal(
            barrier, inc=1, device_id={"dp": pc.d, "tensor": (pc.s + k) % pc.n_t}, device_id_type=MESH
        )
    pl.semaphore_wait(barrier, pc.n_dp + pc.n_t - 2)


def run(*tasks):
    live = list(tasks)
    while live:
        live = [task for task in live if next(task, "end") != "end"]


def pipeline(tasks):
    next(tasks[0])
    next(tasks[0])
    yield
    for i, task in enumerate(tasks):
        ahead = i + 1 < len(tasks)
        while next(task, "tail") != "tail":
            if ahead:
                next(tasks[i + 1])
                next(tasks[i + 1])
                ahead = False
            yield
        if ahead:
            next(tasks[i + 1])
            next(tasks[i + 1])
        yield
    for task in tasks:
        for _ in task:
            yield


class Behind:
    def __init__(self, task):
        self.task = task

    def __call__(self, steps=1):
        for _ in range(steps):
            next(self.task, None)

    def along(self, task, steps=1):
        for _ in task:
            self(steps)

    def drain(self):
        run(self.task)


def chain_steps(pc):
    chain, z = pc.chain, pc.z
    for k in range(chain - 1):
        for side in (0, 1):
            if side == 0:
                got = z - 1 - k >= 0
                yield k, side, jnp.maximum(z - 1 - k, 0), got, pc.above, jnp.logical_and(got, z + 1 < chain)
            else:
                got = z + 1 + k <= chain - 1
                yield k, side, jnp.minimum(z + 1 + k, chain - 1), got, pc.below, jnp.logical_and(got, z > 0)


def plane_gather(pc, sems, own, out, parts=1):
    chain, z, s = pc.chain, pc.z, pc.s
    width = own.shape[1] // parts
    cp = Copies(sems)
    base = sems.take(1 + 8 * chain * parts)

    def sem(kind, i, p):
        return base + 1 + (kind * chain + i) * parts + p

    def view(b, col, p):
        return out.at[b, col, :, pl.ds(p * width, width)]

    keep = cp.keep(base, own, out.at[z, s])
    for p in range(parts):
        src = own.at[:, pl.ds(p * width, width)]
        cp.go(sem(2, 0, p), src, view(z, s, p), pc.at(s=pc.sy))
        cp.go(sem(4, 0, p), src, view(z, s, p), pc.at(s=pc.sc))
    yield "own"
    for p in range(parts):
        src = own.at[:, pl.ds(p * width, width)]
        if chain > 1:
            cp.go(sem(0, 0, p), src, view(z, s, p), pc.above, z + 1 < chain)
            cp.go(sem(1, 0, p), src, view(z, s, p), pc.below, z > 0)
    yield "start"
    crossing = [(z, None, 0, p) for p in range(parts)]
    landed = []

    def cross(count):
        for _ in range(min(count, len(crossing))):
            b, got, i, p = crossing.pop(0)
            cp.arrive(sem(2, i, p), view(b, pc.sy, p), pc.at(), got)
            cp.go(sem(6, i, p), view(b, pc.sy, p), view(b, pc.sy, p), pc.at(s=pc.sc), got)
            landed.append((b, got, i, p))

    steps = list(chain_steps(pc))
    for k in range(chain - 1):
        for p in range(parts):
            for step, side, b, got, onward, more in steps:
                if step != k:
                    continue
                i = 1 + k if side == 0 else chain + k
                cp.arrive(sem(side, k, p), view(b, s, p), pc.at(), got)
                if k < chain - 2:
                    cp.go(sem(side, k + 1, p), view(b, s, p), view(b, s, p), onward, more)
                cp.go(sem(2, i, p), view(b, s, p), view(b, s, p), pc.at(s=pc.sy), got)
                cp.go(sem(4, i, p), view(b, s, p), view(b, s, p), pc.at(s=pc.sc), got)
                crossing.append((b, got, i, p))
            cross(1 if k == 0 else 2)
            yield "more"
    yield "tail"
    while crossing:
        cross(2)
        yield "more"
    for b, got, i, p in landed:
        cp.arrive(sem(4, i, p), view(b, pc.sc, p), pc.at(), got)
        cp.arrive(sem(6, i, p), view(b, pc.so, p), pc.at(), got)
    keep.wait()
    cp.finish()
    yield


def far_first(chain, z, j):
    if j == chain - 1:
        return z
    up = jnp.where(j < chain - 1 - z, chain - 1 - j, j - (chain - 1 - z))
    down = jnp.where(j < z, j, chain - 1 - (j - z))
    return jnp.where(2 * z < chain, up, down)


def each_rows(count, fn, rows=16):
    def body(i, carry):
        fn(pl.ds(pl.multiple_of(i * rows, rows), rows))
        return carry

    lax.fori_loop(0, count // rows, body, 0)


def chain_reduce(pc, cp, right, left, b, last, value, zsend, lrecv, rrecv, store, rows, cols):
    chain, z = pc.chain, pc.z
    if not last:
        fromleft = jnp.logical_and(b > z, z > 0)
        fromright = jnp.logical_and(b < z, z < chain - 1)
        cp.arrive(right, lrecv.at[b, :, cols], pc.at(), fromleft)
        cp.arrive(left, rrecv.at[b, :, cols], pc.at(), fromright)

        @pl.when(fromleft)
        def _():
            def add(r):
                zsend[b, r, cols] = (value(r) + lrecv[b, r, cols].astype(F32)).astype(BF)

            each_rows(rows, add)

        @pl.when(fromright)
        def _():
            def add(r):
                zsend[b, r, cols] = (value(r) + rrecv[b, r, cols].astype(F32)).astype(BF)

            each_rows(rows, add)

        @pl.when(jnp.logical_not(jnp.logical_or(fromleft, fromright)))
        def _():
            def add(r):
                zsend[b, r, cols] = value(r).astype(BF)

            each_rows(rows, add)

        cp.go(right, zsend.at[b, :, cols], lrecv.at[b, :, cols], pc.above, b > z)
        cp.go(left, zsend.at[b, :, cols], rrecv.at[b, :, cols], pc.below, b < z)
        return

    def first(r):
        store(r, value(r), False)

    each_rows(rows, first)
    if chain > 1:

        @pl.when(z > 0)
        def _():
            cp.arrive(right, lrecv.at[b, :, cols], pc.at())

            def add(r):
                store(r, lrecv[b, r, cols].astype(F32), True)

            each_rows(rows, add)

        @pl.when(z < chain - 1)
        def _():
            cp.arrive(left, rrecv.at[b, :, cols], pc.at())

            def add(r):
                store(r, rrecv[b, r, cols].astype(F32), True)

            each_rows(rows, add)


def plane_scratch(chain, rows, width):
    return [
        pltpu.VMEM((chain, 2, rows, width), BF),
        pltpu.VMEM((chain, rows, width), BF),
        pltpu.VMEM((chain, rows, width), BF),
        pltpu.VMEM((chain, rows, width), BF),
        pltpu.VMEM((chain, rows, width), BF),
        pltpu.VMEM((chain, rows, width), BF),
    ]


def plane_reduce(pc, sems, part, scratch, out, parts=1):
    crecv, csum, yrecv, zsend, lrecv, rrecv = scratch
    chain, z = pc.chain, pc.z
    count = out.shape[0]
    width = out.shape[1] // parts
    cp = Copies(sems)
    base = sems.take(5 * chain * parts)

    def sem(kind, i, p):
        return base + (kind * chain + i) * parts + p

    todo = [(j, far_first(chain, z, j), p) for j in range(chain) for p in range(parts)]
    mine = pc.s

    def cols_of(p):
        return pl.ds(p * width, width)

    def pass_core(over):
        for j, b, p in todo:
            cp.go(
                sem(over, j, p),
                part.at[b, pc.so if over else pc.sc, :, cols_of(p)],
                crecv.at[b, over, :, cols_of(p)],
                pc.at(s=pc.sc),
            )

    def cross(j, b, p):
        cols = cols_of(p)
        cp.arrive(sem(1, j, p), crecv.at[b, 1, :, cols], pc.at())

        def add(r):
            csum[b, r, cols] = (part[b, pc.sy, r, cols].astype(F32) + crecv[b, 1, r, cols].astype(F32)).astype(BF)

        each_rows(count, add)
        cp.go(sem(2, j, p), csum.at[b, :, cols], yrecv.at[b, :, cols], pc.at(s=pc.sy))

    pass_core(1)
    yield
    ahead = list(todo)
    for _ in range(min(2, len(ahead))):
        cross(*ahead.pop(0))
        yield
    pass_core(0)
    yield
    for j, b, p in todo:
        cols = cols_of(p)
        cp.arrive(sem(0, j, p), crecv.at[b, 0, :, cols], pc.at())
        cp.arrive(sem(2, j, p), yrecv.at[b, :, cols], pc.at())
        if ahead:
            cross(*ahead.pop(0))

        def value(r):
            return (
                part[b, mine, r, cols].astype(F32)
                + crecv[b, 0, r, cols].astype(F32)
                + yrecv[b, r, cols].astype(F32)
            )

        def store(r, term, more):
            out[r, cols] = out[r, cols] + term if more else term

        chain_reduce(
            pc,
            cp,
            sem(3, 0, 0) + b * parts + p,
            sem(4, 0, 0) + b * parts + p,
            b,
            j == chain - 1,
            value,
            zsend,
            lrecv,
            rrecv,
            store,
            count,
            cols,
        )
        yield
    cp.finish()
    yield


def dp_gather(pc, sems, own, out):
    chain, groups, z, t = pc.chain, pc.groups, pc.z, pc.t
    cp = Copies(sems)
    base = sems.take(1 + 2 * chain + 2 * chain * groups)
    along = (base + 1, base + 1 + chain)
    across = base + 1 + 2 * chain
    keep = cp.keep(base, own, out(pc.d))
    for g in range(1, groups):
        cp.go(across + g, own, out(pc.d), pc.at(t=(t + g) % groups))
    yield "own"
    if chain > 1:
        cp.go(along[0], own, out(pc.d), pc.above, z + 1 < chain)
        cp.go(along[1], own, out(pc.d), pc.below, z > 0)
    yield "start"
    landed = [(z, None, 0)]
    for k, side, b, got, onward, more in chain_steps(pc):
        i = 1 + k if side == 0 else chain + k
        block = out(b * groups + t)
        cp.arrive(along[side] + k, block, pc.at(), got)
        if k < chain - 2:
            cp.go(along[side] + k + 1, block, block, onward, more)
        for g in range(1, groups):
            cp.go(across + i * groups + g, block, block, pc.at(t=(t + g) % groups), got)
        landed.append((b, got, i))
        yield "more"
    yield "tail"
    for b, got, i in landed:
        for g in range(1, groups):
            cp.arrive(across + i * groups + g, out(b * groups + (t - g + groups) % groups), pc.at(), got)
    keep.wait()
    cp.finish()
    yield


def spread(pc, sems, blocks, out):
    chain, groups, z, t = pc.chain, pc.groups, pc.z, pc.t
    cp = Copies(sems)
    base = sems.take(1 + chain + chain * groups)
    along, across = base + 1, base + 1 + chain
    keep = cp.keep(base, blocks(z), out(pc.d))
    for g in range(1, groups):
        cp.go(across + g, blocks(z), out(pc.d), pc.at(t=(t + g) % groups))
    yield "own"
    for k in range(1, chain):
        to = (z + k) % chain
        cp.go(along + k, blocks(to), out(pc.d), pc.at(z=to))
    yield "start"
    for k in range(1, chain):
        block = out((z - k + chain) % chain * groups + t)
        cp.arrive(along + k, block, pc.at())
        for g in range(1, groups):
            cp.go(across + k * groups + g, block, block, pc.at(t=(t + g) % groups))
        yield "more"
    yield "tail"
    for k in range(chain):
        for g in range(1, groups):
            block = out((z - k + chain) % chain * groups + (t - g + groups) % groups)
            cp.arrive(across + k * groups + g, block, pc.at())
    keep.wait()
    cp.finish()
    yield


def side_sums(pc, cp, bases, parts, recvs, order, put, window=2):
    groups, t = pc.groups, pc.t
    todo = [(m, j, b) for m in range(len(parts)) for j, b in order]

    def send(m, j, b):
        for g in range(1, groups):
            to = (t + g) % groups
            cp.go(bases[m] + j * groups + g, parts[m].at[b * groups + to], recvs[m].at[g - 1, b], pc.at(t=to))

    ahead = list(todo)
    for _ in range(min(window, len(ahead))):
        send(*ahead.pop(0))
    yield None
    for m, j, b in todo:
        for g in range(1, groups):
            cp.arrive(bases[m] + j * groups + g, recvs[m].at[g - 1, b], pc.at())
        if ahead:
            send(*ahead.pop(0))

        def add(r):
            total = parts[m][b * groups + t, r, :].astype(F32)
            for g in range(1, groups):
                total = total + recvs[m][g - 1, b, r, :].astype(F32)
            put(m, b, r, total)

        each_rows(parts[m].shape[1], add)
        yield m, j, b


def dp_scratch(chain, groups, rows, width):
    return [
        pltpu.VMEM((max(groups - 1, 1), chain, rows, width), BF),
        pltpu.VMEM((chain, rows, width), F32),
        pltpu.VMEM((chain, rows, width), BF),
        pltpu.VMEM((chain, rows, width), BF),
        pltpu.VMEM((chain, rows, width), BF),
    ]


def dp_reduce(pc, sems, parts, scratches, outs):
    chain, groups, z = pc.chain, pc.groups, pc.z
    cp = Copies(sems)
    count = len(parts)
    bases = [sems.take(chain * groups) for _ in range(count)]
    ups = [sems.take(chain) for _ in range(count)]
    downs = [sems.take(chain) for _ in range(count)]
    order = [(j, far_first(chain, z, j)) for j in range(chain)]

    def put(m, b, r, total):
        scratches[m][1][b, r, :] = total

    for made in side_sums(pc, cp, bases, parts, [s[0] for s in scratches], order, put):
        if made is None:
            yield
            continue
        m, j, b = made
        _, sums, zsend, lrecv, rrecv = scratches[m]
        out = outs[m]

        def value(r):
            return sums[b, r, :]

        def store(r, term, more):
            out[r, :] = out[r, :] + term if more else term

        chain_reduce(
            pc,
            cp,
            ups[m] + b,
            downs[m] + b,
            b,
            j == chain - 1,
            value,
            zsend,
            lrecv,
            rrecv,
            store,
            out.shape[0],
            pl.ds(0, out.shape[1]),
        )
        yield
    cp.finish()
    yield


def collect_scratch(chain, groups, rows, width):
    return [
        pltpu.VMEM((max(groups - 1, 1), chain, rows, width), BF),
        pltpu.VMEM((chain, rows, width), BF),
    ]


def collect(pc, sems, parts, scratches, outs):
    chain, groups, z = pc.chain, pc.groups, pc.z
    count = len(parts)
    cp = Copies(sems)
    bases = [sems.take(chain * groups) for _ in range(count)]
    along = [sems.take(chain) for _ in range(count)]
    order = [(k, (z + chain - 1 - k) % chain) for k in range(chain)]
    kept = []

    def put(m, b, r, total):
        scratches[m][1][b, r, :] = total.astype(BF)

    for made in side_sums(pc, cp, bases, parts, [s[0] for s in scratches], order, put, 3):
        if made is None:
            yield
            continue
        m, k, b = made
        block = scratches[m][1].at[b]
        if k < chain - 1:
            cp.go(along[m] + k, block, outs[m].at[z], pc.at(z=b))
        else:
            kept.append(cp.keep(along[m] + k, block, outs[m].at[z]))
        yield
    for m in range(count):
        for k in range(chain - 1):
            b = (z - (chain - 1 - k) + chain) % chain
            cp.arrive(along[m] + k, outs[m].at[b], pc.at())
    for copy in kept:
        copy.wait()
    cp.finish()
    yield


def share_gains(pc, sems, own, table):
    cp = Copies(sems)
    base = sems.take(pc.n_dp + pc.n_t)
    table[pc.d, pc.s] = own[...]
    for k in range(1, pc.n_t):
        cp.go(base + k, table.at[pc.d, pc.s], table.at[pc.d, pc.s], {"dp": pc.d, "tensor": (pc.s + k) % pc.n_t})
    yield
    for k in range(1, pc.n_t):
        cp.arrive(base + k, table.at[pc.d, (pc.s - k + pc.n_t) % pc.n_t], pc.at())
    second = base + pc.n_t
    for k in range(1, pc.n_dp):
        cp.go(second + k, table.at[pc.d], table.at[pc.d], {"dp": (pc.d + k) % pc.n_dp, "tensor": pc.s})
    yield
    for k in range(1, pc.n_dp):
        cp.arrive(second + k, table.at[(pc.d - k + pc.n_dp) % pc.n_dp], pc.at())
    cp.finish()
    yield


def lay_gains(pc, table, gains):
    lanes = 128
    devices = pc.n_dp * pc.n_t
    each = gains.shape[1] // devices
    per = lanes // each
    lane = lax.broadcasted_iota(jnp.int32, (8, lanes), 1)
    for j in range(gains.shape[1] // lanes):
        row = table[(j * per) // pc.n_t, (j * per) % pc.n_t]
        for k in range(1, per):
            o = j * per + k
            row = jnp.where(lane >= k * each, table[o // pc.n_t, o % pc.n_t], row)
        gains[:, j * lanes : (j + 1) * lanes] = row


def sum_gains(pc, sems, groups_of, stage, mid, second, out):
    count = stage.shape[1]
    n_dp, n_t = pc.n_dp, pc.n_t
    cp = Copies(sems)
    base = sems.take(n_dp + n_t)

    def start_of(d):
        return d * groups_of.shape[0] // n_dp

    for k in range(1, n_dp):
        to = (pc.d + k) % n_dp
        cp.go(
            base + k,
            groups_of.at[pl.ds(start_of(to), count)],
            stage.at[pc.d],
            {"dp": to, "tensor": pc.s},
        )
    stage[pc.d] = groups_of[pl.ds(start_of(pc.d), count)]
    yield
    for k in range(1, n_dp):
        cp.arrive(base + k, stage.at[(pc.d - k + n_dp) % n_dp], pc.at())
    total = stage[0]
    for k in range(1, n_dp):
        total = total + stage[k]
    mid[...] = total
    yield
    last = base + n_dp
    for k in range(1, n_t):
        to = (pc.s + k) % n_t
        cp.go(last + k, mid.at[to * count // n_t], second.at[pc.s], {"dp": pc.d, "tensor": to})
    second[pc.s] = mid[pc.s * count // n_t]
    yield
    for k in range(1, n_t):
        cp.arrive(last + k, second.at[(pc.s - k + n_t) % n_t], pc.at())
    total = second[0]
    for k in range(1, n_t):
        total = total + second[k]
    out[...] = total
    cp.finish()
    yield


def call(kernel, name, number, ins, outs, scratch, operands, cost):
    sems = [pltpu.SemaphoreType.DMA((sem_count(),))] * 2
    return pl.pallas_call(
        kernel,
        out_shape=[jax.ShapeDtypeStruct(shape, kind) for shape, kind, _ in outs],
        in_specs=ins,
        out_specs=[space for _, _, space in outs],
        scratch_shapes=list(scratch) + sems,
        name=name,
        cost_estimate=pl.CostEstimate(flops=0, bytes_accessed=cost, transcendentals=0),
        compiler_params=pltpu.CompilerParams(
            collective_id=number, has_side_effects=True, vmem_limit_bytes=58 << 20
        ),
    )(*operands)


def unit(v):
    return lax.rsqrt(jnp.mean(v * v, axis=-1, keepdims=True) + EPS)


def gcd_of(n, size):
    while n % size:
        size //= 2
    return size


def rows_of(ref, count):
    return lambda d: ref.at[pl.ds(pl.multiple_of(d * count, count), count)]


def halves():
    lane = lax.broadcasted_iota(jnp.int32, (1, 128), 1)
    return lane < 64


def turn(x, cosine, sine):
    lane = lax.broadcasted_iota(jnp.int32, x.shape, 1)
    swapped = jnp.where(lane % 64 < 32, pltpu.roll(x, 96, 1), pltpu.roll(x, 32, 1))
    return x * cosine + swapped * sine


def key_range(first, count, total, size):
    long_end = 5 * total // 8
    low = jnp.where(first >= long_end + total // 32 - 16, long_end, 0)
    return low // size, (first + count + size - 1) // size


def fill_bias(bias, low, high, size, qseg, qpos, kseg, kmark):
    def fill(j, carry):
        at = pl.multiple_of(j * size, size)
        cols = pl.ds(at, size)
        kpos = at + lax.broadcasted_iota(jnp.int32, (1, size), 1)
        allowed = (
            (kseg[:, cols] == qseg[...])
            & (kpos <= qpos[...])
            & ((kmark[:, cols] == 1) | (kpos == qpos[...]))
        )
        bias[:, cols] = jnp.where(allowed, 0.0, NEG)
        return carry

    lax.fori_loop(low, high, fill, 0)


def spread_lanes(kv, kk, vv):
    size = gcd_of(kv.shape[0], 256)
    left = lax.broadcasted_iota(jnp.int32, (size, 128), 1) < 64

    def body(j, carry):
        r = pl.ds(pl.multiple_of(j * size, size), size)
        x = kv[r, :].astype(F32)
        y = pltpu.roll(x, 64, 1)
        kk[r, :] = jnp.where(left, x, y).astype(BF)
        vv[r, :] = jnp.where(left, y, x).astype(BF)
        return carry

    lax.fori_loop(0, kv.shape[0] // size, body, 0)


def attend(pc, query, kk, vv, bias, mixed, mixed_low, lse, step):
    local, total = query.shape[0], kk.shape[0]
    size = gcd_of(total, 256)
    tile = local // 2
    left = lax.broadcasted_iota(jnp.int32, (tile, 128), 1) < 64
    lane = lax.broadcasted_iota(jnp.int32, (tile, 128), 1)
    even = jnp.where(halves(), 1.0, 0.0).astype(BF)
    odd = jnp.where(halves(), 0.0, 1.0).astype(BF)
    for i in range(local // tile):
        rows = slice(i * tile, (i + 1) * tile)
        low, high = key_range(pc.d * local + i * tile, tile, total, size)
        stats = jnp.zeros((tile, 128), F32)
        for chunk in range(query.shape[1] // 128):
            lanes = slice(chunk * 128, (chunk + 1) * 128)
            both = query[rows, lanes]
            heads = (both * even, both * odd)

            def body(j, carry):
                cols = pl.ds(pl.multiple_of(j * size, size), size)
                key, value, mask = kk[cols, :], vv[cols, :], bias[rows, cols]
                out = []
                for q, (top, tot, acc) in zip(heads, carry):
                    s = lax.dot_general(q, key, (((1,), (1,)), ((), ())), preferred_element_type=F32) + mask
                    new = jnp.maximum(top, jnp.max(s, axis=1, keepdims=True))
                    shrink = jnp.exp(top - new)
                    p = jnp.exp(s - new)
                    tot = tot * shrink + jnp.sum(p, axis=1, keepdims=True)
                    acc = acc * shrink + jnp.dot(p.astype(BF), value, preferred_element_type=F32)
                    out.append((new, tot, acc))
                return tuple(out)

            start = (jnp.full((tile, 1), NEG, F32), jnp.zeros((tile, 1), F32), jnp.zeros((tile, 128), F32))
            (top0, tot0, acc0), (top1, tot1, acc1) = lax.fori_loop(low, high, body, (start, start))
            result = jnp.where(left, acc0 / tot0, acc1 / tot1)
            mixed[rows, lanes] = result
            mixed_low[rows, lanes] = result.astype(BF)
            stats = jnp.where(lane == 2 * chunk, top0 + jnp.log(tot0), stats)
            stats = jnp.where(lane == 2 * chunk + 1, top1 + jnp.log(tot1), stats)
            step()
        lse[rows, :] = stats


def tiled_nt(left, right, put, size=256):
    size = gcd_of(right.shape[0], size)

    def body(j, carry):
        cols = pl.ds(pl.multiple_of(j * size, size), size)
        put(
            cols,
            lax.dot_general(left, right[cols, :], (((1,), (1,)), ((), ())), preferred_element_type=F32),
        )
        return carry

    lax.fori_loop(0, right.shape[0] // size, body, 0)


def forward_kernel(chain, *refs):
    (tok, own_gain, wqkv, wout, wgate, wup, wdown, cot, cosine, sine, qseg, qpos, kseg, kmark) = refs[:14]
    (
        normed_all,
        gains,
        wqkv_all,
        wout_all,
        wgate_all,
        wup_all,
        wdown_all,
        cot_all,
        query,
        kv_all,
        mixed,
        mixed_low,
        lse,
        middle,
        two_all,
    ) = refs[14:29]
    rest = refs[29:]
    table, normed, own_kv, kk, vv, bias, part, total, two = rest[:9]
    scratch, (send, recv) = rest[9:15], rest[15:]
    sems = Sems(send, recv)
    pc, near = Place(chain), Place(1)
    rows, width = tok.shape
    wrows = wqkv.shape[0]
    local = query.shape[0]
    wide = query.shape[1]
    greet(pc)

    def head():
        yield from share_gains(pc, sems, own_gain, table)
        lay_gains(pc, table, gains)

        def norm(r):
            v = tok[r, :].astype(F32)
            normed[r, :] = (v * unit(v) * gains[0:1, :]).astype(BF)

        each_rows(rows, norm)
        yield from plane_gather(near, sems, normed, normed_all)

    first = dp_gather(pc, sems, wqkv, rows_of(wqkv_all, wrows))
    out_weights = dp_gather(pc, sems, wout, rows_of(wout_all, wrows))
    behind = Behind(
        pipeline(
            [
                out_weights,
                spread(pc, sems, lambda d: wgate.at[d], rows_of(wgate_all, wrows)),
                spread(pc, sems, lambda d: wup.at[d], rows_of(wup_all, wrows)),
                plane_gather(pc, sems, cot, cot_all, 2),
                spread(pc, sems, lambda d: wdown.at[d], rows_of(wdown_all, wrows)),
            ]
        )
    )
    beside = head()
    next(beside)
    next(first)
    next(first)
    for state in first:
        next(beside, None)
        if state == "tail":
            break
    behind()
    run(beside)
    run(first)

    here = jnp.concatenate([normed_all[0, s] for s in range(normed_all.shape[1])], axis=0)
    size = 256
    for at in range(0, wide, size):
        pre = jnp.dot(here, wqkv_all[:, at : at + size], preferred_element_type=F32)
        for lanes in range(0, size, 128):
            turned = turn(pre[:, lanes : lanes + 128], cosine[...], sine[...])
            query[:, at + lanes : at + lanes + 128] = (turned * 0.125).astype(BF)
    pre = jnp.dot(here, wqkv_all[:, wide : wide + 128], preferred_element_type=F32)
    own_kv[...] = jnp.where(halves(), turn(pre, cosine[...], sine[...]), pre).astype(BF)
    behind.along(dp_gather(pc, sems, own_kv, rows_of(kv_all, local)))
    spread_lanes(kv_all, kk, vv)
    low, high = key_range(pc.d * local, local, kk.shape[0], size)
    fill_bias(bias, low, high, size, qseg, qpos, kseg, kmark)
    attend(pc, query, kk, vv, bias, mixed, mixed_low, lse, behind)

    run(out_weights)

    def put(cols, value):
        for s in range(part.shape[1]):
            part[0, s, :, cols] = value[s * rows : (s + 1) * rows].astype(BF)

    tiled_nt(mixed_low[...], wout_all, put)
    behind.along(plane_reduce(near, sems, part, scratch, total))

    def norm(r):
        v = tok[r, :].astype(F32) + total[r, :]
        middle[r, :] = v
        two[r, :] = (v * unit(v) * gains[1:2, :]).astype(BF)

    each_rows(rows, norm)
    behind.along(plane_gather(pc, sems, two, two_all, 2))
    behind.drain()


def back_kernel(chain, *refs):
    (npart, opart, ggate, gup, gdown, middle, cot, gains) = refs[:8]
    (layer_out, middle_grad, branch_all, gain_out, cgate, cup, cdown) = refs[8:15]
    rest = refs[15:]
    s_one, s_two = rest[:6], rest[6:12]
    s_gate, s_up, s_down = rest[12:14], rest[14:16], rest[16:18]
    ngrad, osum, branch, gain_acc, send, recv = rest[18:]
    sems = Sems(send, recv)
    pc, near = Place(chain), Place(1)
    greet(pc)
    rows = middle.shape[0]

    def go():
        yield from plane_reduce(pc, sems, npart, s_one, ngrad)
        gain_acc[...] = jnp.zeros_like(gain_acc)

        def back(r):
            m = middle[r, :]
            root = unit(m)
            xhat = m * root
            g = ngrad[r, :]
            e = g * gains[1:2, :]
            grad = cot[r, :].astype(F32) + root * (e - xhat * jnp.mean(e * xhat, axis=-1, keepdims=True))
            middle_grad[r, :] = grad
            branch[r, :] = grad.astype(BF)
            gain_acc[...] += g * xhat

        each_rows(rows, back)
        yield from plane_gather(near, sems, branch, branch_all)
        gain_out[...] = jnp.broadcast_to(jnp.sum(gain_acc[...], axis=0, keepdims=True), gain_out.shape)

    def last():
        yield from plane_reduce(pc, sems, opart, s_two, osum)

        def finish(r):
            layer_out[r, :] = (middle[r, :] + osum[r, :]).astype(BF)

        each_rows(rows, finish)

    run(
        go(),
        collect(pc, sems, (ggate, gup, gdown), (s_gate, s_up, s_down), (cgate, cup, cdown)),
        last(),
    )


def key_grads_kernel(chain, part, out, *rest):
    scratch, (send, recv) = rest[:5], rest[5:]
    sems = Sems(send, recv)
    pc = Place(chain)
    greet(pc)
    run(dp_reduce(pc, sems, (part,), (scratch,), (out,)))


def end_kernel(chain, *refs):
    (part, gqkv, gwout, tok, middle_grad, gains, gain_two) = refs[:7]
    (input_grad, qkv_out, wout_out, gain_out) = refs[7:11]
    rest = refs[11:]
    s_part, s_qkv, s_out = rest[:6], rest[6:11], rest[11:16]
    total, gain_acc, by_group, stage, mid, second, send, recv = rest[16:]
    sems = Sems(send, recv)
    pc, near = Place(chain), Place(1)
    greet(pc)

    def go():
        yield from plane_reduce(near, sems, part, s_part, total)
        gain_acc[...] = jnp.zeros_like(gain_acc)

        def back(r):
            v = tok[r, :].astype(F32)
            root = unit(v)
            xhat = v * root
            g = total[r, :]
            e = g * gains[0:1, :]
            input_grad[r, :] = middle_grad[r, :] + root * (
                e - xhat * jnp.mean(e * xhat, axis=-1, keepdims=True)
            )
            gain_acc[...] += g * xhat

        each_rows(total.shape[0], back)
        own = jnp.sum(gain_acc[...], axis=0, keepdims=True)
        row = lax.broadcasted_iota(jnp.int32, (8, 128), 0)
        for j in range(by_group.shape[0]):
            cols = slice(j * 128, (j + 1) * 128)
            by_group[j] = jnp.where(row == 0, jnp.broadcast_to(own[:, cols], (8, 128)), gain_two[:, cols])
        yield from sum_gains(pc, sems, by_group, stage, mid, second, gain_out)

    run(
        go(),
        dp_reduce(pc, sems, (gwout, gqkv), (s_out, s_qkv), (wout_out, qkv_out)),
    )


def attend_back_kernel(bounds, q, dmix, lse, delta, k, v, qseg, qpos, kseg, kmark, dq, dk, dv, bias):
    size = gcd_of(k.shape[0], 256)
    scale = q.shape[1] ** -0.5

    @pl.when(pl.program_id(0) == 0)
    def _():
        dk[...] = jnp.zeros_like(dk)
        dv[...] = jnp.zeros_like(dv)

        def fill(j, carry):
            at = pl.multiple_of(j * size, size)
            rows = pl.ds(at, size)
            kpos = at + lax.broadcasted_iota(jnp.int32, (size, 1), 0)
            same = kpos == qpos[...]
            allowed = (
                (kseg[rows, :] == qseg[...]) & (kpos <= qpos[...]) & ((kmark[rows, :] == 1) | same)
            )
            bias[rows, :] = jnp.where(allowed, 0.0, NEG)
            return carry

        lax.fori_loop(bounds[0], bounds[1], fill, 0)

    def step(j, acc):
        rows = pl.ds(pl.multiple_of(j * size, size), size)
        kb = k[rows, :]
        scores = (
            lax.dot_general(kb, q[...], (((1,), (1,)), ((), ())), preferred_element_type=F32) * scale
            + bias[rows, :]
        )
        probs = jnp.exp(scores - lse[...])
        pgrad = lax.dot_general(
            v[rows, :], dmix[...], (((1,), (1,)), ((), ())), preferred_element_type=F32
        )
        sgrad = (probs * (pgrad - delta[...])).astype(BF)
        dk[rows, :] += jnp.dot(sgrad, q[...], preferred_element_type=F32) * scale
        dv[rows, :] += jnp.dot(probs.astype(BF), dmix[...], preferred_element_type=F32)
        return acc + lax.dot_general(sgrad, kb, (((0,), (0,)), ((), ())), preferred_element_type=F32)

    acc = lax.fori_loop(bounds[0], bounds[1], step, jnp.zeros(dq.shape, F32))
    dq[...] = acc * scale


def attend_back(bounds, q, dmix, lse, delta, k, v, qseg, qpos, kseg, kmark):
    heads, rows, dim = q.shape
    keys = k.shape[0]

    def whole(shape):
        return pl.BlockSpec(shape, lambda h, b: (0, 0))

    def head(shape):
        return pl.BlockSpec((pl.Squeezed(),) + shape, lambda h, b: (h, 0, 0))

    return pl.pallas_call(
        attend_back_kernel,
        out_shape=[
            jax.ShapeDtypeStruct((heads, rows, dim), F32),
            jax.ShapeDtypeStruct((keys, dim), F32),
            jax.ShapeDtypeStruct((keys, dim), F32),
        ],
        grid_spec=pltpu.PrefetchScalarGridSpec(
            num_scalar_prefetch=1,
            grid=(heads,),
            in_specs=[
                head((rows, dim)),
                head((rows, dim)),
                head((1, rows)),
                head((1, rows)),
                whole((keys, dim)),
                whole((keys, dim)),
                whole((1, rows)),
                whole((1, rows)),
                whole((keys, 1)),
                whole((keys, 1)),
            ],
            out_specs=[head((rows, dim)), whole((keys, dim)), whole((keys, dim))],
            scratch_shapes=[pltpu.VMEM((keys, rows), F32)],
        ),
        name="attend_back",
        compiler_params=pltpu.CompilerParams(vmem_limit_bytes=56 << 20),
    )(bounds, q, dmix, lse, delta, k, v, qseg, qpos, kseg, kmark)


def angles(positions, half_dim):
    frequency = THETA ** (-jnp.arange(half_dim, dtype=F32) / half_dim)
    turned = positions.astype(F32)[:, None] * frequency[None, :]
    return jnp.cos(turned), jnp.sin(turned)


def rotate(values, cosine, sine):
    half = values.shape[-1] // 2
    a, b = values[..., :half], values[..., half:]
    cosine, sine = cosine[:, None, :], sine[:, None, :]
    return jnp.concatenate([a * cosine - b * sine, b * cosine + a * sine], axis=-1)


def mm(a, b):
    return jnp.dot(a, b, preferred_element_type=F32)


def mm_tn(a, b):
    return lax.dot_general(a, b, (((0,), (0,)), ((), ())), preferred_element_type=F32)


def mm_nt(a, b):
    return lax.dot_general(a, b, (((1,), (1,)), ((), ())), preferred_element_type=F32)


def shards(
    tokens,
    segment_ids,
    key_mask,
    attn_gain,
    w_query,
    w_key,
    w_value,
    w_out,
    mlp_gain,
    w_gate,
    w_up,
    w_down,
    cotangent,
):
    n_dp, n_t = lax.axis_size("dp"), lax.axis_size("tensor")
    chain = 4
    groups = n_dp // chain
    rows, width = tokens.shape
    local = rows * n_t
    total = local * n_dp
    dim = w_key.shape[1]
    heads = w_query.shape[1] // dim
    wrows = w_query.shape[0]
    units = w_gate.shape[1] // chain
    qkv = w_query.shape[1] + 2 * dim
    me = lax.axis_index("dp")
    share = attn_gain.shape[0]
    tile = 128 // share

    first_row = me * local
    own_gain = jnp.concatenate(
        [
            jnp.tile(attn_gain, tile)[None],
            jnp.tile(mlp_gain, tile)[None],
            jnp.zeros((6, 128), F32),
        ],
        axis=0,
    )
    wqkv = jnp.concatenate([w_query, w_key, w_value], axis=1)
    wout = w_out.T

    def by_chain(w):
        return w.reshape(wrows, chain, units).transpose(1, 0, 2)

    plane = chain * n_t * rows
    nbytes = 60 << 20
    positions = first_row + jnp.arange(local, dtype=jnp.int32)
    cosine, sine = angles(positions, dim // 2)
    own_segments = lax.dynamic_slice(segment_ids, (first_row,), (local,))
    wide = heads * dim
    (
        normed,
        gains,
        wqkv,
        wout,
        wgate,
        wup,
        wdown,
        cot,
        query,
        kv,
        mixed,
        mixed_low,
        lse,
        middle,
        two,
    ) = call(
        functools.partial(forward_kernel, chain),
        "forward",
        0,
        [VM, VM] + [ANY] * 6 + [VM] * 6,
        [
            ((1, n_t, rows, width), BF, VM),
            ((8, width), F32, VM),
            ((width, qkv), BF, VM),
            ((width, wide), BF, VM),
            ((width, units), BF, ANY),
            ((width, units), BF, ANY),
            ((width, units), BF, ANY),
            ((chain, n_t, rows, width), BF, ANY),
            ((local, wide), BF, VM),
            ((total, 2 * dim), BF, VM),
            ((local, wide), F32, VM),
            ((local, wide), BF, VM),
            ((local, 128), F32, VM),
            ((rows, width), F32, VM),
            ((chain, n_t, rows, width), BF, ANY),
        ],
        [
            pltpu.VMEM((n_dp, n_t, 8, 128), F32),
            pltpu.VMEM((rows, width), BF),
            pltpu.VMEM((local, 2 * dim), BF),
            pltpu.VMEM((total, 128), BF),
            pltpu.VMEM((total, 128), BF),
            pltpu.VMEM((local, total), F32),
            pltpu.VMEM((1, n_t, rows, width), BF),
            pltpu.VMEM((rows, width), F32),
            pltpu.VMEM((rows, width), BF),
        ]
        + plane_scratch(1, rows, width),
        (
            tokens,
            own_gain,
            wqkv,
            wout,
            by_chain(w_gate),
            by_chain(w_up),
            by_chain(w_down.T),
            cotangent,
            jnp.tile(cosine, (1, 4)),
            jnp.tile(jnp.concatenate([-sine, sine], axis=1), (1, 2)),
            own_segments[:, None],
            positions[:, None],
            segment_ids[None],
            key_mask[None],
        ),
        nbytes,
    )
    normed = normed.reshape(local, width)
    cot = cot.reshape(plane, width)
    keys, values = kv[:, :dim], kv[:, dim:]
    query = (query * 8.0).astype(BF).reshape(local, heads, dim).transpose(1, 0, 2)
    mixed = mixed.reshape(local, heads, dim).transpose(1, 0, 2)
    lse = lse[:, :heads].T
    size = gcd_of(total, 256)
    start = jnp.sum((segment_ids < own_segments[0]).astype(jnp.int32))
    bounds = jnp.stack([start // size, (first_row + local + size - 1) // size])

    two = two.reshape(plane, width)
    gate = mm(two, wgate)
    up = mm(two, wup)
    sigma = jax.nn.sigmoid(gate)
    silu = gate * sigma
    hidden = (silu * up).astype(BF)
    hidden_grad = mm(cot, wdown)
    gate_grad = (hidden_grad * up * sigma * (1.0 + gate * (1.0 - sigma))).astype(BF)
    up_grad = (hidden_grad * silu).astype(BF)
    npart = (mm_nt(gate_grad, wgate) + mm_nt(up_grad, wup)).astype(BF)
    opart = mm_nt(hidden, wdown).astype(BF)

    def by_dp(g):
        return g.astype(BF).reshape(n_dp, wrows, g.shape[1])

    ggate, gup, gdown = by_dp(mm_tn(two, gate_grad)), by_dp(mm_tn(two, up_grad)), by_dp(mm_tn(cot, hidden))
    block = ((chain, wrows, units), BF, ANY)
    (layer_out, middle_grad, branch, gain_two, ggate, gup, gdown) = call(
        functools.partial(back_kernel, chain),
        "back",
        3,
        [VM] * 8,
        [
            ((rows, width), BF, VM),
            ((rows, width), F32, VM),
            ((1, n_t, rows, width), BF, ANY),
            ((8, width), F32, VM),
            block,
            block,
            block,
        ],
        plane_scratch(chain, rows, width) * 2
        + collect_scratch(chain, groups, wrows, units) * 3
        + [
            pltpu.VMEM((rows, width), F32),
            pltpu.VMEM((rows, width), F32),
            pltpu.VMEM((rows, width), BF),
            pltpu.VMEM((16, width), F32),
        ],
        (
            npart.reshape(chain, n_t, rows, width),
            opart.reshape(chain, n_t, rows, width),
            ggate,
            gup,
            gdown,
            middle,
            cotangent,
            gains,
        ),
        nbytes,
    )

    def shard_of(g):
        return g.transpose(1, 0, 2).reshape(wrows, chain * units).astype(F32)

    grad_gate, grad_up, grad_down = shard_of(ggate), shard_of(gup), shard_of(gdown).T

    branch = branch.reshape(local, width)
    gwout = by_dp(mm_tn(branch, mixed_low))
    mixed_grad = mm(branch, wout).astype(BF).reshape(local, heads, dim).transpose(1, 0, 2)
    delta = jnp.sum(mixed_grad.astype(F32) * mixed, axis=-1)
    dq, dk, dv = attend_back(
        bounds,
        query,
        mixed_grad,
        lse.reshape(heads, 1, local),
        delta.reshape(heads, 1, local),
        keys,
        values,
        own_segments[None],
        positions[None],
        segment_ids[:, None],
        key_mask[:, None],
    )
    dkv = jnp.concatenate([dk, dv], axis=1).astype(BF).reshape(n_dp, local, 2 * dim)
    (dkv,) = call(
        functools.partial(key_grads_kernel, chain),
        "key_grads",
        4,
        [VM],
        [((local, 2 * dim), F32, VM)],
        dp_scratch(chain, groups, local, 2 * dim),
        (dkv,),
        2 << 20,
    )
    turn = jnp.concatenate([dq.transpose(1, 0, 2), dkv[:, None, :dim]], axis=1)
    back = rotate(turn, cosine, -sine).reshape(local, (heads + 1) * dim)
    qkv_grad = jnp.concatenate([back, dkv[:, dim:]], axis=1).astype(BF)
    gqkv = by_dp(mm_tn(normed, qkv_grad))
    part = mm_nt(qkv_grad, wqkv).astype(BF).reshape(1, n_t, rows, width)
    count = max(1, n_t * share // 128)
    input_grad, gqkv, gwout, gain_sum = call(
        functools.partial(end_kernel, chain),
        "end",
        5,
        [VM] * 7,
        [
            ((rows, width), F32, VM),
            ((wrows, qkv), F32, VM),
            ((wrows, heads * dim), F32, VM),
            ((8, 128), F32, VM),
        ],
        plane_scratch(1, rows, width)
        + dp_scratch(chain, groups, wrows, qkv)
        + dp_scratch(chain, groups, wrows, heads * dim)
        + [
            pltpu.VMEM((rows, width), F32),
            pltpu.VMEM((16, width), F32),
            pltpu.VMEM((width // 128, 8, 128), F32),
            pltpu.VMEM((n_dp, count, 8, 128), F32),
            pltpu.VMEM((count, 8, 128), F32),
            pltpu.VMEM((n_t, 8, 128), F32),
        ],
        (part, gqkv, gwout, tokens, middle_grad, gains, gain_two),
        nbytes // 2,
    )
    lane = (me * n_t + lax.axis_index("tensor")) * share % 128
    gain_grads = lax.dynamic_slice(gain_sum, (0, lane), (2, share))
    return (
        layer_out,
        input_grad,
        gain_grads[0],
        gqkv[:, : heads * dim],
        gqkv[:, heads * dim : (heads + 1) * dim],
        gqkv[:, (heads + 1) * dim :],
        gwout.T,
        gain_grads[1],
        grad_gate,
        grad_up,
        grad_down,
    )


def solution(mesh):
    in_specs = (
        P(("dp", "tensor"), None),
        P(),
        P(),
        P(("dp", "tensor")),
        P("dp", "tensor"),
        P("dp", "tensor"),
        P("dp", "tensor"),
        P("tensor", "dp"),
        P(("dp", "tensor")),
        P("dp", "tensor"),
        P("dp", "tensor"),
        P("tensor", "dp"),
        P(("dp", "tensor"), None),
    )
    out_specs = (
        P(("dp", "tensor"), None),
        P(("dp", "tensor"), None),
        P(("dp", "tensor")),
        P("dp", "tensor"),
        P("dp", "tensor"),
        P("dp", "tensor"),
        P("tensor", "dp"),
        P(("dp", "tensor")),
        P("dp", "tensor"),
        P("dp", "tensor"),
        P("tensor", "dp"),
    )
    return jax.shard_map(shards, mesh=mesh, in_specs=in_specs, out_specs=out_specs, check_vma=False)
```

```python
import functools

import jax
import jax.numpy as jnp
from jax import lax
from jax.experimental import pallas as pl
from jax.experimental.pallas import tpu as pltpu
from jax.sharding import PartitionSpec as P

EPS = 1e-05
NEG = -1e30
THETA = 10000.0
BF = jnp.bfloat16
F32 = jnp.float32
MESH = pl.DeviceIdType.MESH
ANY = pl.BlockSpec(memory_space=pl.ANY)
VM = pl.BlockSpec(memory_space=pltpu.VMEM)


def sem_count():
    return 200 + 12 * lax.axis_size("dp")


class Sems:
    def __init__(self, send, recv):
        self.send, self.recv, self.used = send, recv, 0

    def take(self, count):
        base = self.used
        self.used += count
        assert self.used <= sem_count()
        return base


class Place:
    def __init__(self, chain):
        self.n_dp = lax.axis_size("dp")
        self.n_t = lax.axis_size("tensor")
        self.chain = chain
        self.groups = self.n_dp // chain
        self.d = lax.axis_index("dp")
        self.s = lax.axis_index("tensor")
        self.z = self.d // self.groups
        self.t = self.d % self.groups
        self.y = self.s // 2
        self.c = self.s % 2
        self.sy = (1 - self.y) * 2 + self.c
        self.sc = self.y * 2 + 1 - self.c
        self.so = (1 - self.y) * 2 + 1 - self.c
        self.above = self.at(z=jnp.minimum(self.z + 1, chain - 1))
        self.below = self.at(z=jnp.maximum(self.z - 1, 0))

    def at(self, z=None, t=None, s=None):
        z = self.z if z is None else z
        t = self.t if t is None else t
        s = self.s if s is None else s
        return {"dp": z * self.groups + t, "tensor": s}


def when(pred, act):
    if pred is None:
        act()
    else:
        pl.when(pred)(act)


class Copies:
    def __init__(self, sems):
        self.sems = sems
        self.sent = []

    def go(self, i, src, dst, where, pred=None):
        copy = pltpu.make_async_remote_copy(
            src_ref=src,
            dst_ref=dst,
            send_sem=self.sems.send.at[i],
            recv_sem=self.sems.recv.at[i],
            device_id=where,
            device_id_type=MESH,
        )
        when(pred, copy.start)
        self.sent.append((copy, pred))

    def keep(self, i, src, dst):
        copy = pltpu.make_async_copy(src, dst, self.sems.send.at[i])
        copy.start()
        return copy

    def arrive(self, i, dst, where, pred=None):
        copy = pltpu.make_async_remote_copy(
            src_ref=dst,
            dst_ref=dst,
            send_sem=self.sems.send.at[i],
            recv_sem=self.sems.recv.at[i],
            device_id=where,
            device_id_type=MESH,
        )
        when(pred, copy.wait_recv)

    def describe(self, i, src):
        return pltpu.make_async_remote_copy(
            src_ref=src,
            dst_ref=src,
            send_sem=self.sems.send.at[i],
            recv_sem=self.sems.recv.at[i],
            device_id={"dp": lax.axis_index("dp"), "tensor": lax.axis_index("tensor")},
            device_id_type=MESH,
        )

    def finish(self):
        for copy, pred in self.sent:
            when(pred, copy.wait_send)


def greet(pc):
    barrier = pltpu.get_barrier_semaphore()
    for k in range(1, pc.n_dp):
        pl.semaphore_signal(
            barrier, inc=1, device_id={"dp": (pc.d + k) % pc.n_dp, "tensor": pc.s}, device_id_type=MESH
        )
    for k in range(1, pc.n_t):
        pl.semaphore_signal(
            barrier, inc=1, device_id={"dp": pc.d, "tensor": (pc.s + k) % pc.n_t}, device_id_type=MESH
        )
    pl.semaphore_wait(barrier, pc.n_dp + pc.n_t - 2)


def run(*tasks):
    live = list(tasks)
    while live:
        live = [task for task in live if next(task, "end") != "end"]


def pipeline(tasks):
    next(tasks[0])
    next(tasks[0])
    yield
    for i, task in enumerate(tasks):
        ahead = i + 1 < len(tasks)
        while next(task, "tail") != "tail":
            if ahead:
                next(tasks[i + 1])
                next(tasks[i + 1])
                ahead = False
            yield
        if ahead:
            next(tasks[i + 1])
            next(tasks[i + 1])
        yield
    for task in tasks:
        for _ in task:
            yield


def rounds(*tasks):
    live = list(tasks)
    while live:
        live = [task for task in live if next(task, "end") != "end"]
        yield


class Behind:
    def __init__(self, task):
        self.task = task

    def __call__(self, steps=1):
        for _ in range(steps):
            next(self.task, None)

    def along(self, task, steps=1):
        for _ in task:
            self(steps)

    def drain(self):
        run(self.task)


def chain_steps(pc):
    chain, z = pc.chain, pc.z
    for k in range(chain - 1):
        for side in (0, 1):
            if side == 0:
                got = z - 1 - k >= 0
                yield k, side, jnp.maximum(z - 1 - k, 0), got, pc.above, jnp.logical_and(got, z + 1 < chain)
            else:
                got = z + 1 + k <= chain - 1
                yield k, side, jnp.minimum(z + 1 + k, chain - 1), got, pc.below, jnp.logical_and(got, z > 0)


def plane_gather(pc, sems, own, out, parts=1):
    chain, z, s = pc.chain, pc.z, pc.s
    width = own.shape[1] // parts
    cp = Copies(sems)
    base = sems.take(1 + 8 * chain * parts)

    def sem(kind, i, p):
        return base + 1 + (kind * chain + i) * parts + p

    def view(b, col, p):
        return out.at[b, col, :, pl.ds(p * width, width)]

    keep = cp.keep(base, own, out.at[z, s])
    for p in range(parts):
        src = own.at[:, pl.ds(p * width, width)]
        cp.go(sem(2, 0, p), src, view(z, s, p), pc.at(s=pc.sy))
        cp.go(sem(4, 0, p), src, view(z, s, p), pc.at(s=pc.sc))
    yield "own"
    for p in range(parts):
        src = own.at[:, pl.ds(p * width, width)]
        if chain > 1:
            cp.go(sem(0, 0, p), src, view(z, s, p), pc.above, z + 1 < chain)
            cp.go(sem(1, 0, p), src, view(z, s, p), pc.below, z > 0)
    yield "start"
    crossing = [(z, None, 0, p) for p in range(parts)]
    landed = []

    def cross(count):
        for _ in range(min(count, len(crossing))):
            b, got, i, p = crossing.pop(0)
            cp.arrive(sem(2, i, p), view(b, pc.sy, p), pc.at(), got)
            cp.go(sem(6, i, p), view(b, pc.sy, p), view(b, pc.sy, p), pc.at(s=pc.sc), got)
            landed.append((b, got, i, p))

    steps = list(chain_steps(pc))
    for k in range(chain - 1):
        for p in range(parts):
            for step, side, b, got, onward, more in steps:
                if step != k:
                    continue
                i = 1 + k if side == 0 else chain + k
                cp.arrive(sem(side, k, p), view(b, s, p), pc.at(), got)
                if k < chain - 2:
                    cp.go(sem(side, k + 1, p), view(b, s, p), view(b, s, p), onward, more)
                cp.go(sem(2, i, p), view(b, s, p), view(b, s, p), pc.at(s=pc.sy), got)
                cp.go(sem(4, i, p), view(b, s, p), view(b, s, p), pc.at(s=pc.sc), got)
                crossing.append((b, got, i, p))
            cross(1 if k == 0 else 2)
            yield "more"
    yield "tail"
    while crossing:
        cross(2)
        yield "more"
    for b, got, i, p in landed:
        cp.arrive(sem(4, i, p), view(b, pc.sc, p), pc.at(), got)
        cp.arrive(sem(6, i, p), view(b, pc.so, p), pc.at(), got)
    keep.wait()
    cp.finish()
    yield


def far_first(chain, z, j):
    if isinstance(j, int) and j == chain - 1:
        return z
    up = jnp.where(j < chain - 1 - z, chain - 1 - j, j - (chain - 1 - z))
    down = jnp.where(j < z, j, chain - 1 - (j - z))
    return jnp.where(j == chain - 1, z, jnp.where(2 * z < chain, up, down))


def each_rows(count, fn, rows=16):
    def body(i, carry):
        fn(pl.ds(pl.multiple_of(i * rows, rows), rows))
        return carry

    lax.fori_loop(0, count // rows, body, 0)


def chain_reduce(pc, cp, right, left, b, last, value, zsend, came, store, rows, cols):
    chain, z = pc.chain, pc.z
    if not last:
        fromleft = jnp.logical_and(b > z, z > 0)
        fromright = jnp.logical_and(b < z, z < chain - 1)
        cp.arrive(right, came.at[b, :, cols], pc.at(), fromleft)
        cp.arrive(left, came.at[b, :, cols], pc.at(), fromright)
        some = jnp.logical_or(fromleft, fromright)

        @pl.when(some)
        def _():
            def add(r):
                zsend[b, r, cols] = (value(r) + came[b, r, cols].astype(F32)).astype(BF)

            each_rows(rows, add)

        @pl.when(jnp.logical_not(some))
        def _():
            def add(r):
                zsend[b, r, cols] = value(r).astype(BF)

            each_rows(rows, add)

        cp.go(right, zsend.at[b, :, cols], came.at[b, :, cols], pc.above, b > z)
        slot = jnp.where(b == z - 1, chain, b)
        cp.go(left, zsend.at[b, :, cols], came.at[slot, :, cols], pc.below, b < z)
        return

    def first(r):
        store(r, value(r), False)

    each_rows(rows, first)
    if chain > 1:

        @pl.when(z > 0)
        def _():
            cp.arrive(right, came.at[b, :, cols], pc.at())

            def add(r):
                store(r, came[b, r, cols].astype(F32), True)

            each_rows(rows, add)

        @pl.when(z < chain - 1)
        def _():
            cp.arrive(left, came.at[chain, :, cols], pc.at())

            def add(r):
                store(r, came[chain, r, cols].astype(F32), True)

            each_rows(rows, add)


def plane_scratch(chain, rows, width):
    return [
        pltpu.VMEM((chain, 2, rows, width), BF),
        pltpu.VMEM((chain, rows, width), BF),
        pltpu.VMEM((chain, rows, width), BF),
        pltpu.VMEM((chain if chain > 1 else 1, rows, width) if chain > 1 else (1, 16, 128), BF),
        pltpu.VMEM((chain + 1, rows, width) if chain > 1 else (1, 16, 128), BF),
    ]


class PlaneReduce:
    def __init__(self, pc, sems, part, scratch, out):
        self.pc, self.part, self.out = pc, part, out
        self.crecv, self.csum, self.yrecv, self.zsend, self.came = scratch
        self.cp = Copies(sems)
        self.base = sems.take(5 * pc.chain)
        self.rows, self.width = out.shape

    def sem(self, kind, i):
        return self.base + kind * self.pc.chain + i

    def block(self, j):
        return far_first(self.pc.chain, self.pc.z, j)

    def pass_core(self, over, j, b, cp=None):
        pc = self.pc
        (cp or self.cp).go(
            self.sem(over, j),
            self.part.at[b, pc.so if over else pc.sc],
            self.crecv.at[b, over],
            pc.at(s=pc.sc),
        )

    def cross(self, j, b, cp=None):
        pc, part, crecv, csum = self.pc, self.part, self.crecv, self.csum
        cp = cp or self.cp
        cp.arrive(self.sem(1, j), crecv.at[b, 1], pc.at())

        def add(r):
            csum[b, r, :] = (part[b, pc.sy, r, :].astype(F32) + crecv[b, 1, r, :].astype(F32)).astype(BF)

        each_rows(self.rows, add)
        cp.go(self.sem(2, j), csum.at[b], self.yrecv.at[b], pc.at(s=pc.sy))

    def started(self):
        for j in range(self.pc.chain):
            b = self.block(j)
            for kind, src in ((1, self.part.at[b, 0]), (0, self.part.at[b, 0]), (2, self.csum.at[b])):
                self.cp.sent.append((self.cp.describe(self.sem(kind, j), src), None))

    def steps(self, crossed=False):
        pc = self.pc
        chain, z = pc.chain, pc.z
        part, crecv, yrecv, out = self.part, self.crecv, self.yrecv, self.out
        cp = self.cp
        todo = [(j, self.block(j)) for j in range(chain)]
        ahead = []
        if crossed:
            self.started()
        else:
            for j, b in todo:
                self.pass_core(1, j, b)
            yield
            ahead = list(todo)
            for _ in range(min(2, chain)):
                self.cross(*ahead.pop(0))
                yield
            for j, b in todo:
                self.pass_core(0, j, b)
            yield
        for j, b in todo:
            cp.arrive(self.sem(0, j), crecv.at[b, 0], pc.at())
            cp.arrive(self.sem(2, j), yrecv.at[b], pc.at())
            if ahead:
                self.cross(*ahead.pop(0))

            def value(r):
                return (
                    part[b, pc.s, r, :].astype(F32)
                    + crecv[b, 0, r, :].astype(F32)
                    + yrecv[b, r, :].astype(F32)
                )

            def store(r, term, more):
                out[r, :] = out[r, :] + term if more else term

            chain_reduce(
                pc,
                cp,
                self.sem(3, b),
                self.sem(4, b),
                b,
                j == chain - 1,
                value,
                self.zsend,
                self.came,
                store,
                self.rows,
                pl.ds(0, self.width),
            )
            yield
        cp.finish()
        yield


def plane_reduce(pc, sems, part, scratch, out):
    return PlaneReduce(pc, sems, part, scratch, out).steps()


def dp_gather(pc, sems, own, out):
    chain, groups, z, t = pc.chain, pc.groups, pc.z, pc.t
    cp = Copies(sems)
    base = sems.take(1 + 2 * chain + 2 * chain * groups)
    along = (base + 1, base + 1 + chain)
    across = base + 1 + 2 * chain
    keep = cp.keep(base, own, out(pc.d))
    for g in range(1, groups):
        cp.go(across + g, own, out(pc.d), pc.at(t=(t + g) % groups))
    yield "own"
    if chain > 1:
        cp.go(along[0], own, out(pc.d), pc.above, z + 1 < chain)
        cp.go(along[1], own, out(pc.d), pc.below, z > 0)
    yield "start"
    landed = [(z, None, 0)]
    for k, side, b, got, onward, more in chain_steps(pc):
        i = 1 + k if side == 0 else chain + k
        block = out(b * groups + t)
        cp.arrive(along[side] + k, block, pc.at(), got)
        if k < chain - 2:
            cp.go(along[side] + k + 1, block, block, onward, more)
        for g in range(1, groups):
            cp.go(across + i * groups + g, block, block, pc.at(t=(t + g) % groups), got)
        landed.append((b, got, i))
        yield "more"
    yield "tail"
    for b, got, i in landed:
        for g in range(1, groups):
            cp.arrive(across + i * groups + g, out(b * groups + (t - g + groups) % groups), pc.at(), got)
    keep.wait()
    cp.finish()
    yield "end"


def spread(pc, sems, blocks, out):
    chain, groups, z, t = pc.chain, pc.groups, pc.z, pc.t
    cp = Copies(sems)
    base = sems.take(1 + chain + chain * groups)
    along, across = base + 1, base + 1 + chain
    keep = cp.keep(base, blocks(z), out(pc.d))
    for g in range(1, groups):
        cp.go(across + g, blocks(z), out(pc.d), pc.at(t=(t + g) % groups))
    yield "own"
    for k in range(1, chain):
        to = (z + k) % chain
        cp.go(along + k, blocks(to), out(pc.d), pc.at(z=to))
    yield "start"
    for k in range(1, chain):
        block = out((z - k + chain) % chain * groups + t)
        cp.arrive(along + k, block, pc.at())
        for g in range(1, groups):
            cp.go(across + k * groups + g, block, block, pc.at(t=(t + g) % groups))
        yield "more"
    yield "tail"
    for k in range(chain):
        for g in range(1, groups):
            block = out((z - k + chain) % chain * groups + (t - g + groups) % groups)
            cp.arrive(across + k * groups + g, block, pc.at())
    keep.wait()
    cp.finish()
    yield "end"


class Side:
    def __init__(self, pc, sems, part, recv):
        self.pc, self.part, self.recv = pc, part, recv
        self.rows, self.width = recv.shape[2], recv.shape[3]
        self.base = sems.take(pc.chain * pc.groups)

    def start(self, i):
        return pl.multiple_of(i * self.rows, self.rows)

    def send(self, cp, j, b):
        pc = self.pc
        for g in range(1, pc.groups):
            to = (pc.t + g) % pc.groups
            cp.go(
                self.base + j * pc.groups + g,
                self.part.at[pl.ds(self.start(b * pc.groups + to), self.rows)],
                self.recv.at[g - 1, b],
                pc.at(t=to),
            )

    def arrive(self, cp, j, b):
        for g in range(1, self.pc.groups):
            cp.arrive(self.base + j * self.pc.groups + g, self.recv.at[g - 1, b], self.pc.at())

    def value(self, b, r):
        at = self.start(b * self.pc.groups + self.pc.t)
        total = self.part[pl.ds(pl.multiple_of(at + r.start, 16), r.size), :].astype(F32)
        for g in range(1, self.pc.groups):
            total = total + self.recv[g - 1, b, r, :].astype(F32)
        return total


def dp_scratch(chain, groups, rows, width):
    return [
        pltpu.VMEM((max(groups - 1, 1), chain, rows, width), BF),
        pltpu.VMEM((chain, rows, width), BF),
        pltpu.VMEM((chain + 1, rows, width), BF),
    ]


def dp_reduce(pc, sems, part, scratch, out, window=2):
    recv, zsend, came = scratch
    chain, z = pc.chain, pc.z
    cp = Copies(sems)
    side = Side(pc, sems, part, recv)
    up, down = sems.take(chain), sems.take(chain)
    todo = [(j, far_first(chain, z, j)) for j in range(chain)]
    ahead = list(todo)
    for _ in range(min(window, chain)):
        side.send(cp, *ahead.pop(0))
    yield
    for j, b in todo:
        side.arrive(cp, j, b)
        if ahead:
            side.send(cp, *ahead.pop(0))

        def value(r):
            return side.value(b, r)

        def store(r, term, more):
            out[r, :] = out[r, :] + term if more else term

        chain_reduce(
            pc, cp, up + b, down + b, b, j == chain - 1, value, zsend, came, store, side.rows, pl.ds(0, side.width)
        )
        yield
    cp.finish()
    yield


def collect_scratch(chain, groups, rows, width):
    return [
        pltpu.VMEM((max(groups - 1, 1), chain, rows, width), BF),
        pltpu.VMEM((chain, rows, width), BF),
    ]


def collect(pc, sems, part, scratch, out, window=2):
    recv, sums = scratch
    chain, z = pc.chain, pc.z
    cp = Copies(sems)
    side = Side(pc, sems, part, recv)
    along = sems.take(chain)
    todo = [(k, (z + chain - 1 - k) % chain) for k in range(chain)]
    ahead = list(todo)
    for _ in range(min(window, chain)):
        side.send(cp, *ahead.pop(0))
    yield "own"
    for k, b in todo:
        side.arrive(cp, k, b)
        if ahead:
            side.send(cp, *ahead.pop(0))

        def add(r):
            sums[b, r, :] = side.value(b, r).astype(BF)

        each_rows(side.rows, add)
        if k < chain - 1:
            cp.go(along + k, sums.at[b], out.at[z], pc.at(z=b))
        else:
            keep = cp.keep(along + k, sums.at[b], out.at[z])
        yield "more"
    yield "tail"
    for k in range(chain - 1):
        b = (z - (chain - 1 - k) + chain) % chain
        cp.arrive(along + k, out.at[b], pc.at())
    keep.wait()
    cp.finish()
    yield "end"


def follow(tasks):
    next(tasks[0])
    yield
    for i, task in enumerate(tasks):
        steps = 0
        while next(task, "tail") != "tail":
            steps += 1
            if steps == 2 and i + 1 < len(tasks):
                next(tasks[i + 1])
            yield
    for task in tasks:
        for _ in task:
            yield


def share_gains(pc, sems, own, table):
    cp = Copies(sems)
    base = sems.take(pc.n_dp + pc.n_t)
    table[pc.d, pc.s] = own[...]
    for k in range(1, pc.n_t):
        cp.go(base + k, table.at[pc.d, pc.s], table.at[pc.d, pc.s], {"dp": pc.d, "tensor": (pc.s + k) % pc.n_t})
    yield
    for k in range(1, pc.n_t):
        cp.arrive(base + k, table.at[pc.d, (pc.s - k + pc.n_t) % pc.n_t], pc.at())
    second = base + pc.n_t
    for k in range(1, pc.n_dp):
        cp.go(second + k, table.at[pc.d], table.at[pc.d], {"dp": (pc.d + k) % pc.n_dp, "tensor": pc.s})
    yield
    for k in range(1, pc.n_dp):
        cp.arrive(second + k, table.at[(pc.d - k + pc.n_dp) % pc.n_dp], pc.at())
    cp.finish()
    yield


def lay_gains(pc, table, gains):
    lanes = 128
    devices = pc.n_dp * pc.n_t
    each = gains.shape[1] // devices
    per = lanes // each
    lane = lax.broadcasted_iota(jnp.int32, (8, lanes), 1)
    for j in range(gains.shape[1] // lanes):
        row = table[(j * per) // pc.n_t, (j * per) % pc.n_t]
        for k in range(1, per):
            o = j * per + k
            row = jnp.where(lane >= k * each, table[o // pc.n_t, o % pc.n_t], row)
        gains[:, j * lanes : (j + 1) * lanes] = row


def sum_gains(pc, sems, groups_of, stage, mid, second, out):
    count = stage.shape[1]
    n_dp, n_t = pc.n_dp, pc.n_t
    cp = Copies(sems)
    base = sems.take(n_dp + n_t)

    def start_of(d):
        return d * groups_of.shape[0] // n_dp

    for k in range(1, n_dp):
        to = (pc.d + k) % n_dp
        cp.go(
            base + k,
            groups_of.at[pl.ds(start_of(to), count)],
            stage.at[pc.d],
            {"dp": to, "tensor": pc.s},
        )
    stage[pc.d] = groups_of[pl.ds(start_of(pc.d), count)]
    yield
    for k in range(1, n_dp):
        cp.arrive(base + k, stage.at[(pc.d - k + n_dp) % n_dp], pc.at())
    total = stage[0]
    for k in range(1, n_dp):
        total = total + stage[k]
    mid[...] = total
    yield
    last = base + n_dp
    for k in range(1, n_t):
        to = (pc.s + k) % n_t
        cp.go(last + k, mid.at[to * count // n_t], second.at[pc.s], {"dp": pc.d, "tensor": to})
    second[pc.s] = mid[pc.s * count // n_t]
    yield
    for k in range(1, n_t):
        cp.arrive(last + k, second.at[(pc.s - k + n_t) % n_t], pc.at())
    total = second[0]
    for k in range(1, n_t):
        total = total + second[k]
    out[...] = total
    cp.finish()
    yield


def call(kernel, name, number, ins, outs, scratch, operands, cost):
    sems = [pltpu.SemaphoreType.DMA((sem_count(),))] * 2
    return pl.pallas_call(
        kernel,
        out_shape=[jax.ShapeDtypeStruct(shape, kind) for shape, kind, _ in outs],
        in_specs=ins,
        out_specs=[space for _, _, space in outs],
        scratch_shapes=list(scratch) + sems,
        name=name,
        cost_estimate=pl.CostEstimate(flops=0, bytes_accessed=cost, transcendentals=0),
        compiler_params=pltpu.CompilerParams(
            collective_id=number, has_side_effects=True, vmem_limit_bytes=63 << 20
        ),
    )(*operands)


def unit(v):
    return lax.rsqrt(jnp.mean(v * v, axis=-1, keepdims=True) + EPS)


def gcd_of(n, size):
    while n % size:
        size //= 2
    return size


def rows_of(ref, count):
    return lambda d: ref.at[pl.ds(pl.multiple_of(d * count, count), count)]


def halves():
    lane = lax.broadcasted_iota(jnp.int32, (1, 128), 1)
    return lane < 64


def turn(x, cosine, sine):
    lane = lax.broadcasted_iota(jnp.int32, x.shape, 1)
    swapped = jnp.where(lane % 64 < 32, pltpu.roll(x, 96, 1), pltpu.roll(x, 32, 1))
    return x * cosine + swapped * sine


def key_range(first, count, total, size):
    long_end = 5 * total // 8
    low = jnp.where(first >= long_end + total // 32 - 16, long_end, 0)
    return low // size, (first + count + size - 1) // size


def fill_bias(bias, low, high, size, qseg, qpos, kseg, kmark):
    def fill(j, carry):
        at = pl.multiple_of(j * size, size)
        cols = pl.ds(at, size)
        kpos = at + lax.broadcasted_iota(jnp.int32, (1, size), 1)
        allowed = (
            (kseg[:, cols] == qseg[...])
            & (kpos <= qpos[...])
            & ((kmark[:, cols] == 1) | (kpos == qpos[...]))
        )
        bias[:, cols] = jnp.where(allowed, 0.0, NEG).astype(BF)
        return carry

    lax.fori_loop(low, high, fill, 0)


def spread_lanes(kv, kk, vv):
    size = gcd_of(kv.shape[0], 256)
    left = lax.broadcasted_iota(jnp.int32, (size, 128), 1) < 64

    def body(j, carry):
        r = pl.ds(pl.multiple_of(j * size, size), size)
        x = kv[r, :].astype(F32)
        y = pltpu.roll(x, 64, 1)
        kk[r, :] = jnp.where(left, x, y).astype(BF)
        vv[r, :] = jnp.where(left, y, x).astype(BF)
        return carry

    lax.fori_loop(0, kv.shape[0] // size, body, 0)


def attend(pc, query, kk, vv, bias, mixed, mixed_low, lse, step):
    local, total = query.shape[0], kk.shape[0]
    size = gcd_of(total, 256)
    tile = local // 2
    left = lax.broadcasted_iota(jnp.int32, (tile, 128), 1) < 64
    lane = lax.broadcasted_iota(jnp.int32, (tile, 128), 1)
    even = jnp.where(halves(), 1.0, 0.0).astype(BF)
    odd = jnp.where(halves(), 0.0, 1.0).astype(BF)
    for i in range(local // tile):
        rows = slice(i * tile, (i + 1) * tile)
        low, high = key_range(pc.d * local + i * tile, tile, total, size)
        stats = jnp.zeros((tile, 128), F32)
        for chunk in range(query.shape[1] // 128):
            lanes = slice(chunk * 128, (chunk + 1) * 128)
            both = query[rows, lanes]
            heads = (both * even, both * odd)

            def body(j, carry):
                cols = pl.ds(pl.multiple_of(j * size, size), size)
                key, value, mask = kk[cols, :], vv[cols, :], bias[rows, cols].astype(F32)
                out = []
                for q, (top, tot, acc) in zip(heads, carry):
                    s = lax.dot_general(q, key, (((1,), (1,)), ((), ())), preferred_element_type=F32) + mask
                    new = jnp.maximum(top, jnp.max(s, axis=1, keepdims=True))
                    shrink = jnp.exp(top - new)
                    p = jnp.exp(s - new)
                    tot = tot * shrink + jnp.sum(p, axis=1, keepdims=True)
                    acc = acc * shrink + jnp.dot(p.astype(BF), value, preferred_element_type=F32)
                    out.append((new, tot, acc))
                return tuple(out)

            start = (jnp.full((tile, 1), NEG, F32), jnp.zeros((tile, 1), F32), jnp.zeros((tile, 128), F32))
            (top0, tot0, acc0), (top1, tot1, acc1) = lax.fori_loop(low, high, body, (start, start))
            result = jnp.where(left, acc0 / tot0, acc1 / tot1)
            mixed[rows, lanes] = result
            mixed_low[rows, lanes] = result.astype(BF)
            stats = jnp.where(lane == 2 * chunk, top0 + jnp.log(tot0), stats)
            stats = jnp.where(lane == 2 * chunk + 1, top1 + jnp.log(tot1), stats)
            step()
        lse[rows, :] = stats


def tiled_nt(left, right, put, size=256):
    size = gcd_of(right.shape[0], size)

    def body(j, carry):
        cols = pl.ds(pl.multiple_of(j * size, size), size)
        put(
            cols,
            lax.dot_general(left, right[cols, :], (((1,), (1,)), ((), ())), preferred_element_type=F32),
        )
        return carry

    lax.fori_loop(0, right.shape[0] // size, body, 0)


def forward_kernel(chain, *refs):
    (tok, own_gain, wqkv, wout, wgate, wup, wdown, cot, cosine, sine, qseg, qpos, kseg, kmark) = refs[:14]
    (
        normed_all,
        gains,
        wqkv_all,
        wout_all,
        wgate_all,
        wup_all,
        wdown_all,
        cot_all,
        query,
        kk,
        vv,
        mixed,
        mixed_low,
        lse,
        middle,
        two_all,
    ) = refs[14:30]
    rest = refs[30:]
    table, normed, own_kv, kv_all, bias, part, total, two = rest[:8]
    scratch, (send, recv) = rest[8:13], rest[13:]
    sems = Sems(send, recv)
    pc, near = Place(chain), Place(1)
    rows, width = tok.shape
    wrows = wqkv.shape[0]
    local = query.shape[0]
    wide = query.shape[1]
    greet(pc)

    def head():
        yield from share_gains(pc, sems, own_gain, table)
        lay_gains(pc, table, gains)

        def norm(r):
            v = tok[r, :].astype(F32)
            normed[r, :] = (v * unit(v) * gains[0:1, :]).astype(BF)

        each_rows(rows, norm)
        yield from plane_gather(near, sems, normed, normed_all)

    first = dp_gather(pc, sems, wqkv, rows_of(wqkv_all, wrows))
    out_weights = dp_gather(pc, sems, wout, rows_of(wout_all, wrows))
    behind = Behind(
        pipeline(
            [
                out_weights,
                spread(pc, sems, lambda d: wgate.at[d], rows_of(wgate_all, wrows)),
                spread(pc, sems, lambda d: wup.at[d], rows_of(wup_all, wrows)),
                plane_gather(pc, sems, cot, cot_all, 2),
                spread(pc, sems, lambda d: wdown.at[d], rows_of(wdown_all, wrows)),
            ]
        )
    )
    beside = head()
    next(beside)
    next(first)
    next(first)
    for state in first:
        next(beside, None)
        if state == "tail":
            break
    behind()
    run(beside)
    run(first)

    here = jnp.concatenate([normed_all[0, s] for s in range(normed_all.shape[1])], axis=0)
    size = 256
    for at in range(0, wide, size):
        pre = jnp.dot(here, wqkv_all[:, at : at + size], preferred_element_type=F32)
        for lanes in range(0, size, 128):
            turned = turn(pre[:, lanes : lanes + 128], cosine[...], sine[...])
            query[:, at + lanes : at + lanes + 128] = (turned * 0.125).astype(BF)
    pre = jnp.dot(here, wqkv_all[:, wide : wide + 128], preferred_element_type=F32)
    own_kv[...] = jnp.where(halves(), turn(pre, cosine[...], sine[...]), pre).astype(BF)
    behind.along(dp_gather(pc, sems, own_kv, rows_of(kv_all, local)))
    spread_lanes(kv_all, kk, vv)
    low, high = key_range(pc.d * local, local, kk.shape[0], size)
    fill_bias(bias, low, high, size, qseg, qpos, kseg, kmark)
    attend(pc, query, kk, vv, bias, mixed, mixed_low, lse, behind)

    run(out_weights)

    def put(cols, value):
        for s in range(part.shape[1]):
            part[0, s, :, cols] = value[s * rows : (s + 1) * rows].astype(BF)

    tiled_nt(mixed_low[...], wout_all, put)
    behind.along(plane_reduce(near, sems, part, scratch, total))

    def norm(r):
        v = tok[r, :].astype(F32) + total[r, :]
        middle[r, :] = v
        two[r, :] = (v * unit(v) * gains[1:2, :]).astype(BF)

    each_rows(rows, norm)
    behind.along(plane_gather(pc, sems, two, two_all, 2))
    behind.drain()


def dot_nt(a, b):
    return lax.dot_general(a, b, (((1,), (1,)), ((), ())), preferred_element_type=F32)


def dot_tn(a, b):
    return lax.dot_general(a, b, (((0,), (0,)), ((), ())), preferred_element_type=F32)


def grads_into(left, right, out, size=256):
    def body(j, carry):
        at = pl.ds(pl.multiple_of(j * size, size), size)
        out[at, :] = dot_tn(left[:, at], right[...]).astype(BF)
        return carry

    lax.fori_loop(0, out.shape[0] // size, body, 0)


def norm_back(r, v, grad, gain, extra, gain_acc):
    root = unit(v)
    xhat = v * root
    e = grad * gain
    gain_acc[...] += grad * xhat
    return extra + root * (e - xhat * jnp.mean(e * xhat, axis=-1, keepdims=True))


def feed_kernel(chain, *refs):
    (two, cotan, wgate, wup, wdown, middle, cot, gains) = refs[:8]
    (opart, middle_grad, branch_all, gain_out, cgate, cup, cdown) = refs[8:15]
    rest = refs[15:]
    npart, hidden, dgate, dup, ggate, gup, gdown = rest[:7]
    s_part = rest[7:12]
    s_gate, s_up, s_down = rest[12:14], rest[14:16], rest[16:18]
    ngrad, branch, gain_acc, send, recv = rest[18:]
    sems = Sems(send, recv)
    pc, near = Place(chain), Place(1)
    greet(pc)
    rows = middle.shape[0]
    n_t = npart.shape[1]
    local = n_t * rows
    reduce = PlaneReduce(pc, sems, npart, s_part, ngrad)

    def tile(j, carry):
        b = far_first(chain, pc.z, j)
        at = pl.ds(pl.multiple_of(b * local, local), local)
        x = two[at, :]
        g = jnp.dot(x, wgate[...], preferred_element_type=F32)
        u = jnp.dot(x, wup[...], preferred_element_type=F32)
        sigma = 1.0 / (1.0 + jnp.exp(-g))
        silu = g * sigma
        hidden[at, :] = (silu * u).astype(BF)
        h = jnp.dot(cotan[at, :], wdown[...], preferred_element_type=F32)
        dg = (h * u * sigma * (1.0 + g * (1.0 - sigma))).astype(BF)
        du = (h * silu).astype(BF)
        dgate[at, :] = dg
        dup[at, :] = du

        def back(i, inner):
            cols = pl.ds(pl.multiple_of(i * 256, 256), 256)
            value = (dot_nt(dg, wgate[cols, :]) + dot_nt(du, wup[cols, :])).astype(BF)
            for s in range(n_t):
                npart[b, s, :, cols] = value[s * rows : (s + 1) * rows]
            return inner

        lax.fori_loop(0, two.shape[1] // 256, back, 0)
        mine = Copies(sems)
        reduce.pass_core(1, j, b, mine)
        reduce.pass_core(0, j, b, mine)

        @pl.when(j > 0)
        def _():
            reduce.cross(j - 1, far_first(chain, pc.z, j - 1), mine)

        return carry

    lax.fori_loop(0, chain, tile, 0)
    reduce.cross(chain - 1, pc.z, Copies(sems))
    steps = reduce.steps(True)
    grads_into(two, dgate, ggate)
    behind = Behind(
        follow(
            [
                collect(pc, sems, ggate, s_gate, cgate),
                collect(pc, sems, gup, s_up, cup),
                collect(pc, sems, gdown, s_down, cdown),
            ]
        )
    )
    behind()
    next(steps)
    grads_into(two, dup, gup)
    behind()
    next(steps)
    grads_into(cotan, hidden, gdown)
    behind()
    next(steps)

    def out_tile(i, carry):
        cols = pl.ds(pl.multiple_of(i * 256, 256), 256)
        for b in range(chain):
            value = dot_nt(hidden[b * local : (b + 1) * local, :], wdown[cols, :]).astype(BF)
            for s in range(n_t):
                opart[b, s, :, cols] = value[s * rows : (s + 1) * rows]
        return carry

    lax.fori_loop(0, two.shape[1] // 256, out_tile, 0)
    behind.along(steps)
    gain_acc[...] = jnp.zeros_like(gain_acc)

    def back(r):
        grad = norm_back(r, middle[r, :], ngrad[r, :], gains[1:2, :], cot[r, :].astype(F32), gain_acc)
        middle_grad[r, :] = grad
        branch[r, :] = grad.astype(BF)

    each_rows(rows, back)
    behind.along(plane_gather(near, sems, branch, branch_all))
    gain_out[...] = jnp.broadcast_to(jnp.sum(gain_acc[...], axis=0, keepdims=True), gain_out.shape)
    behind.drain()


def attend_back(pc, query, dmix, mixed, lse, kk, vv, bias, dsum, dquery, step):
    local, total = query.shape[0], kk.shape[0]
    size = gcd_of(total, 256)
    tile = local // 2
    left = lax.broadcasted_iota(jnp.int32, (tile, 128), 1) < 64
    even = jnp.where(halves(), 1.0, 0.0).astype(BF)
    odd = jnp.where(halves(), 0.0, 1.0).astype(BF)
    for i in range(local // tile):
        rows = slice(i * tile, (i + 1) * tile)
        low, high = key_range(pc.d * local + i * tile, tile, total, size)
        for chunk in range(query.shape[1] // 128):
            lanes = slice(chunk * 128, (chunk + 1) * 128)
            q, dm = query[rows, lanes], dmix[rows, lanes]
            product = dm.astype(F32) * mixed[rows, lanes]
            heads = []
            for k, pick in enumerate((even, odd)):
                mask = left if k == 0 else jnp.logical_not(left)
                delta = jnp.sum(jnp.where(mask, product, 0.0), axis=1, keepdims=True)
                heads.append((q * pick, dm * pick, lse[rows, 2 * chunk + k : 2 * chunk + k + 1], delta))

            def body(j, carry):
                cols = pl.ds(pl.multiple_of(j * size, size), size)
                key, value, mask = kk[cols, :], vv[cols, :], bias[rows, cols].astype(F32)
                out = []
                dk = jnp.zeros((size, 128), F32)
                dv = jnp.zeros((size, 128), F32)
                for (qh, dh, top, delta), acc in zip(heads, carry):
                    p = jnp.exp(dot_nt(qh, key) + mask - top)
                    dp = dot_nt(dh, value)
                    ds = (p * (dp - delta)).astype(BF)
                    dk = dk + dot_tn(ds, qh)
                    dv = dv + dot_tn(p.astype(BF), dh)
                    out.append(acc + jnp.dot(ds, key, preferred_element_type=F32))
                dsum[cols, :] += jnp.where(halves(), dk + pltpu.roll(dk, 64, 1), dv + pltpu.roll(dv, 64, 1))
                return tuple(out)

            zero = jnp.zeros((tile, 128), F32)
            acc0, acc1 = lax.fori_loop(low, high, body, (zero, zero))
            dquery[rows, lanes] = jnp.where(left, acc0, acc1)
            step()


def low_rows(full, low):
    size = gcd_of(full.shape[0], 256)

    def body(j, carry):
        r = pl.ds(pl.multiple_of(j * size, size), size)
        low[r, :] = full[r, :].astype(BF)
        return carry

    lax.fori_loop(0, full.shape[0] // size, body, 0)


def zero_rows(*refs):
    size = gcd_of(refs[0].shape[0], 256)

    def body(j, carry):
        r = pl.ds(pl.multiple_of(j * size, size), size)
        for ref in refs:
            ref[r, :] = jnp.zeros((size, ref.shape[1]), ref.dtype)
        return carry

    lax.fori_loop(0, refs[0].shape[0] // size, body, 0)


def backward_kernel(chain, *refs):
    (branch, wout, wqkv, normed, query, kk, vv, mixed, mixed_low, lse) = refs[:10]
    (tok, middle_grad, gains, gain_two, middle, opart) = refs[10:16]
    (cosine, sine, qseg, qpos, kseg, kmark) = refs[16:22]
    (layer_out, input_grad, qkv_out, kv_out, wout_out, gain_out) = refs[22:28]
    rest = refs[28:]
    (bias, dmix, dsum, dkv, dquery, dkv_own, dqkv, gwo, gq, gkv, part, osum, gain_acc) = rest[:13]
    rest = rest[13:]
    s_out, s_near = rest[:5], rest[5:10]
    s_gwo, s_gq, s_gkv, s_keys = rest[10:13], rest[13:16], rest[16:19], rest[19:22]
    by_group, stage, mid, second, send, recv = rest[22:]
    sems = Sems(send, recv)
    pc, near = Place(chain), Place(1)
    rows, width = tok.shape
    local, wide = query.shape
    greet(pc)

    def finish():
        yield from plane_reduce(pc, sems, opart, s_out, osum)

        def add(r):
            layer_out[r, :] = (middle[r, :] + osum[r, :]).astype(BF)

        each_rows(rows, add)

    whole = branch[...]
    grads_into(branch, mixed_low, gwo)
    behind = Behind(rounds(dp_reduce(pc, sems, gwo, s_gwo, wout_out), finish()))
    behind()
    for at in range(0, wide, 256):
        dmix[:, at : at + 256] = jnp.dot(whole, wout[:, at : at + 256], preferred_element_type=F32).astype(BF)
    size = gcd_of(kk.shape[0], 256)
    low, high = key_range(pc.d * local, local, kk.shape[0], size)
    fill_bias(bias, low, high, size, qseg, qpos, kseg, kmark)
    zero_rows(dsum)
    attend_back(pc, query, dmix, mixed, lse, kk, vv, bias, dsum, dquery, behind)
    low_rows(dsum, dkv)
    keys = dp_reduce(pc, sems, dkv, s_keys, dkv_own)
    next(keys)
    for at in range(0, wide, 128):
        turned = turn(dquery[:, at : at + 128] * 0.125, cosine[...], -sine[...])
        dqkv[:, at : at + 128] = turned.astype(BF)
    def query_grads(j, carry):
        at = pl.ds(pl.multiple_of(j * 256, 256), 256)
        left = jnp.concatenate([normed[0, s, :, at] for s in range(normed.shape[1])], axis=0)
        gq[at, :] = dot_tn(left, dqkv[:, :wide]).astype(BF)
        return carry

    lax.fori_loop(0, width // 256, query_grads, 0)
    last = [dp_reduce(pc, sems, gq, s_gq, qkv_out), dp_reduce(pc, sems, gkv, s_gkv, kv_out)]
    behind.along(keys)
    next(last[0])
    pre = dkv_own[...]
    dqkv[:, wide : wide + 128] = jnp.where(halves(), turn(pre, cosine[...], -sine[...]), pre).astype(BF)

    def put(cols, value):
        for s in range(part.shape[1]):
            part[0, s, :, cols] = value[s * rows : (s + 1) * rows].astype(BF)

    tiled_nt(dqkv[...], wqkv, put)

    def ending():
        yield from plane_reduce(near, sems, part, s_near, input_grad)
        gain_acc[...] = jnp.zeros_like(gain_acc)

        def back(r):
            v = tok[r, :].astype(F32)
            input_grad[r, :] = norm_back(r, v, input_grad[r, :], gains[0:1, :], middle_grad[r, :], gain_acc)

        each_rows(rows, back)
        own = jnp.sum(gain_acc[...], axis=0, keepdims=True)
        row = lax.broadcasted_iota(jnp.int32, (8, 128), 0)
        for j in range(by_group.shape[0]):
            cols = slice(j * 128, (j + 1) * 128)
            by_group[j] = jnp.where(row == 0, jnp.broadcast_to(own[:, cols], (8, 128)), gain_two[:, cols])
        yield from sum_gains(pc, sems, by_group, stage, mid, second, gain_out)

    end = ending()
    next(end)

    def key_grads(j, carry):
        at = pl.ds(pl.multiple_of(j * 256, 256), 256)
        left = jnp.concatenate([normed[0, s, :, at] for s in range(normed.shape[1])], axis=0)
        gkv[at, :] = dot_tn(left, dqkv[:, wide : wide + 128]).astype(BF)
        return carry

    lax.fori_loop(0, width // 256, key_grads, 0)
    run(end, *last, behind.task)


def angles(positions, half_dim):
    frequency = THETA ** (-jnp.arange(half_dim, dtype=F32) / half_dim)
    turned = positions.astype(F32)[:, None] * frequency[None, :]
    return jnp.cos(turned), jnp.sin(turned)


def shards(
    tokens,
    segment_ids,
    key_mask,
    attn_gain,
    w_query,
    w_key,
    w_value,
    w_out,
    mlp_gain,
    w_gate,
    w_up,
    w_down,
    cotangent,
):
    n_dp, n_t = lax.axis_size("dp"), lax.axis_size("tensor")
    chain = 4
    groups = n_dp // chain
    rows, width = tokens.shape
    local = rows * n_t
    total = local * n_dp
    dim = w_key.shape[1]
    heads = w_query.shape[1] // dim
    wrows = w_query.shape[0]
    units = w_gate.shape[1] // chain
    qkv = w_query.shape[1] + 2 * dim
    me = lax.axis_index("dp")
    share = attn_gain.shape[0]
    tile = 128 // share

    first_row = me * local
    own_gain = jnp.concatenate(
        [
            jnp.tile(attn_gain, tile)[None],
            jnp.tile(mlp_gain, tile)[None],
            jnp.zeros((6, 128), F32),
        ],
        axis=0,
    )
    wqkv = jnp.concatenate([w_query, w_key, w_value], axis=1)
    wout = w_out.T

    def by_chain(w):
        return w.reshape(wrows, chain, units).transpose(1, 0, 2)

    plane = chain * n_t * rows
    nbytes = 60 << 20
    positions = first_row + jnp.arange(local, dtype=jnp.int32)
    cosine, sine = angles(positions, dim // 2)
    cosine = jnp.tile(cosine, (1, 4))
    sine = jnp.tile(jnp.concatenate([-sine, sine], axis=1), (1, 2))
    own_segments = lax.dynamic_slice(segment_ids, (first_row,), (local,))
    wide = heads * dim
    (
        normed,
        gains,
        wqkv,
        wout,
        wgate,
        wup,
        wdown,
        cot,
        query,
        kk,
        vv,
        mixed,
        mixed_low,
        lse,
        middle,
        two,
    ) = call(
        functools.partial(forward_kernel, chain),
        "forward",
        0,
        [VM, VM] + [ANY] * 6 + [VM] * 6,
        [
            ((1, n_t, rows, width), BF, VM),
            ((8, width), F32, VM),
            ((width, qkv), BF, VM),
            ((width, wide), BF, VM),
            ((width, units), BF, ANY),
            ((width, units), BF, ANY),
            ((width, units), BF, ANY),
            ((chain, n_t, rows, width), BF, ANY),
            ((local, wide), BF, VM),
            ((total, 128), BF, VM),
            ((total, 128), BF, VM),
            ((local, wide), F32, VM),
            ((local, wide), BF, VM),
            ((local, 128), F32, VM),
            ((rows, width), F32, VM),
            ((chain, n_t, rows, width), BF, ANY),
        ],
        [
            pltpu.VMEM((n_dp, n_t, 8, 128), F32),
            pltpu.VMEM((rows, width), BF),
            pltpu.VMEM((local, 2 * dim), BF),
            pltpu.VMEM((total, 128), BF),
            pltpu.VMEM((local, total), BF),
            pltpu.VMEM((1, n_t, rows, width), BF),
            pltpu.VMEM((rows, width), F32),
            pltpu.VMEM((rows, width), BF),
        ]
        + plane_scratch(1, rows, width),
        (
            tokens,
            own_gain,
            wqkv,
            wout,
            by_chain(w_gate),
            by_chain(w_up),
            by_chain(w_down.T),
            cotangent,
            cosine,
            sine,
            own_segments[:, None],
            positions[:, None],
            segment_ids[None],
            key_mask[None],
        ),
        nbytes,
    )
    cols_sums = [s for _ in range(3) for s in collect_scratch(chain, groups, wrows, units)]
    block = ((chain, wrows, units), BF, ANY)
    (opart, middle_grad, branch, gain_two, ggate, gup, gdown) = call(
        functools.partial(feed_kernel, chain),
        "feed",
        1,
        [VM] * 8,
        [
            ((chain, n_t, rows, width), BF, VM),
            ((rows, width), F32, VM),
            ((1, n_t, rows, width), BF, VM),
            ((8, width), F32, VM),
            block,
            block,
            block,
        ],
        [
            pltpu.VMEM((chain, n_t, rows, width), BF),
            pltpu.VMEM((plane, units), BF),
            pltpu.VMEM((plane, units), BF),
            pltpu.VMEM((plane, units), BF),
            pltpu.VMEM((width, units), BF),
            pltpu.VMEM((width, units), BF),
            pltpu.VMEM((width, units), BF),
        ]
        + plane_scratch(chain, rows, width)
        + cols_sums
        + [
            pltpu.VMEM((rows, width), F32),
            pltpu.VMEM((rows, width), BF),
            pltpu.VMEM((16, width), F32),
        ],
        (two.reshape(plane, width), cot.reshape(plane, width), wgate, wup, wdown, middle, cotangent, gains),
        nbytes,
    )

    def shard_of(g):
        return g.transpose(1, 0, 2).reshape(wrows, chain * units).astype(F32)

    grad_gate, grad_up, grad_down = shard_of(ggate), shard_of(gup), shard_of(gdown).T

    count = max(1, n_t * share // 128)
    layer_out, input_grad, gq, gkv, gwout, gain_sum = call(
        functools.partial(backward_kernel, chain),
        "backward",
        2,
        [VM] * 22,
        [
            ((rows, width), BF, VM),
            ((rows, width), F32, VM),
            ((wrows, wide), F32, VM),
            ((wrows, 2 * dim), F32, VM),
            ((wrows, wide), F32, VM),
            ((8, 128), F32, VM),
        ],
        [
            pltpu.VMEM((local, total), BF),
            pltpu.VMEM((local, wide), BF),
            pltpu.VMEM((total, 128), F32),
            pltpu.VMEM((total, 128), BF),
            pltpu.VMEM((local, wide), F32),
            pltpu.VMEM((local, 128), F32),
            pltpu.VMEM((local, qkv), BF),
            pltpu.VMEM((width, wide), BF),
            pltpu.VMEM((width, wide), BF),
            pltpu.VMEM((width, 128), BF),
            pltpu.VMEM((1, n_t, rows, width), BF),
            pltpu.VMEM((rows, width), F32),
            pltpu.VMEM((16, width), F32),
        ]
        + plane_scratch(chain, rows, width)
        + plane_scratch(1, rows, width)
        + dp_scratch(chain, groups, wrows, wide)
        + dp_scratch(chain, groups, wrows, wide)
        + dp_scratch(chain, groups, wrows, 128)
        + dp_scratch(chain, groups, local, 128)
        + [
            pltpu.VMEM((width // 128, 8, 128), F32),
            pltpu.VMEM((n_dp, count, 8, 128), F32),
            pltpu.VMEM((count, 8, 128), F32),
            pltpu.VMEM((n_t, 8, 128), F32),
        ],
        (
            branch.reshape(local, width),
            wout,
            wqkv,
            normed,
            query,
            kk,
            vv,
            mixed,
            mixed_low,
            lse,
            tokens,
            middle_grad,
            gains,
            gain_two,
            middle,
            opart,
            cosine,
            sine,
            own_segments[:, None],
            positions[:, None],
            segment_ids[None],
            key_mask[None],
        ),
        nbytes,
    )
    lane = (me * n_t + lax.axis_index("tensor")) * share % 128
    gain_grads = lax.dynamic_slice(gain_sum, (0, lane), (2, share))
    return (
        layer_out,
        input_grad,
        gain_grads[0],
        gq,
        gkv[:, :dim],
        gkv[:, dim:],
        gwout.T,
        gain_grads[1],
        grad_gate,
        grad_up,
        grad_down,
    )


def solution(mesh):
    in_specs = (
        P(("dp", "tensor"), None),
        P(),
        P(),
        P(("dp", "tensor")),
        P("dp", "tensor"),
        P("dp", "tensor"),
        P("dp", "tensor"),
        P("tensor", "dp"),
        P(("dp", "tensor")),
        P("dp", "tensor"),
        P("dp", "tensor"),
        P("tensor", "dp"),
        P(("dp", "tensor"), None),
    )
    out_specs = (
        P(("dp", "tensor"), None),
        P(("dp", "tensor"), None),
        P(("dp", "tensor")),
        P("dp", "tensor"),
        P("dp", "tensor"),
        P("dp", "tensor"),
        P("tensor", "dp"),
        P(("dp", "tensor")),
        P("dp", "tensor"),
        P("dp", "tensor"),
        P("tensor", "dp"),
    )
    return jax.shard_map(shards, mesh=mesh, in_specs=in_specs, out_specs=out_specs, check_vma=False)
```

```python
import functools

import jax
import jax.numpy as jnp
from jax import lax
from jax.experimental import pallas as pl
from jax.experimental.pallas import tpu as pltpu
from jax.sharding import PartitionSpec as P

EPS = 1e-05
NEG = -1e30
THETA = 10000.0
BF = jnp.bfloat16
F32 = jnp.float32
MESH = pl.DeviceIdType.MESH
ANY = pl.BlockSpec(memory_space=pl.ANY)
VM = pl.BlockSpec(memory_space=pltpu.VMEM)


def sem_count():
    return 200 + 18 * lax.axis_size("dp")


class Sems:
    def __init__(self, send, recv):
        self.send, self.recv, self.used = send, recv, 0

    def take(self, count):
        base = self.used
        self.used += count
        assert self.used <= sem_count()
        return base


class Place:
    def __init__(self, chain):
        self.n_dp = lax.axis_size("dp")
        self.n_t = lax.axis_size("tensor")
        self.chain = chain
        self.groups = self.n_dp // chain
        self.d = lax.axis_index("dp")
        self.s = lax.axis_index("tensor")
        self.z = self.d // self.groups
        self.t = self.d % self.groups
        self.y = self.s // 2
        self.c = self.s % 2
        self.sy = (1 - self.y) * 2 + self.c
        self.sc = self.y * 2 + 1 - self.c
        self.so = (1 - self.y) * 2 + 1 - self.c
        self.above = self.at(z=jnp.minimum(self.z + 1, chain - 1))
        self.below = self.at(z=jnp.maximum(self.z - 1, 0))

    def at(self, z=None, t=None, s=None):
        z = self.z if z is None else z
        t = self.t if t is None else t
        s = self.s if s is None else s
        return {"dp": z * self.groups + t, "tensor": s}


def when(pred, act):
    if pred is None:
        act()
    else:
        pl.when(pred)(act)


class Copies:
    def __init__(self, sems):
        self.sems = sems
        self.sent = []

    def go(self, i, src, dst, where, pred=None):
        copy = pltpu.make_async_remote_copy(
            src_ref=src,
            dst_ref=dst,
            send_sem=self.sems.send.at[i],
            recv_sem=self.sems.recv.at[i],
            device_id=where,
            device_id_type=MESH,
        )
        when(pred, copy.start)
        self.sent.append((copy, pred))

    def keep(self, i, src, dst):
        copy = pltpu.make_async_copy(src, dst, self.sems.send.at[i])
        copy.start()
        return copy

    def arrive(self, i, dst, where, pred=None):
        copy = pltpu.make_async_remote_copy(
            src_ref=dst,
            dst_ref=dst,
            send_sem=self.sems.send.at[i],
            recv_sem=self.sems.recv.at[i],
            device_id=where,
            device_id_type=MESH,
        )
        when(pred, copy.wait_recv)

    def describe(self, i, src):
        return pltpu.make_async_remote_copy(
            src_ref=src,
            dst_ref=src,
            send_sem=self.sems.send.at[i],
            recv_sem=self.sems.recv.at[i],
            device_id={"dp": lax.axis_index("dp"), "tensor": lax.axis_index("tensor")},
            device_id_type=MESH,
        )

    def finish(self):
        for copy, pred in self.sent:
            when(pred, copy.wait_send)


def greet(pc):
    barrier = pltpu.get_barrier_semaphore()
    for k in range(1, pc.n_dp):
        pl.semaphore_signal(
            barrier, inc=1, device_id={"dp": (pc.d + k) % pc.n_dp, "tensor": pc.s}, device_id_type=MESH
        )
    for k in range(1, pc.n_t):
        pl.semaphore_signal(
            barrier, inc=1, device_id={"dp": pc.d, "tensor": (pc.s + k) % pc.n_t}, device_id_type=MESH
        )
    pl.semaphore_wait(barrier, pc.n_dp + pc.n_t - 2)


def run(*tasks):
    live = list(tasks)
    while live:
        live = [task for task in live if next(task, "end") != "end"]


def go(task, steps):
    for _ in range(steps):
        next(task, None)


class Points:
    def __init__(self, *acts):
        self.acts = list(acts)

    def __call__(self):
        if self.acts:
            for act in self.acts.pop(0):
                act()

    def drain(self):
        while self.acts:
            self()


def chain_steps(pc):
    chain, z = pc.chain, pc.z
    for k in range(chain - 1):
        for side in (0, 1):
            if side == 0:
                got = z - 1 - k >= 0
                yield k, side, jnp.maximum(z - 1 - k, 0), got, pc.above, jnp.logical_and(got, z + 1 < chain)
            else:
                got = z + 1 + k <= chain - 1
                yield k, side, jnp.minimum(z + 1 + k, chain - 1), got, pc.below, jnp.logical_and(got, z > 0)


def plane_gather(pc, sems, own, out, parts=1):
    chain, z, s = pc.chain, pc.z, pc.s
    width = own.shape[1] // parts
    cp = Copies(sems)
    base = sems.take(1 + 8 * chain * parts)

    def sem(kind, i, p):
        return base + 1 + (kind * chain + i) * parts + p

    def view(b, col, p):
        return out.at[b, col, :, pl.ds(p * width, width)]

    keep = cp.keep(base, own, out.at[z, s])
    for p in range(parts):
        src = own.at[:, pl.ds(p * width, width)]
        cp.go(sem(2, 0, p), src, view(z, s, p), pc.at(s=pc.sy))
        cp.go(sem(4, 0, p), src, view(z, s, p), pc.at(s=pc.sc))
    yield "own"
    for p in range(parts):
        src = own.at[:, pl.ds(p * width, width)]
        if chain > 1:
            cp.go(sem(0, 0, p), src, view(z, s, p), pc.above, z + 1 < chain)
            cp.go(sem(1, 0, p), src, view(z, s, p), pc.below, z > 0)
    yield "start"
    crossing = [(z, None, 0, p) for p in range(parts)]
    landed = []

    def cross(count):
        for _ in range(min(count, len(crossing))):
            b, got, i, p = crossing.pop(0)
            cp.arrive(sem(2, i, p), view(b, pc.sy, p), pc.at(), got)
            cp.go(sem(6, i, p), view(b, pc.sy, p), view(b, pc.sy, p), pc.at(s=pc.sc), got)
            landed.append((b, got, i, p))

    steps = list(chain_steps(pc))
    for k in range(chain - 1):
        for p in range(parts):
            for step, side, b, got, onward, more in steps:
                if step != k:
                    continue
                i = 1 + k if side == 0 else chain + k
                cp.arrive(sem(side, k, p), view(b, s, p), pc.at(), got)
                if k < chain - 2:
                    cp.go(sem(side, k + 1, p), view(b, s, p), view(b, s, p), onward, more)
                cp.go(sem(2, i, p), view(b, s, p), view(b, s, p), pc.at(s=pc.sy), got)
                cp.go(sem(4, i, p), view(b, s, p), view(b, s, p), pc.at(s=pc.sc), got)
                crossing.append((b, got, i, p))
            cross(1 if k == 0 else 2)
            yield "more"
    yield "tail"
    while crossing:
        cross(2)
        yield "more"
    for b, got, i, p in landed:
        cp.arrive(sem(4, i, p), view(b, pc.sc, p), pc.at(), got)
        cp.arrive(sem(6, i, p), view(b, pc.so, p), pc.at(), got)
    keep.wait()
    cp.finish()
    yield


def far_first(chain, z, j):
    if isinstance(j, int) and j == chain - 1:
        return z
    up = jnp.where(j < chain - 1 - z, chain - 1 - j, j - (chain - 1 - z))
    down = jnp.where(j < z, j, chain - 1 - (j - z))
    return jnp.where(j == chain - 1, z, jnp.where(2 * z < chain, up, down))


def each_rows(count, fn, rows=16):
    def body(i, carry):
        fn(pl.ds(pl.multiple_of(i * rows, rows), rows))
        return carry

    lax.fori_loop(0, count // rows, body, 0)


def chain_reduce(pc, cp, right, left, b, last, value, zsend, came, store, rows, cols):
    chain, z = pc.chain, pc.z
    if not last:
        fromleft = jnp.logical_and(b > z, z > 0)
        fromright = jnp.logical_and(b < z, z < chain - 1)
        cp.arrive(right, came.at[b, :, cols], pc.at(), fromleft)
        cp.arrive(left, came.at[b, :, cols], pc.at(), fromright)
        some = jnp.logical_or(fromleft, fromright)

        @pl.when(some)
        def _():
            def add(r):
                zsend[b, r, cols] = (value(r) + came[b, r, cols].astype(F32)).astype(BF)

            each_rows(rows, add)

        @pl.when(jnp.logical_not(some))
        def _():
            def add(r):
                zsend[b, r, cols] = value(r).astype(BF)

            each_rows(rows, add)

        cp.go(right, zsend.at[b, :, cols], came.at[b, :, cols], pc.above, b > z)
        slot = jnp.where(b == z - 1, chain, b)
        cp.go(left, zsend.at[b, :, cols], came.at[slot, :, cols], pc.below, b < z)
        return

    def first(r):
        store(r, value(r), False)

    each_rows(rows, first)
    if chain > 1:

        @pl.when(z > 0)
        def _():
            cp.arrive(right, came.at[b, :, cols], pc.at())

            def add(r):
                store(r, came[b, r, cols].astype(F32), True)

            each_rows(rows, add)

        @pl.when(z < chain - 1)
        def _():
            cp.arrive(left, came.at[chain, :, cols], pc.at())

            def add(r):
                store(r, came[chain, r, cols].astype(F32), True)

            each_rows(rows, add)


def plane_scratch(chain, rows, width):
    return [
        pltpu.VMEM((chain, 2, rows, width), BF),
        pltpu.VMEM((chain, rows, width), BF),
        pltpu.VMEM((chain, rows, width), BF),
        pltpu.VMEM((chain if chain > 1 else 1, rows, width) if chain > 1 else (1, 16, 128), BF),
        pltpu.VMEM((chain + 1, rows, width) if chain > 1 else (1, 16, 128), BF),
    ]


class PlaneReduce:
    def __init__(self, pc, sems, part, scratch, out):
        self.pc, self.part, self.out = pc, part, out
        self.crecv, self.csum, self.yrecv, self.zsend, self.came = scratch
        self.cp = Copies(sems)
        self.base = sems.take(5 * pc.chain)
        self.rows, self.width = out.shape

    def sem(self, kind, i):
        return self.base + kind * self.pc.chain + i

    def block(self, j):
        return far_first(self.pc.chain, self.pc.z, j)

    def pass_core(self, over, j, b, cp=None):
        pc = self.pc
        (cp or self.cp).go(
            self.sem(over, j),
            self.part.at[b, pc.so if over else pc.sc],
            self.crecv.at[b, over],
            pc.at(s=pc.sc),
        )

    def cross(self, j, b, cp=None):
        pc, part, crecv, csum = self.pc, self.part, self.crecv, self.csum
        cp = cp or self.cp
        cp.arrive(self.sem(1, j), crecv.at[b, 1], pc.at())

        def add(r):
            csum[b, r, :] = (part[b, pc.sy, r, :].astype(F32) + crecv[b, 1, r, :].astype(F32)).astype(BF)

        each_rows(self.rows, add)
        cp.go(self.sem(2, j), csum.at[b], self.yrecv.at[b], pc.at(s=pc.sy))

    def started(self):
        for j in range(self.pc.chain):
            b = self.block(j)
            for kind, src in ((1, self.part.at[b, 0]), (0, self.part.at[b, 0]), (2, self.csum.at[b])):
                self.cp.sent.append((self.cp.describe(self.sem(kind, j), src), None))

    def steps(self, crossed=False):
        pc = self.pc
        chain, z = pc.chain, pc.z
        part, crecv, yrecv, out = self.part, self.crecv, self.yrecv, self.out
        cp = self.cp
        todo = [(j, self.block(j)) for j in range(chain)]
        ahead = []
        if crossed:
            self.started()
        else:
            for j, b in todo:
                self.pass_core(1, j, b)
            yield
            ahead = list(todo)
            for _ in range(min(2, chain)):
                self.cross(*ahead.pop(0))
                yield
            for j, b in todo:
                self.pass_core(0, j, b)
            yield
        for j, b in todo:
            cp.arrive(self.sem(0, j), crecv.at[b, 0], pc.at())
            cp.arrive(self.sem(2, j), yrecv.at[b], pc.at())
            if ahead:
                self.cross(*ahead.pop(0))

            def value(r):
                return (
                    part[b, pc.s, r, :].astype(F32)
                    + crecv[b, 0, r, :].astype(F32)
                    + yrecv[b, r, :].astype(F32)
                )

            def store(r, term, more):
                out[r, :] = out[r, :] + term if more else term

            chain_reduce(
                pc,
                cp,
                self.sem(3, b),
                self.sem(4, b),
                b,
                j == chain - 1,
                value,
                self.zsend,
                self.came,
                store,
                self.rows,
                pl.ds(0, self.width),
            )
            yield
        cp.finish()
        yield


def plane_reduce(pc, sems, part, scratch, out):
    return PlaneReduce(pc, sems, part, scratch, out).steps()


def dp_gather(pc, sems, own, out, parts=1):
    chain, groups, z, t = pc.chain, pc.groups, pc.z, pc.t
    cp = Copies(sems)
    base = sems.take(1 + (2 * chain + 2 * chain * groups) * parts)
    rows = own.shape[0] // parts

    def cut(ref, p):
        return ref.at[pl.ds(p * rows, rows)]

    def along(side, k, p):
        return base + 1 + (side * chain + k) * parts + p

    def across(i, g, p):
        return base + 1 + (2 * chain + i * groups + g) * parts + p

    keep = cp.keep(base, own, out(pc.d))
    for p in range(parts):
        for g in range(1, groups):
            cp.go(across(0, g, p), cut(own, p), cut(out(pc.d), p), pc.at(t=(t + g) % groups))
    yield "own"
    if chain > 1:
        for p in range(parts):
            cp.go(along(0, 0, p), cut(own, p), cut(out(pc.d), p), pc.above, z + 1 < chain)
            cp.go(along(1, 0, p), cut(own, p), cut(out(pc.d), p), pc.below, z > 0)
    yield "start"
    landed = [(z, None, 0)]
    for k in range(chain - 1):
        for p in range(parts):
            for step, side, b, got, onward, more in chain_steps(pc):
                if step != k:
                    continue
                i = 1 + k if side == 0 else chain + k
                block = cut(out(b * groups + t), p)
                cp.arrive(along(side, k, p), block, pc.at(), got)
                if k < chain - 2:
                    cp.go(along(side, k + 1, p), block, block, onward, more)
                for g in range(1, groups):
                    cp.go(across(i, g, p), block, block, pc.at(t=(t + g) % groups), got)
                if p == 0:
                    landed.append((b, got, i))
            yield "more"
    yield "tail"
    for b, got, i in landed:
        for p in range(parts):
            for g in range(1, groups):
                cp.arrive(across(i, g, p), cut(out(b * groups + (t - g + groups) % groups), p), pc.at(), got)
    keep.wait()
    cp.finish()
    yield "end"


def plane_direct(pc, sems, own, out):
    chain, z, s = pc.chain, pc.z, pc.s
    cp = Copies(sems)
    base = sems.take(1 + 4 * chain)

    def sem(kind, k):
        return base + 1 + kind * chain + k

    keep = cp.keep(base, own, out.at[z, s])
    cp.go(sem(1, 0), own, out.at[z, s], pc.at(s=pc.sy))
    cp.go(sem(2, 0), own, out.at[z, s], pc.at(s=pc.sc))
    yield "own"
    for k in range(1, chain):
        to = (z + k) % chain
        cp.go(sem(0, k), own, out.at[z, s], pc.at(z=to))
    yield "start"
    for k in range(1, chain):
        b = (z - k + chain) % chain
        cp.arrive(sem(0, k), out.at[b, s], pc.at())
        cp.go(sem(1, k), out.at[b, s], out.at[b, s], pc.at(s=pc.sy))
        cp.go(sem(2, k), out.at[b, s], out.at[b, s], pc.at(s=pc.sc))
    yield "turned"
    for k in range(chain):
        b = (z - k + chain) % chain
        cp.arrive(sem(1, k), out.at[b, pc.sy], pc.at())
        cp.go(sem(3, k), out.at[b, pc.sy], out.at[b, pc.sy], pc.at(s=pc.sc))
    yield "crossed"
    for k in range(chain):
        b = (z - k + chain) % chain
        cp.arrive(sem(2, k), out.at[b, pc.sc], pc.at())
        cp.arrive(sem(3, k), out.at[b, pc.so], pc.at())
    keep.wait()
    cp.finish()
    yield "end"


def spread(pc, sems, blocks, out):
    chain, groups, z, t = pc.chain, pc.groups, pc.z, pc.t
    cp = Copies(sems)
    base = sems.take(1 + chain + chain * groups)
    along, across = base + 1, base + 1 + chain
    keep = cp.keep(base, blocks(z), out(pc.d))
    for g in range(1, groups):
        cp.go(across + g, blocks(z), out(pc.d), pc.at(t=(t + g) % groups))
    yield "own"
    for k in range(1, chain):
        to = (z + k) % chain
        cp.go(along + k, blocks(to), out(pc.d), pc.at(z=to))
    yield "start"
    for k in range(1, chain):
        block = out((z - k + chain) % chain * groups + t)
        cp.arrive(along + k, block, pc.at())
        for g in range(1, groups):
            cp.go(across + k * groups + g, block, block, pc.at(t=(t + g) % groups))
        yield "more"
    yield "tail"
    for k in range(chain):
        for g in range(1, groups):
            block = out((z - k + chain) % chain * groups + (t - g + groups) % groups)
            cp.arrive(across + k * groups + g, block, pc.at())
    keep.wait()
    cp.finish()
    yield "end"


class Side:
    def __init__(self, pc, sems, part, recv):
        self.pc, self.part, self.recv = pc, part, recv
        self.rows, self.width = recv.shape[2], recv.shape[3]
        self.base = sems.take(pc.chain * pc.groups)

    def start(self, i):
        return pl.multiple_of(i * self.rows, self.rows)

    def send(self, cp, j, b):
        pc = self.pc
        for g in range(1, pc.groups):
            to = (pc.t + g) % pc.groups
            cp.go(
                self.base + j * pc.groups + g,
                self.part.at[pl.ds(self.start(b * pc.groups + to), self.rows)],
                self.recv.at[g - 1, b],
                pc.at(t=to),
            )

    def arrive(self, cp, j, b):
        for g in range(1, self.pc.groups):
            cp.arrive(self.base + j * self.pc.groups + g, self.recv.at[g - 1, b], self.pc.at())

    def value(self, b, r):
        at = self.start(b * self.pc.groups + self.pc.t)
        total = self.part[pl.ds(pl.multiple_of(at + r.start, 16), r.size), :].astype(F32)
        for g in range(1, self.pc.groups):
            total = total + self.recv[g - 1, b, r, :].astype(F32)
        return total


def dp_scratch(chain, groups, rows, width):
    return [
        pltpu.VMEM((max(groups - 1, 1), chain, rows, width), BF),
        pltpu.VMEM((chain, rows, width), BF),
        pltpu.VMEM((chain, rows, width), BF),
    ]


class Collect:
    def __init__(self, pc, sems, part, scratch, out, summed):
        self.pc, self.out, self.summed = pc, out, summed
        self.side = Side(pc, sems, part, scratch[0])
        self.sums = scratch[1]
        self.came = scratch[2] if summed else out
        self.cp = Copies(sems)
        self.along = sems.take(pc.chain)
        self.kept = None

    def block(self, k):
        return (self.pc.z + self.pc.chain - 1 - k) % self.pc.chain

    def send(self, *which):
        for k in which or range(self.pc.chain):
            self.side.send(self.cp, k, self.block(k))

    def turn(self, *which):
        pc, chain, z, side = self.pc, self.pc.chain, self.pc.z, self.side
        for k in which or range(chain):
            b = self.block(k)
            side.arrive(self.cp, k, b)
            if k == chain - 1 and self.summed:

                def first(r):
                    self.out[r, :] = side.value(b, r)

                each_rows(side.rows, first)
                continue

            def add(r):
                self.sums[b, r, :] = side.value(b, r).astype(BF)

            each_rows(side.rows, add)
            if k < chain - 1:
                self.cp.go(self.along + k, self.sums.at[b], self.came.at[z], pc.at(z=b))
            else:
                self.kept = self.cp.keep(self.along + k, self.sums.at[b], self.out.at[z])

    def finish(self):
        pc, chain, z, side = self.pc, self.pc.chain, self.pc.z, self.side
        for k in range(chain - 1):
            b = (z - (chain - 1 - k) + chain) % chain
            self.cp.arrive(self.along + k, self.came.at[b], pc.at())
            if self.summed:

                def add(r):
                    self.out[r, :] = self.out[r, :] + self.came[b, r, :].astype(F32)

                each_rows(side.rows, add)
        if self.kept is not None:
            self.kept.wait()
        self.cp.finish()


def collect_scratch(chain, groups, rows, width):
    return dp_scratch(chain, groups, rows, width)[:2]


def share_gains(pc, sems, own, table):
    cp = Copies(sems)
    base = sems.take(pc.n_dp + pc.n_t)
    table[pc.d, pc.s] = own[...]
    for k in range(1, pc.n_t):
        cp.go(base + k, table.at[pc.d, pc.s], table.at[pc.d, pc.s], {"dp": pc.d, "tensor": (pc.s + k) % pc.n_t})
    yield
    for k in range(1, pc.n_t):
        cp.arrive(base + k, table.at[pc.d, (pc.s - k + pc.n_t) % pc.n_t], pc.at())
    second = base + pc.n_t
    for k in range(1, pc.n_dp):
        cp.go(second + k, table.at[pc.d], table.at[pc.d], {"dp": (pc.d + k) % pc.n_dp, "tensor": pc.s})
    yield
    for k in range(1, pc.n_dp):
        cp.arrive(second + k, table.at[(pc.d - k + pc.n_dp) % pc.n_dp], pc.at())
    cp.finish()
    yield


def lay_gains(pc, table, gains):
    lanes = 128
    devices = pc.n_dp * pc.n_t
    each = gains.shape[1] // devices
    per = lanes // each
    lane = lax.broadcasted_iota(jnp.int32, (8, lanes), 1)
    for j in range(gains.shape[1] // lanes):
        row = table[(j * per) // pc.n_t, (j * per) % pc.n_t]
        for k in range(1, per):
            o = j * per + k
            row = jnp.where(lane >= k * each, table[o // pc.n_t, o % pc.n_t], row)
        gains[:, j * lanes : (j + 1) * lanes] = row


def sum_gains(pc, sems, groups_of, stage, mid, second, out):
    count = stage.shape[1]
    n_dp, n_t = pc.n_dp, pc.n_t
    cp = Copies(sems)
    base = sems.take(n_dp + n_t)

    def start_of(d):
        return d * groups_of.shape[0] // n_dp

    for k in range(1, n_dp):
        to = (pc.d + k) % n_dp
        cp.go(
            base + k,
            groups_of.at[pl.ds(start_of(to), count)],
            stage.at[pc.d],
            {"dp": to, "tensor": pc.s},
        )
    stage[pc.d] = groups_of[pl.ds(start_of(pc.d), count)]
    yield
    for k in range(1, n_dp):
        cp.arrive(base + k, stage.at[(pc.d - k + n_dp) % n_dp], pc.at())
    total = stage[0]
    for k in range(1, n_dp):
        total = total + stage[k]
    mid[...] = total
    yield
    last = base + n_dp
    for k in range(1, n_t):
        to = (pc.s + k) % n_t
        cp.go(last + k, mid.at[to * count // n_t], second.at[pc.s], {"dp": pc.d, "tensor": to})
    second[pc.s] = mid[pc.s * count // n_t]
    yield
    for k in range(1, n_t):
        cp.arrive(last + k, second.at[(pc.s - k + n_t) % n_t], pc.at())
    total = second[0]
    for k in range(1, n_t):
        total = total + second[k]
    out[...] = total
    cp.finish()
    yield


def call(kernel, name, number, ins, outs, scratch, operands, cost):
    sems = [pltpu.SemaphoreType.DMA((sem_count(),))] * 2
    return pl.pallas_call(
        kernel,
        out_shape=[jax.ShapeDtypeStruct(shape, kind) for shape, kind, _ in outs],
        in_specs=ins,
        out_specs=[space for _, _, space in outs],
        scratch_shapes=list(scratch) + sems,
        name=name,
        cost_estimate=pl.CostEstimate(flops=0, bytes_accessed=cost, transcendentals=0),
        compiler_params=pltpu.CompilerParams(
            collective_id=number, has_side_effects=True, vmem_limit_bytes=63 << 20
        ),
    )(*operands)


def unit(v):
    return lax.rsqrt(jnp.mean(v * v, axis=-1, keepdims=True) + EPS)


def gcd_of(n, size):
    while n % size:
        size //= 2
    return size


def rows_of(ref, count):
    return lambda d: ref.at[pl.ds(pl.multiple_of(d * count, count), count)]


def halves():
    lane = lax.broadcasted_iota(jnp.int32, (1, 128), 1)
    return lane < 64


def turn(x, cosine, sine):
    lane = lax.broadcasted_iota(jnp.int32, x.shape, 1)
    swapped = jnp.where(lane % 64 < 32, pltpu.roll(x, 96, 1), pltpu.roll(x, 32, 1))
    return x * cosine + swapped * sine


def key_range(first, count, total, size):
    long_end = 5 * total // 8
    low = jnp.where(first >= long_end + total // 32 - 16, long_end, 0)
    return low // size, (first + count + size - 1) // size


def fill_bias(bias, low, high, size, qseg, qpos, kseg, kmark):
    def fill(j, carry):
        at = pl.multiple_of(j * size, size)
        cols = pl.ds(at, size)
        kpos = at + lax.broadcasted_iota(jnp.int32, (1, size), 1)
        allowed = (
            (kseg[:, cols] == qseg[...])
            & (kpos <= qpos[...])
            & ((kmark[:, cols] == 1) | (kpos == qpos[...]))
        )
        bias[cols, :] = jnp.where(allowed, 0.0, NEG).T.astype(BF)
        return carry

    lax.fori_loop(low, high, fill, 0)


def turn_values(kv, vt):
    size = gcd_of(kv.shape[0], 256)
    vt[64:80, :] = jnp.ones((16, kv.shape[0]), BF)

    def body(j, carry):
        r = pl.ds(pl.multiple_of(j * size, size), size)
        vt[0:64, r] = kv[r, :].astype(F32).T[64:128, :].astype(BF)
        return carry

    lax.fori_loop(0, kv.shape[0] // size, body, 0)


def turn_keys(kv, kt):
    size = gcd_of(kv.shape[0], 256)

    def body(j, carry):
        r = pl.ds(pl.multiple_of(j * size, size), size)
        kt[:, r] = kv[r, :].astype(F32).T[0:64, :].astype(BF)
        return carry

    lax.fori_loop(0, kv.shape[0] // size, body, 0)


def attend(pc, query_t, kv, vt, bias, mixed_t, mixed_low, lse, step):
    local, total = query_t.shape[1], kv.shape[0]
    size = gcd_of(total, 256)
    low, high = key_range(pc.d * local, local, total, size)
    for chunk in range(query_t.shape[0] // 128):
        first = chunk * 128
        queries = (query_t[first : first + 64, :], query_t[first + 64 : first + 128, :])

        def body(j, carry):
            rows = pl.ds(pl.multiple_of(j * size, size), size)
            key, value, mask = kv[rows, 0:64], vt[:, rows], bias[rows, :].astype(F32)
            out = []
            for q, (top, acc) in zip(queries, carry):
                s = jnp.dot(key, q, preferred_element_type=F32) + mask
                new = jnp.maximum(top, jnp.max(s, axis=0, keepdims=True))
                p = jnp.exp(s - new).astype(BF)
                acc = acc * jnp.exp(top - new) + jnp.dot(value, p, preferred_element_type=F32)
                out.append((new, acc))
            return tuple(out)

        start = (jnp.full((1, local), NEG, F32), jnp.zeros((80, local), F32))
        done = lax.fori_loop(low, high, body, (start, start))
        pair = []
        for k, (top, acc) in enumerate(done):
            tot = acc[64:65, :]
            pair.append(acc[0:64, :] / tot)
            lse[2 * chunk + k : 2 * chunk + k + 1, :] = top + jnp.log(tot)
        both = jnp.concatenate(pair, axis=0)
        mixed_t[first : first + 128, :] = both
        mixed_low[:, first : first + 128] = both.T.astype(BF)
        step()


def tiled_nt(left, right, put, size=256):
    size = gcd_of(right.shape[0], size)

    def body(j, carry):
        cols = pl.ds(pl.multiple_of(j * size, size), size)
        put(
            cols,
            lax.dot_general(left, right[cols, :], (((1,), (1,)), ((), ())), preferred_element_type=F32),
        )
        return carry

    lax.fori_loop(0, right.shape[0] // size, body, 0)


def forward_kernel(chain, *refs):
    (tok, own_gain, wqkv, wout, wgate, wup, wdown, cot, cosine, sine, qseg, qpos, kseg, kmark) = refs[:14]
    (
        normed_all,
        gains,
        wqkv_all,
        wout_all,
        wgu_all,
        wdown_all,
        cot_all,
        query,
        query_t,
        kv_all,
        mixed_t,
        mixed_low,
        lse,
        middle,
        two_all,
    ) = refs[14:29]
    rest = refs[29:]
    table, normed, own_kv, vt, bias, part, total, two = rest[:8]
    scratch, (send, recv) = rest[8:13], rest[13:]
    sems = Sems(send, recv)
    pc, near = Place(chain), Place(1)
    rows, width = tok.shape
    wrows = wqkv.shape[0]
    local = query.shape[0]
    wide = query.shape[1]
    greet(pc)

    def head():
        yield from share_gains(pc, sems, own_gain, table)
        lay_gains(pc, table, gains)

        def norm(r):
            v = tok[r, :].astype(F32)
            normed[r, :] = (v * unit(v) * gains[0:1, :]).astype(BF)

        each_rows(rows, norm)
        yield from plane_gather(near, sems, normed, normed_all)

    first = dp_gather(pc, sems, wqkv, rows_of(wqkv_all, wrows), 2)
    outw = dp_gather(pc, sems, wout, rows_of(wout_all, wrows), 2)
    half = wgu_all.shape[1] // 2
    gatew = spread(pc, sems, lambda d: wgate.at[d], rows_of(wgu_all.at[:, pl.ds(0, half)], wrows))
    upw = spread(pc, sems, lambda d: wup.at[d], rows_of(wgu_all.at[:, pl.ds(half, half)], wrows))
    downw = spread(pc, sems, lambda d: wdown.at[d], rows_of(wdown_all, wrows))
    cots = plane_gather(pc, sems, cot, cot_all, 2)
    beside = head()
    go(first, 2)
    go(beside, 1)
    go(cots, 1)
    go(first, 2)
    go(beside, 1)
    go(first, 2)
    go(cots, 1)
    go(beside, 2)
    go(first, 3)
    go(outw, 2)
    run(beside)
    run(first)
    go(outw, 2)
    go(cots, 2)

    here = jnp.concatenate([normed_all[0, s] for s in range(normed_all.shape[1])], axis=0)
    size = 256
    for at in range(0, wide, size):
        pre = jnp.dot(here, wqkv_all[:, at : at + size], preferred_element_type=F32)
        for lanes in range(0, size, 128):
            turned = turn(pre[:, lanes : lanes + 128], cosine[...], sine[...])
            turned = turned * 0.125
            query[:, at + lanes : at + lanes + 128] = turned.astype(BF)
            query_t[at + lanes : at + lanes + 128, :] = turned.T.astype(BF)
    pre = jnp.dot(here, wqkv_all[:, wide : wide + 128], preferred_element_type=F32)
    own_kv[...] = jnp.where(halves(), turn(pre, cosine[...], sine[...]), pre).astype(BF)
    go(outw, 2)
    run(dp_gather(pc, sems, own_kv, rows_of(kv_all, local)))
    go(gatew, 2)
    go(outw, 3)
    go(cots, 2)
    turn_values(kv_all, vt)
    low, high = key_range(pc.d * local, local, kv_all.shape[0], size)
    fill_bias(bias, low, high, size, qseg, qpos, kseg, kmark)
    go(upw, 2)
    stops = Points(
        [lambda: go(cots, 2)],
        [lambda: go(downw, 2)],
        [lambda: go(gatew, 3)],
        [lambda: run(outw)],
    )
    attend(pc, query_t, kv_all, vt, bias, mixed_t, mixed_low, lse, stops)
    stops.drain()


    def put(cols, value):
        for s in range(part.shape[1]):
            part[0, s, :, cols] = value[s * rows : (s + 1) * rows].astype(BF)

    tiled_nt(mixed_low[...], wout_all, put)
    run(plane_reduce(near, sems, part, scratch, total))
    go(upw, 3)

    def norm(r):
        v = tok[r, :].astype(F32) + total[r, :]
        middle[r, :] = v
        two[r, :] = (v * unit(v) * gains[1:2, :]).astype(BF)

    each_rows(rows, norm)
    twos = plane_gather(pc, sems, two, two_all, 2)
    go(twos, 2)
    go(cots, 3)
    go(twos, 2)
    go(downw, 3)
    run(twos)
    run(cots, gatew, upw, downw)


def dot_nt(a, b):
    return lax.dot_general(a, b, (((1,), (1,)), ((), ())), preferred_element_type=F32)


def dot_tn(a, b):
    return lax.dot_general(a, b, (((0,), (0,)), ((), ())), preferred_element_type=F32)


def grads_into(left, right, out, size=256):
    def body(j, carry):
        at = pl.ds(pl.multiple_of(j * size, size), size)
        out[at, :] = dot_tn(left[:, at], right[...]).astype(BF)
        return carry

    lax.fori_loop(0, out.shape[0] // size, body, 0)


def norm_back(r, v, grad, gain, extra, gain_acc):
    root = unit(v)
    xhat = v * root
    e = grad * gain
    gain_acc[...] += grad * xhat
    return extra + root * (e - xhat * jnp.mean(e * xhat, axis=-1, keepdims=True))


def feed_kernel(chain, *refs):
    (two_all, cot_all, wgu_all, wdn_all, middle, cot, gains) = refs[:7]
    (opart_all, middle_grad, branch_all, gain_out, cgu, cdn) = refs[7:13]
    rest = refs[13:]
    two, cotan, wgu, wdn, opart, gu, h, both, hidden, npart, ggu, gdn = rest[:12]
    s_part = rest[12:17]
    s_gu, s_dn = rest[17:19], rest[19:21]
    branch, gain_acc, local_sem, send, recv = rest[21:]
    sems = Sems(send, recv)
    pc, near = Place(chain), Place(1)
    fetches = []
    for i, (src, dst) in enumerate(((wgu_all, wgu), (two_all, two), (wdn_all, wdn), (cot_all, cotan))):
        fetches.append(pltpu.make_async_copy(src, dst, local_sem.at[i]))
        fetches[-1].start()
    greet(pc)
    rows, width = middle.shape
    n_t = npart.shape[1]
    units = hidden.shape[1]
    reduce = PlaneReduce(pc, sems, npart, s_part, middle_grad)
    fetches[0].wait()
    fetches[1].wait()
    for at in range(0, 2 * units, 256):
        gu[:, at : at + 256] = jnp.dot(two[...], wgu[:, at : at + 256], preferred_element_type=F32)
    fetches[2].wait()
    fetches[3].wait()
    for at in range(0, units, 128):
        h[:, at : at + 128] = jnp.dot(cotan[...], wdn[:, at : at + 128], preferred_element_type=F32)

    def gates(r):
        for at in range(0, units, 128):
            left, right = pl.ds(at, 128), pl.ds(units + at, 128)
            g, u, k = gu[r, left], gu[r, right], h[r, left]
            sigma = 1.0 / (1.0 + jnp.exp(-g))
            silu = g * sigma
            hidden[r, left] = (silu * u).astype(BF)
            both[r, left] = (k * u * sigma * (1.0 + g * (1.0 - sigma))).astype(BF)
            both[r, right] = (k * silu).astype(BF)

    each_rows(two.shape[0], gates, 32)

    def tiled_out(left, right, out):
        def body(i, carry):
            cols = pl.ds(pl.multiple_of(i * 256, 256), 256)
            value = dot_nt(left[...], right[cols, :]).astype(BF)
            out[:, :, :, cols] = value.reshape(chain, n_t, rows, 256)
            return carry

        lax.fori_loop(0, width // 256, body, 0)

    tiled_out(both, wgu, npart)
    steps = reduce.steps()
    go(steps, 4)
    gus = Collect(pc, sems, ggu, s_gu, cgu, False)
    dns = Collect(pc, sems, gdn, s_dn, cdn, False)
    grads_into(two, both, ggu)
    gus.send(0, 1)
    go(steps, 1)
    grads_into(cotan, hidden, gdn)
    go(steps, 1)
    gus.turn(0, 1)
    gus.send(2, 3)
    go(steps, 1)
    dns.send()
    run(steps)
    gus.turn(2, 3)
    gain_acc[...] = jnp.zeros_like(gain_acc)

    def back(r):
        grad = norm_back(r, middle[r, :], middle_grad[r, :], gains[1:2, :], cot[r, :].astype(F32), gain_acc)
        middle_grad[r, :] = grad
        branch[r, :] = grad.astype(BF)

    each_rows(rows, back)
    spreading = plane_gather(near, sems, branch, branch_all)
    go(spreading, 2)
    tiled_out(hidden, wdn, opart)
    store = pltpu.make_async_copy(opart, opart_all, local_sem.at[0])
    store.start()
    run(spreading)
    gain_out[...] = jnp.broadcast_to(jnp.sum(gain_acc[...], axis=0, keepdims=True), gain_out.shape)
    dns.turn()
    gus.finish()
    dns.finish()
    store.wait()


def attend_back(pc, query, query_t, dmix, mixed_t, lse, kv, kt, bias, dsum, put, step):
    local, total = query.shape[0], kv.shape[0]
    size = gcd_of(total, 256)
    low, high = key_range(pc.d * local, local, total, size)
    even = jnp.where(halves(), 1.0, 0.0).astype(BF)
    odd = jnp.where(halves(), 0.0, 1.0).astype(BF)
    none = jnp.zeros((64, local), BF)
    for chunk in range(query.shape[1] // 128):
        first = chunk * 128
        lanes = slice(first, first + 128)
        q, dm = query[:, lanes], dmix[:, lanes]
        turned = dm.astype(F32).T
        product = turned * mixed_t[lanes, :]
        turned = turned.astype(BF)
        heads = []
        for k, pick in enumerate((even, odd)):
            at = slice(k * 64, k * 64 + 64)
            heads.append(
                (
                    query_t[first + k * 64 : first + k * 64 + 64, :],
                    jnp.concatenate([none, turned[at, :]], axis=0),
                    q * pick,
                    dm * pick,
                    lse[2 * chunk + k : 2 * chunk + k + 1, :],
                    jnp.sum(product[at, :], axis=0, keepdims=True),
                )
            )

        def body(j, carry):
            rows = pl.ds(pl.multiple_of(j * size, size), size)
            both, key, key_t, mask = kv[rows, :], kv[rows, 0:64], kt[:, rows], bias[rows, :].astype(F32)
            out = []
            dk = jnp.zeros((size, 128), F32)
            dv = jnp.zeros((size, 128), F32)
            for (qt, dmt, qh, dh, top, delta), acc in zip(heads, carry):
                p = jnp.exp(jnp.dot(key, qt, preferred_element_type=F32) + mask - top)
                dp = jnp.dot(both, dmt, preferred_element_type=F32)
                ds = (p * (dp - delta)).astype(BF)
                dk = dk + jnp.dot(ds, qh, preferred_element_type=F32)
                dv = dv + jnp.dot(p.astype(BF), dh, preferred_element_type=F32)
                out.append(acc + jnp.dot(key_t, ds, preferred_element_type=F32))
            dsum[rows, :] += jnp.where(halves(), dk + pltpu.roll(dk, 64, 1), dv + pltpu.roll(dv, 64, 1))
            return tuple(out)

        zero = jnp.zeros((64, local), F32)
        done = lax.fori_loop(low, high, body, (zero, zero))
        put(lanes, jnp.concatenate(done, axis=0).T)
        step()


def low_rows(full, low):
    size = gcd_of(full.shape[0], 256)

    def body(j, carry):
        r = pl.ds(pl.multiple_of(j * size, size), size)
        low[r, :] = full[r, :].astype(BF)
        return carry

    lax.fori_loop(0, full.shape[0] // size, body, 0)


def zero_rows(*refs):
    size = gcd_of(refs[0].shape[0], 256)

    def body(j, carry):
        r = pl.ds(pl.multiple_of(j * size, size), size)
        for ref in refs:
            ref[r, :] = jnp.zeros((size, ref.shape[1]), ref.dtype)
        return carry

    lax.fori_loop(0, refs[0].shape[0] // size, body, 0)


def backward_kernel(chain, *refs):
    (branch, wout, wqkv, normed, query, query_t, kv, mixed_t, mixed_low, lse) = refs[:10]
    (tok, middle_grad, gains, gain_two, middle, opart) = refs[10:16]
    (cosine, sine, qseg, qpos, kseg, kmark) = refs[16:22]
    (layer_out, input_grad, qkv_out, kv_out, wout_out, gain_out) = refs[22:28]
    rest = refs[28:]
    (kt, bias, dmix, dsum, dkv, dkv_own, dqkv, gwo, gkv, part, osum, gain_acc) = rest[:12]
    gq = gwo
    rest = rest[12:]
    s_out, s_near = rest[:5], rest[5:10]
    s_gwo, s_gq, s_gkv, s_keys = rest[10:13], rest[13:16], rest[16:19], rest[19:22]
    by_group, stage, mid, second, send, recv = rest[22:]
    sems = Sems(send, recv)
    pc, near = Place(chain), Place(1)
    rows, width = tok.shape
    local, wide = query.shape
    greet(pc)

    def finish():
        yield from plane_reduce(pc, sems, opart, s_out, osum)

        def add(r):
            layer_out[r, :] = (middle[r, :] + osum[r, :]).astype(BF)

        each_rows(rows, add)

    whole = branch[...]
    grads_into(branch, mixed_low, gwo)
    out_sum = Collect(pc, sems, gwo, s_gwo, wout_out, True)
    out_sum.send()
    laying = finish()
    go(laying, 1)
    for at in range(0, wide, 256):
        dmix[:, at : at + 256] = jnp.dot(whole, wout[:, at : at + 256], preferred_element_type=F32).astype(BF)
    turn_keys(kv, kt)
    size = gcd_of(kv.shape[0], 256)
    low, high = key_range(pc.d * local, local, kv.shape[0], size)
    fill_bias(bias, low, high, size, qseg, qpos, kseg, kmark)
    zero_rows(dsum)
    stops = Points(
        [lambda: go(laying, 3)],
        [lambda: go(laying, 1)],
        [out_sum.turn, lambda: go(laying, 1)],
        [lambda: go(laying, 1)],
    )

    def put_query(lanes, value):
        dqkv[:, lanes] = turn(value * 0.125, cosine[...], -sine[...]).astype(BF)

    attend_back(pc, query, query_t, dmix, mixed_t, lse, kv, kt, bias, dsum, put_query, stops)
    stops.drain()
    low_rows(dsum, dkv)
    keys = Collect(pc, sems, dkv, s_keys, dkv_own, True)
    keys.send()
    out_sum.finish()
    def query_grads(j, carry):
        at = pl.ds(pl.multiple_of(j * 256, 256), 256)
        left = jnp.concatenate([normed[0, s, :, at] for s in range(normed.shape[1])], axis=0)
        gq[at, :] = dot_tn(left, dqkv[:, :wide]).astype(BF)
        return carry

    lax.fori_loop(0, width // 256, query_grads, 0)
    query_sum = Collect(pc, sems, gq, s_gq, qkv_out, True)
    kv_sum = Collect(pc, sems, gkv, s_gkv, kv_out, True)
    keys.turn()
    query_sum.send()
    keys.finish()
    pre = dkv_own[...]
    dqkv[:, wide : wide + 128] = jnp.where(halves(), turn(pre, cosine[...], -sine[...]), pre).astype(BF)

    def put(cols, value):
        for s in range(part.shape[1]):
            part[0, s, :, cols] = value[s * rows : (s + 1) * rows].astype(BF)

    tiled_nt(dqkv[...], wqkv, put)

    def ending():
        yield from plane_reduce(near, sems, part, s_near, input_grad)
        gain_acc[...] = jnp.zeros_like(gain_acc)

        def back(r):
            v = tok[r, :].astype(F32)
            input_grad[r, :] = norm_back(r, v, input_grad[r, :], gains[0:1, :], middle_grad[r, :], gain_acc)

        each_rows(rows, back)
        own = jnp.sum(gain_acc[...], axis=0, keepdims=True)
        row = lax.broadcasted_iota(jnp.int32, (8, 128), 0)
        for j in range(by_group.shape[0]):
            cols = slice(j * 128, (j + 1) * 128)
            by_group[j] = jnp.where(row == 0, jnp.broadcast_to(own[:, cols], (8, 128)), gain_two[:, cols])
        yield from sum_gains(pc, sems, by_group, stage, mid, second, gain_out)

    end = ending()
    go(end, 1)

    def key_grads(j, carry):
        at = pl.ds(pl.multiple_of(j * 256, 256), 256)
        left = jnp.concatenate([normed[0, s, :, at] for s in range(normed.shape[1])], axis=0)
        gkv[at, :] = dot_tn(left, dqkv[:, wide : wide + 128]).astype(BF)
        return carry

    lax.fori_loop(0, width // 256, key_grads, 0)
    kv_sum.send()
    query_sum.turn(0, 1)
    go(end, 5)
    query_sum.turn(2, 3)
    kv_sum.turn()
    run(end)
    run(laying)
    query_sum.finish()
    kv_sum.finish()


def angles(positions, half_dim):
    frequency = THETA ** (-jnp.arange(half_dim, dtype=F32) / half_dim)
    turned = positions.astype(F32)[:, None] * frequency[None, :]
    return jnp.cos(turned), jnp.sin(turned)


def shards(
    tokens,
    segment_ids,
    key_mask,
    attn_gain,
    w_query,
    w_key,
    w_value,
    w_out,
    mlp_gain,
    w_gate,
    w_up,
    w_down,
    cotangent,
):
    n_dp, n_t = lax.axis_size("dp"), lax.axis_size("tensor")
    chain = 4
    groups = n_dp // chain
    rows, width = tokens.shape
    local = rows * n_t
    total = local * n_dp
    dim = w_key.shape[1]
    heads = w_query.shape[1] // dim
    wrows = w_query.shape[0]
    units = w_gate.shape[1] // chain
    qkv = w_query.shape[1] + 2 * dim
    me = lax.axis_index("dp")
    share = attn_gain.shape[0]
    tile = 128 // share

    first_row = me * local
    own_gain = jnp.concatenate(
        [
            jnp.tile(attn_gain, tile)[None],
            jnp.tile(mlp_gain, tile)[None],
            jnp.zeros((6, 128), F32),
        ],
        axis=0,
    )
    wqkv = jnp.concatenate([w_query, w_key, w_value], axis=1)
    wout = w_out.T

    held = (units + 127) // 128 * 128

    def by_chain(w):
        w = jnp.pad(w.reshape(wrows, chain, units), ((0, 0), (0, 0), (0, held - units)))
        return w.transpose(1, 0, 2)

    plane = chain * n_t * rows
    nbytes = 60 << 20
    positions = first_row + jnp.arange(local, dtype=jnp.int32)
    cosine, sine = angles(positions, dim // 2)
    cosine = jnp.tile(cosine, (1, 4))
    sine = jnp.tile(jnp.concatenate([-sine, sine], axis=1), (1, 2))
    own_segments = lax.dynamic_slice(segment_ids, (first_row,), (local,))
    wide = heads * dim
    (
        normed,
        gains,
        wqkv,
        wout,
        wgu,
        wdn,
        cot,
        query,
        query_t,
        kv,
        mixed,
        mixed_low,
        lse,
        middle,
        two,
    ) = call(
        functools.partial(forward_kernel, chain),
        "forward",
        0,
        [VM, VM] + [ANY] * 6 + [VM] * 6,
        [
            ((1, n_t, rows, width), BF, VM),
            ((8, width), F32, VM),
            ((width, qkv), BF, VM),
            ((width, wide), BF, VM),
            ((width, 2 * held), BF, ANY),
            ((width, held), BF, ANY),
            ((chain, n_t, rows, width), BF, ANY),
            ((local, wide), BF, VM),
            ((wide, local), BF, VM),
            ((total, 128), BF, VM),
            ((wide, local), F32, VM),
            ((local, wide), BF, VM),
            ((heads, local), F32, VM),
            ((rows, width), F32, VM),
            ((chain, n_t, rows, width), BF, ANY),
        ],
        [
            pltpu.VMEM((n_dp, n_t, 8, 128), F32),
            pltpu.VMEM((rows, width), BF),
            pltpu.VMEM((local, 2 * dim), BF),
            pltpu.VMEM((80, total), BF),
            pltpu.VMEM((total, local), BF),
            pltpu.VMEM((1, n_t, rows, width), BF),
            pltpu.VMEM((rows, width), F32),
            pltpu.VMEM((rows, width), BF),
        ]
        + plane_scratch(1, rows, width),
        (
            tokens,
            own_gain,
            wqkv,
            wout,
            by_chain(w_gate),
            by_chain(w_up),
            by_chain(w_down.T),
            cotangent,
            cosine,
            sine,
            own_segments[:, None],
            positions[:, None],
            segment_ids[None],
            key_mask[None],
        ),
        nbytes,
    )
    (opart, middle_grad, branch, gain_two, ggu, gdn) = call(
        functools.partial(feed_kernel, chain),
        "feed",
        1,
        [ANY] * 4 + [VM] * 3,
        [
            ((chain, n_t, rows, width), BF, ANY),
            ((rows, width), F32, VM),
            ((1, n_t, rows, width), BF, ANY),
            ((8, width), F32, VM),
            ((chain, wrows, 2 * held), BF, ANY),
            ((chain, wrows, held), BF, ANY),
        ],
        [
            pltpu.VMEM((plane, width), BF),
            pltpu.VMEM((plane, width), BF),
            pltpu.VMEM((width, 2 * held), BF),
            pltpu.VMEM((width, held), BF),
            pltpu.VMEM((chain, n_t, rows, width), BF),
            pltpu.VMEM((plane, 2 * held), F32),
            pltpu.VMEM((plane, held), F32),
            pltpu.VMEM((plane, 2 * held), BF),
            pltpu.VMEM((plane, held), BF),
            pltpu.VMEM((chain, n_t, rows, width), BF),
            pltpu.VMEM((width, 2 * held), BF),
            pltpu.VMEM((width, held), BF),
        ]
        + plane_scratch(chain, rows, width)
        + collect_scratch(chain, groups, wrows, 2 * held)
        + collect_scratch(chain, groups, wrows, held)
        + [
            pltpu.VMEM((rows, width), BF),
            pltpu.VMEM((16, width), F32),
            pltpu.SemaphoreType.DMA((4,)),
        ],
        (two.reshape(plane, width), cot.reshape(plane, width), wgu, wdn, middle, cotangent, gains),
        nbytes,
    )

    def shard_of(g):
        return g[:, :, :units].transpose(1, 0, 2).reshape(wrows, chain * units).astype(F32)

    grad_gate, grad_up, grad_down = shard_of(ggu), shard_of(ggu[:, :, held:]), shard_of(gdn).T

    count = max(1, n_t * share // 128)
    layer_out, input_grad, gq, gkv, gwout, gain_sum = call(
        functools.partial(backward_kernel, chain),
        "backward",
        2,
        [VM] * 22,
        [
            ((rows, width), BF, VM),
            ((rows, width), F32, VM),
            ((wrows, wide), F32, VM),
            ((wrows, 2 * dim), F32, VM),
            ((wrows, wide), F32, VM),
            ((8, 128), F32, VM),
        ],
        [
            pltpu.VMEM((64, total), BF),
            pltpu.VMEM((total, local), BF),
            pltpu.VMEM((local, wide), BF),
            pltpu.VMEM((total, 128), F32),
            pltpu.VMEM((total, 128), BF),
            pltpu.VMEM((local, 128), F32),
            pltpu.VMEM((local, qkv), BF),
            pltpu.VMEM((width, wide), BF),
            pltpu.VMEM((width, 128), BF),
            pltpu.VMEM((1, n_t, rows, width), BF),
            pltpu.VMEM((rows, width), F32),
            pltpu.VMEM((16, width), F32),
        ]
        + plane_scratch(chain, rows, width)
        + plane_scratch(1, rows, width)
        + dp_scratch(chain, groups, wrows, wide)
        + dp_scratch(chain, groups, wrows, wide)
        + dp_scratch(chain, groups, wrows, 128)
        + dp_scratch(chain, groups, local, 128)
        + [
            pltpu.VMEM((width // 128, 8, 128), F32),
            pltpu.VMEM((n_dp, count, 8, 128), F32),
            pltpu.VMEM((count, 8, 128), F32),
            pltpu.VMEM((n_t, 8, 128), F32),
        ],
        (
            branch.reshape(local, width),
            wout,
            wqkv,
            normed,
            query,
            query_t,
            kv,
            mixed,
            mixed_low,
            lse,
            tokens,
            middle_grad,
            gains,
            gain_two,
            middle,
            opart,
            cosine,
            sine,
            own_segments[:, None],
            positions[:, None],
            segment_ids[None],
            key_mask[None],
        ),
        nbytes,
    )
    lane = (me * n_t + lax.axis_index("tensor")) * share % 128
    gain_grads = lax.dynamic_slice(gain_sum, (0, lane), (2, share))
    return (
        layer_out,
        input_grad,
        gain_grads[0],
        gq,
        gkv[:, :dim],
        gkv[:, dim:],
        gwout.T,
        gain_grads[1],
        grad_gate,
        grad_up,
        grad_down,
    )


def solution(mesh):
    in_specs = (
        P(("dp", "tensor"), None),
        P(),
        P(),
        P(("dp", "tensor")),
        P("dp", "tensor"),
        P("dp", "tensor"),
        P("dp", "tensor"),
        P("tensor", "dp"),
        P(("dp", "tensor")),
        P("dp", "tensor"),
        P("dp", "tensor"),
        P("tensor", "dp"),
        P(("dp", "tensor"), None),
    )
    out_specs = (
        P(("dp", "tensor"), None),
        P(("dp", "tensor"), None),
        P(("dp", "tensor")),
        P("dp", "tensor"),
        P("dp", "tensor"),
        P("dp", "tensor"),
        P("tensor", "dp"),
        P(("dp", "tensor")),
        P("dp", "tensor"),
        P("dp", "tensor"),
        P("tensor", "dp"),
    )
    return jax.shard_map(shards, mesh=mesh, in_specs=in_specs, out_specs=out_specs, check_vma=False)
```

```python
import functools

import jax
import jax.numpy as jnp
from jax import lax
from jax.experimental import pallas as pl
from jax.experimental.pallas import tpu as pltpu
from jax.sharding import PartitionSpec as P

EPS = 1e-05
NEG = -1e30
THETA = 10000.0
BF = jnp.bfloat16
F32 = jnp.float32
MESH = pl.DeviceIdType.MESH
ANY = pl.BlockSpec(memory_space=pl.ANY)
VM = pl.BlockSpec(memory_space=pltpu.VMEM)


def sem_count():
    return 200 + 18 * lax.axis_size("dp")


class Sems:
    def __init__(self, send, recv):
        self.send, self.recv, self.used = send, recv, 0

    def take(self, count):
        base = self.used
        self.used += count
        assert self.used <= sem_count()
        return base


class Place:
    def __init__(self, chain):
        self.n_dp = lax.axis_size("dp")
        self.n_t = lax.axis_size("tensor")
        self.chain = chain
        self.groups = self.n_dp // chain
        self.d = lax.axis_index("dp")
        self.s = lax.axis_index("tensor")
        self.z = self.d // self.groups
        self.t = self.d % self.groups
        self.y = self.s // 2
        self.c = self.s % 2
        self.sy = (1 - self.y) * 2 + self.c
        self.sc = self.y * 2 + 1 - self.c
        self.so = (1 - self.y) * 2 + 1 - self.c
        self.above = self.at(z=jnp.minimum(self.z + 1, chain - 1))
        self.below = self.at(z=jnp.maximum(self.z - 1, 0))

    def at(self, z=None, t=None, s=None):
        z = self.z if z is None else z
        t = self.t if t is None else t
        s = self.s if s is None else s
        return {"dp": z * self.groups + t, "tensor": s}


def when(pred, act):
    if pred is None:
        act()
    else:
        pl.when(pred)(act)


class Copies:
    def __init__(self, sems):
        self.sems = sems
        self.sent = []

    def go(self, i, src, dst, where, pred=None):
        copy = pltpu.make_async_remote_copy(
            src_ref=src,
            dst_ref=dst,
            send_sem=self.sems.send.at[i],
            recv_sem=self.sems.recv.at[i],
            device_id=where,
            device_id_type=MESH,
        )
        when(pred, copy.start)
        self.sent.append((copy, pred))

    def keep(self, i, src, dst):
        copy = pltpu.make_async_copy(src, dst, self.sems.send.at[i])
        copy.start()
        return copy

    def arrive(self, i, dst, where, pred=None):
        copy = pltpu.make_async_remote_copy(
            src_ref=dst,
            dst_ref=dst,
            send_sem=self.sems.send.at[i],
            recv_sem=self.sems.recv.at[i],
            device_id=where,
            device_id_type=MESH,
        )
        when(pred, copy.wait_recv)

    def describe(self, i, src):
        return pltpu.make_async_remote_copy(
            src_ref=src,
            dst_ref=src,
            send_sem=self.sems.send.at[i],
            recv_sem=self.sems.recv.at[i],
            device_id={"dp": lax.axis_index("dp"), "tensor": lax.axis_index("tensor")},
            device_id_type=MESH,
        )

    def finish(self):
        for copy, pred in self.sent:
            when(pred, copy.wait_send)


def greet(pc):
    barrier = pltpu.get_barrier_semaphore()
    for k in range(1, pc.n_dp):
        pl.semaphore_signal(
            barrier, inc=1, device_id={"dp": (pc.d + k) % pc.n_dp, "tensor": pc.s}, device_id_type=MESH
        )
    for k in range(1, pc.n_t):
        pl.semaphore_signal(
            barrier, inc=1, device_id={"dp": pc.d, "tensor": (pc.s + k) % pc.n_t}, device_id_type=MESH
        )
    pl.semaphore_wait(barrier, pc.n_dp + pc.n_t - 2)


def run(*tasks):
    live = list(tasks)
    while live:
        live = [task for task in live if next(task, "end") != "end"]


def go(task, steps):
    for _ in range(steps):
        next(task, None)


class Points:
    def __init__(self, *acts):
        self.acts = list(acts)

    def __call__(self):
        if self.acts:
            for act in self.acts.pop(0):
                act()

    def drain(self):
        while self.acts:
            self()


def chain_steps(pc):
    chain, z = pc.chain, pc.z
    for k in range(chain - 1):
        for side in (0, 1):
            if side == 0:
                got = z - 1 - k >= 0
                yield k, side, jnp.maximum(z - 1 - k, 0), got, pc.above, jnp.logical_and(got, z + 1 < chain)
            else:
                got = z + 1 + k <= chain - 1
                yield k, side, jnp.minimum(z + 1 + k, chain - 1), got, pc.below, jnp.logical_and(got, z > 0)


def plane_gather(pc, sems, own, out, parts=1):
    chain, z, s = pc.chain, pc.z, pc.s
    width = own.shape[1] // parts
    cp = Copies(sems)
    base = sems.take(1 + 8 * chain * parts)

    def sem(kind, i, p):
        return base + 1 + (kind * chain + i) * parts + p

    def view(b, col, p):
        return out.at[b, col, :, pl.ds(p * width, width)]

    keep = cp.keep(base, own, out.at[z, s])
    for p in range(parts):
        src = own.at[:, pl.ds(p * width, width)]
        cp.go(sem(2, 0, p), src, view(z, s, p), pc.at(s=pc.sy))
        cp.go(sem(4, 0, p), src, view(z, s, p), pc.at(s=pc.sc))
    yield "own"
    for p in range(parts):
        src = own.at[:, pl.ds(p * width, width)]
        if chain > 1:
            cp.go(sem(0, 0, p), src, view(z, s, p), pc.above, z + 1 < chain)
            cp.go(sem(1, 0, p), src, view(z, s, p), pc.below, z > 0)
    yield "start"
    crossing = [(z, None, 0, p) for p in range(parts)]
    landed = []

    def cross(count):
        for _ in range(min(count, len(crossing))):
            b, got, i, p = crossing.pop(0)
            cp.arrive(sem(2, i, p), view(b, pc.sy, p), pc.at(), got)
            cp.go(sem(6, i, p), view(b, pc.sy, p), view(b, pc.sy, p), pc.at(s=pc.sc), got)
            landed.append((b, got, i, p))

    steps = list(chain_steps(pc))
    for k in range(chain - 1):
        for p in range(parts):
            for step, side, b, got, onward, more in steps:
                if step != k:
                    continue
                i = 1 + k if side == 0 else chain + k
                cp.arrive(sem(side, k, p), view(b, s, p), pc.at(), got)
                if k < chain - 2:
                    cp.go(sem(side, k + 1, p), view(b, s, p), view(b, s, p), onward, more)
                cp.go(sem(2, i, p), view(b, s, p), view(b, s, p), pc.at(s=pc.sy), got)
                cp.go(sem(4, i, p), view(b, s, p), view(b, s, p), pc.at(s=pc.sc), got)
                crossing.append((b, got, i, p))
            cross(1 if k == 0 else 2)
            yield "more"
    yield "tail"
    while crossing:
        cross(2)
        yield "more"
    for b, got, i, p in landed:
        cp.arrive(sem(4, i, p), view(b, pc.sc, p), pc.at(), got)
        cp.arrive(sem(6, i, p), view(b, pc.so, p), pc.at(), got)
    keep.wait()
    cp.finish()
    yield


def far_first(chain, z, j):
    if isinstance(j, int) and j == chain - 1:
        return z
    up = jnp.where(j < chain - 1 - z, chain - 1 - j, j - (chain - 1 - z))
    down = jnp.where(j < z, j, chain - 1 - (j - z))
    return jnp.where(j == chain - 1, z, jnp.where(2 * z < chain, up, down))


def each_rows(count, fn, rows=16):
    def body(i, carry):
        fn(pl.ds(pl.multiple_of(i * rows, rows), rows))
        return carry

    lax.fori_loop(0, count // rows, body, 0)


def chain_reduce(pc, cp, right, left, b, last, value, zsend, came, store, rows, cols):
    chain, z = pc.chain, pc.z
    if not last:
        fromleft = jnp.logical_and(b > z, z > 0)
        fromright = jnp.logical_and(b < z, z < chain - 1)
        cp.arrive(right, came.at[b, :, cols], pc.at(), fromleft)
        cp.arrive(left, came.at[b, :, cols], pc.at(), fromright)
        some = jnp.logical_or(fromleft, fromright)

        @pl.when(some)
        def _():
            def add(r):
                zsend[b, r, cols] = (value(r) + came[b, r, cols].astype(F32)).astype(BF)

            each_rows(rows, add)

        @pl.when(jnp.logical_not(some))
        def _():
            def add(r):
                zsend[b, r, cols] = value(r).astype(BF)

            each_rows(rows, add)

        cp.go(right, zsend.at[b, :, cols], came.at[b, :, cols], pc.above, b > z)
        slot = jnp.where(b == z - 1, chain, b)
        cp.go(left, zsend.at[b, :, cols], came.at[slot, :, cols], pc.below, b < z)
        return

    def first(r):
        store(r, value(r), False)

    each_rows(rows, first)
    if chain > 1:

        @pl.when(z > 0)
        def _():
            cp.arrive(right, came.at[b, :, cols], pc.at())

            def add(r):
                store(r, came[b, r, cols].astype(F32), True)

            each_rows(rows, add)

        @pl.when(z < chain - 1)
        def _():
            cp.arrive(left, came.at[chain, :, cols], pc.at())

            def add(r):
                store(r, came[chain, r, cols].astype(F32), True)

            each_rows(rows, add)


def plane_scratch(chain, rows, width):
    return [
        pltpu.VMEM((chain, 2, rows, width), BF),
        pltpu.VMEM((chain, rows, width), BF),
        pltpu.VMEM((chain, rows, width), BF),
        pltpu.VMEM((chain if chain > 1 else 1, rows, width) if chain > 1 else (1, 16, 128), BF),
        pltpu.VMEM((chain + 1, rows, width) if chain > 1 else (1, 16, 128), BF),
    ]


class PlaneReduce:
    def __init__(self, pc, sems, part, scratch, out, held=None):
        self.pc, self.part, self.out, self.held = pc, part, out, held
        self.crecv, self.csum, self.yrecv, self.zsend, self.came = scratch
        self.cp = Copies(sems)
        self.base = sems.take(5 * pc.chain)
        self.rows, self.width = out.shape

    def sem(self, kind, i):
        return self.base + kind * self.pc.chain + i

    def block(self, j):
        return far_first(self.pc.chain, self.pc.z, j)

    def pass_core(self, over, j, b, cp=None):
        pc = self.pc
        (cp or self.cp).go(
            self.sem(over, j),
            self.part.at[b, pc.so if over else pc.sc],
            self.crecv.at[b, over],
            pc.at(s=pc.sc),
        )

    def cross(self, j, b, cp=None):
        pc, crecv, csum = self.pc, self.crecv, self.csum
        cp = cp or self.cp
        cp.arrive(self.sem(1, j), crecv.at[b, 1], pc.at())

        def add(r):
            csum[b, r, :] = (self.own(0, b, r).astype(F32) + crecv[b, 1, r, :].astype(F32)).astype(BF)

        each_rows(self.rows, add)
        cp.go(self.sem(2, j), csum.at[b], self.yrecv.at[b], pc.at(s=pc.sy))

    def own(self, here, b, r):
        if self.held is not None:
            return self.held[here, b, r, :]
        return self.part[b, self.pc.s if here else self.pc.sy, r, :]

    def steps(self):
        pc = self.pc
        chain, z = pc.chain, pc.z
        crecv, yrecv, out = self.crecv, self.yrecv, self.out
        cp = self.cp
        todo = [(j, self.block(j)) for j in range(chain)]
        for j, b in todo:
            self.pass_core(1, j, b)
        yield
        ahead = list(todo)
        for _ in range(min(2, chain)):
            self.cross(*ahead.pop(0))
            yield
        for j, b in todo:
            self.pass_core(0, j, b)
        yield
        for j, b in todo:
            cp.arrive(self.sem(0, j), crecv.at[b, 0], pc.at())
            cp.arrive(self.sem(2, j), yrecv.at[b], pc.at())
            if ahead:
                self.cross(*ahead.pop(0))

            def value(r):
                return (
                    self.own(1, b, r).astype(F32)
                    + crecv[b, 0, r, :].astype(F32)
                    + yrecv[b, r, :].astype(F32)
                )

            def store(r, term, more):
                out[r, :] = out[r, :] + term if more else term

            chain_reduce(
                pc,
                cp,
                self.sem(3, b),
                self.sem(4, b),
                b,
                j == chain - 1,
                value,
                self.zsend,
                self.came,
                store,
                self.rows,
                pl.ds(0, self.width),
            )
            yield
        cp.finish()
        yield


def plane_reduce(pc, sems, part, scratch, out):
    return PlaneReduce(pc, sems, part, scratch, out).steps()


def dp_gather(pc, sems, own, out, parts=1):
    chain, groups, z, t = pc.chain, pc.groups, pc.z, pc.t
    cp = Copies(sems)
    base = sems.take(1 + (2 * chain + 2 * chain * groups) * parts)
    rows = own.shape[0] // parts

    def cut(ref, p):
        return ref.at[pl.ds(p * rows, rows)]

    def along(side, k, p):
        return base + 1 + (side * chain + k) * parts + p

    def across(i, g, p):
        return base + 1 + (2 * chain + i * groups + g) * parts + p

    keep = cp.keep(base, own, out(pc.d))
    for p in range(parts):
        for g in range(1, groups):
            cp.go(across(0, g, p), cut(own, p), cut(out(pc.d), p), pc.at(t=(t + g) % groups))
    yield "own"
    if chain > 1:
        for p in range(parts):
            cp.go(along(0, 0, p), cut(own, p), cut(out(pc.d), p), pc.above, z + 1 < chain)
            cp.go(along(1, 0, p), cut(own, p), cut(out(pc.d), p), pc.below, z > 0)
    yield "start"
    landed = [(z, None, 0)]
    for k in range(chain - 1):
        for p in range(parts):
            for step, side, b, got, onward, more in chain_steps(pc):
                if step != k:
                    continue
                i = 1 + k if side == 0 else chain + k
                block = cut(out(b * groups + t), p)
                cp.arrive(along(side, k, p), block, pc.at(), got)
                if k < chain - 2:
                    cp.go(along(side, k + 1, p), block, block, onward, more)
                for g in range(1, groups):
                    cp.go(across(i, g, p), block, block, pc.at(t=(t + g) % groups), got)
                if p == 0:
                    landed.append((b, got, i))
            yield "more"
    yield "tail"
    for b, got, i in landed:
        for p in range(parts):
            for g in range(1, groups):
                cp.arrive(across(i, g, p), cut(out(b * groups + (t - g + groups) % groups), p), pc.at(), got)
    keep.wait()
    cp.finish()
    yield "end"


def plane_direct(pc, sems, own, out):
    chain, z, s = pc.chain, pc.z, pc.s
    cp = Copies(sems)
    base = sems.take(1 + 4 * chain)

    def sem(kind, k):
        return base + 1 + kind * chain + k

    keep = cp.keep(base, own, out.at[z, s])
    cp.go(sem(1, 0), own, out.at[z, s], pc.at(s=pc.sy))
    cp.go(sem(2, 0), own, out.at[z, s], pc.at(s=pc.sc))
    yield "own"
    for k in range(1, chain):
        to = (z + k) % chain
        cp.go(sem(0, k), own, out.at[z, s], pc.at(z=to))
    yield "start"
    for k in range(1, chain):
        b = (z - k + chain) % chain
        cp.arrive(sem(0, k), out.at[b, s], pc.at())
        cp.go(sem(1, k), out.at[b, s], out.at[b, s], pc.at(s=pc.sy))
        cp.go(sem(2, k), out.at[b, s], out.at[b, s], pc.at(s=pc.sc))
    yield "turned"
    for k in range(chain):
        b = (z - k + chain) % chain
        cp.arrive(sem(1, k), out.at[b, pc.sy], pc.at())
        cp.go(sem(3, k), out.at[b, pc.sy], out.at[b, pc.sy], pc.at(s=pc.sc))
    yield "crossed"
    for k in range(chain):
        b = (z - k + chain) % chain
        cp.arrive(sem(2, k), out.at[b, pc.sc], pc.at())
        cp.arrive(sem(3, k), out.at[b, pc.so], pc.at())
    keep.wait()
    cp.finish()
    yield "end"


def spread(pc, sems, blocks, out):
    chain, groups, z, t = pc.chain, pc.groups, pc.z, pc.t
    cp = Copies(sems)
    base = sems.take(1 + chain + chain * groups)
    along, across = base + 1, base + 1 + chain
    keep = cp.keep(base, blocks(z), out(pc.d))
    for g in range(1, groups):
        cp.go(across + g, blocks(z), out(pc.d), pc.at(t=(t + g) % groups))
    yield "own"
    for k in range(1, chain):
        to = (z + k) % chain
        cp.go(along + k, blocks(to), out(pc.d), pc.at(z=to))
    yield "start"
    for k in range(1, chain):
        block = out((z - k + chain) % chain * groups + t)
        cp.arrive(along + k, block, pc.at())
        for g in range(1, groups):
            cp.go(across + k * groups + g, block, block, pc.at(t=(t + g) % groups))
        yield "more"
    yield "tail"
    for k in range(chain):
        for g in range(1, groups):
            block = out((z - k + chain) % chain * groups + (t - g + groups) % groups)
            cp.arrive(across + k * groups + g, block, pc.at())
    keep.wait()
    cp.finish()
    yield "end"


class Side:
    def __init__(self, pc, sems, part, recv):
        self.pc, self.part, self.recv = pc, part, recv
        self.rows, self.width = recv.shape[2], recv.shape[3]
        self.base = sems.take(pc.chain * pc.groups)

    def start(self, i):
        return pl.multiple_of(i * self.rows, self.rows)

    def send(self, cp, j, b):
        pc = self.pc
        for g in range(1, pc.groups):
            to = (pc.t + g) % pc.groups
            cp.go(
                self.base + j * pc.groups + g,
                self.part.at[pl.ds(self.start(b * pc.groups + to), self.rows)],
                self.recv.at[g - 1, b],
                pc.at(t=to),
            )

    def arrive(self, cp, j, b):
        for g in range(1, self.pc.groups):
            cp.arrive(self.base + j * self.pc.groups + g, self.recv.at[g - 1, b], self.pc.at())

    def value(self, b, r):
        at = self.start(b * self.pc.groups + self.pc.t)
        total = self.part[pl.ds(pl.multiple_of(at + r.start, 16), r.size), :].astype(F32)
        for g in range(1, self.pc.groups):
            total = total + self.recv[g - 1, b, r, :].astype(F32)
        return total


def dp_scratch(chain, groups, rows, width):
    return [
        pltpu.VMEM((max(groups - 1, 1), chain, rows, width), BF),
        pltpu.VMEM((chain, rows, width), BF),
        pltpu.VMEM((chain, rows, width), BF),
    ]


class Moves:
    def __init__(self, sem):
        self.sem, self.count = sem, 0

    def start(self, src, dst):
        copy = pltpu.make_async_copy(src, dst, self.sem.at[self.count])
        self.count += 1
        copy.start()
        return copy


class Collect:
    def __init__(self, pc, sems, part, scratch, out, summed):
        self.pc, self.out, self.summed = pc, out, summed
        self.side = Side(pc, sems, part, scratch[0])
        self.sums = scratch[1]
        self.came = scratch[2] if summed else out
        self.cp = Copies(sems)
        self.along = sems.take(pc.chain)
        self.kept = None

    def block(self, k):
        return (self.pc.z + self.pc.chain - 1 - k) % self.pc.chain

    def send(self, *which):
        for k in which or range(self.pc.chain):
            self.side.send(self.cp, k, self.block(k))

    def turn(self, *which):
        pc, chain, z, side = self.pc, self.pc.chain, self.pc.z, self.side
        for k in which or range(chain):
            b = self.block(k)
            side.arrive(self.cp, k, b)
            if k == chain - 1 and self.summed:

                def first(r):
                    self.out[r, :] = side.value(b, r)

                each_rows(side.rows, first)
                continue

            def add(r):
                self.sums[b, r, :] = side.value(b, r).astype(BF)

            each_rows(side.rows, add)
            if k < chain - 1:
                self.cp.go(self.along + k, self.sums.at[b], self.came.at[z], pc.at(z=b))
            else:
                self.kept = self.cp.keep(self.along + k, self.sums.at[b], self.out.at[z])

    def finish(self):
        pc, chain, z, side = self.pc, self.pc.chain, self.pc.z, self.side
        for k in range(chain - 1):
            b = (z - (chain - 1 - k) + chain) % chain
            self.cp.arrive(self.along + k, self.came.at[b], pc.at())
            if self.summed:

                def add(r):
                    self.out[r, :] = self.out[r, :] + self.came[b, r, :].astype(F32)

                each_rows(side.rows, add)
        if self.kept is not None:
            self.kept.wait()
        self.cp.finish()


def collect_scratch(chain, groups, rows, width):
    return dp_scratch(chain, groups, rows, width)[:2]


def share_gains(pc, sems, own, table):
    cp = Copies(sems)
    base = sems.take(pc.n_dp + pc.n_t)
    table[pc.d, pc.s] = own[...]
    for k in range(1, pc.n_t):
        cp.go(base + k, table.at[pc.d, pc.s], table.at[pc.d, pc.s], {"dp": pc.d, "tensor": (pc.s + k) % pc.n_t})
    yield
    for k in range(1, pc.n_t):
        cp.arrive(base + k, table.at[pc.d, (pc.s - k + pc.n_t) % pc.n_t], pc.at())
    second = base + pc.n_t
    for k in range(1, pc.n_dp):
        cp.go(second + k, table.at[pc.d], table.at[pc.d], {"dp": (pc.d + k) % pc.n_dp, "tensor": pc.s})
    yield
    for k in range(1, pc.n_dp):
        cp.arrive(second + k, table.at[(pc.d - k + pc.n_dp) % pc.n_dp], pc.at())
    cp.finish()
    yield


def lay_gains(pc, table, gains):
    lanes = 128
    devices = pc.n_dp * pc.n_t
    each = gains.shape[1] // devices
    per = lanes // each
    lane = lax.broadcasted_iota(jnp.int32, (8, lanes), 1)
    for j in range(gains.shape[1] // lanes):
        row = table[(j * per) // pc.n_t, (j * per) % pc.n_t]
        for k in range(1, per):
            o = j * per + k
            row = jnp.where(lane >= k * each, table[o // pc.n_t, o % pc.n_t], row)
        gains[:, j * lanes : (j + 1) * lanes] = row


def sum_gains(pc, sems, groups_of, stage, mid, second, out):
    count = stage.shape[1]
    n_dp, n_t = pc.n_dp, pc.n_t
    cp = Copies(sems)
    base = sems.take(n_dp + n_t)

    def start_of(d):
        return d * groups_of.shape[0] // n_dp

    for k in range(1, n_dp):
        to = (pc.d + k) % n_dp
        cp.go(
            base + k,
            groups_of.at[pl.ds(start_of(to), count)],
            stage.at[pc.d],
            {"dp": to, "tensor": pc.s},
        )
    stage[pc.d] = groups_of[pl.ds(start_of(pc.d), count)]
    yield
    for k in range(1, n_dp):
        cp.arrive(base + k, stage.at[(pc.d - k + n_dp) % n_dp], pc.at())
    total = stage[0]
    for k in range(1, n_dp):
        total = total + stage[k]
    mid[...] = total
    yield
    last = base + n_dp
    for k in range(1, n_t):
        to = (pc.s + k) % n_t
        cp.go(last + k, mid.at[to * count // n_t], second.at[pc.s], {"dp": pc.d, "tensor": to})
    second[pc.s] = mid[pc.s * count // n_t]
    yield
    for k in range(1, n_t):
        cp.arrive(last + k, second.at[(pc.s - k + n_t) % n_t], pc.at())
    total = second[0]
    for k in range(1, n_t):
        total = total + second[k]
    out[...] = total
    cp.finish()
    yield


def call(kernel, name, number, ins, outs, scratch, operands, cost):
    sems = [pltpu.SemaphoreType.DMA((sem_count(),))] * 2
    return pl.pallas_call(
        kernel,
        out_shape=[jax.ShapeDtypeStruct(shape, kind) for shape, kind, _ in outs],
        in_specs=ins,
        out_specs=[space for _, _, space in outs],
        scratch_shapes=list(scratch) + sems,
        name=name,
        cost_estimate=pl.CostEstimate(flops=0, bytes_accessed=cost, transcendentals=0),
        compiler_params=pltpu.CompilerParams(
            collective_id=number, has_side_effects=True, vmem_limit_bytes=63 << 20
        ),
    )(*operands)


def unit(v):
    return lax.rsqrt(jnp.mean(v * v, axis=-1, keepdims=True) + EPS)


def gcd_of(n, size):
    while n % size:
        size //= 2
    return size


def rows_of(ref, count):
    return lambda d: ref.at[pl.ds(pl.multiple_of(d * count, count), count)]


def halves():
    lane = lax.broadcasted_iota(jnp.int32, (1, 128), 1)
    return lane < 64


def turn(x, cosine, sine):
    lane = lax.broadcasted_iota(jnp.int32, x.shape, 1)
    swapped = jnp.where(lane % 64 < 32, pltpu.roll(x, 96, 1), pltpu.roll(x, 32, 1))
    return x * cosine + swapped * sine


def key_range(first, count, total, size):
    long_end = 5 * total // 8
    low = jnp.where(first >= long_end + total // 32 - 16, long_end, 0)
    return low // size, (first + count + size - 1) // size


def fill_bias(bias, first, low, high, size, qinfo, kinfo):
    qpos = first + lax.broadcasted_iota(jnp.int32, qinfo.shape, 0)

    def fill(j, carry):
        at = pl.multiple_of(j * size, size)
        cols = pl.ds(at, size)
        kpos = at + lax.broadcasted_iota(jnp.int32, (1, size), 1)
        allowed = (kpos == qpos) | ((kinfo[:, cols] == qinfo[...]) & (kpos < qpos))
        bias[cols, :] = jnp.where(allowed, 0.0, NEG).T.astype(BF)
        return carry

    lax.fori_loop(low, high, fill, 0)


def turn_values(kv, vt):
    size = gcd_of(kv.shape[0], 256)
    vt[64:80, :] = jnp.ones((16, kv.shape[0]), BF)

    def body(j, carry):
        r = pl.ds(pl.multiple_of(j * size, size), size)
        vt[0:64, r] = kv[r, :].astype(F32).T[64:128, :].astype(BF)
        return carry

    lax.fori_loop(0, kv.shape[0] // size, body, 0)


def turn_keys(kv, kt):
    size = gcd_of(kv.shape[0], 256)

    def body(j, carry):
        r = pl.ds(pl.multiple_of(j * size, size), size)
        kt[:, r] = kv[r, :].astype(F32).T[0:64, :].astype(BF)
        return carry

    lax.fori_loop(0, kv.shape[0] // size, body, 0)


def attend(pc, query_t, kv, vt, bias, mixed_t, mixed_low, lse, step):
    local, total = query_t.shape[1], kv.shape[0]
    size = gcd_of(total, 640)
    low, high = key_range(pc.d * local, local, total, size)
    for chunk in range(query_t.shape[0] // 128):
        first = chunk * 128
        queries = (query_t[first : first + 64, :], query_t[first + 64 : first + 128, :])

        def body(j, carry):
            rows = pl.ds(pl.multiple_of(j * size, size), size)
            key, value, mask = kv[rows, 0:64], vt[:, rows], bias[rows, :].astype(F32)
            out = []
            for q, (top, acc) in zip(queries, carry):
                s = jnp.dot(key, q, preferred_element_type=F32) + mask
                new = jnp.maximum(top, jnp.max(s, axis=0, keepdims=True))
                p = jnp.exp(s - new).astype(BF)
                acc = acc * jnp.exp(top - new) + jnp.dot(value, p, preferred_element_type=F32)
                out.append((new, acc))
            return tuple(out)

        start = (jnp.full((1, local), NEG, F32), jnp.zeros((80, local), F32))
        done = lax.fori_loop(low, high, body, (start, start))
        pair = []
        for k, (top, acc) in enumerate(done):
            tot = acc[64:65, :]
            pair.append(acc[0:64, :] / tot)
            lse[2 * chunk + k : 2 * chunk + k + 1, :] = top + jnp.log(tot)
        both = jnp.concatenate(pair, axis=0)
        mixed_t[first : first + 128, :] = both
        mixed_low[:, first : first + 128] = both.T.astype(BF)
        step()


def tiled_nt(left, right, put, size=256):
    size = gcd_of(right.shape[0], size)

    def body(j, carry):
        cols = pl.ds(pl.multiple_of(j * size, size), size)
        put(
            cols,
            lax.dot_general(left, right[cols, :], (((1,), (1,)), ((), ())), preferred_element_type=F32),
        )
        return carry

    lax.fori_loop(0, right.shape[0] // size, body, 0)


def forward_kernel(chain, *refs):
    (tok, own_gain, wqkv, wout, wgate, wup, wdown, cot, cosine, sine, qinfo, kinfo) = refs[:12]
    (
        gains,
        wgu_all,
        wdown_all,
        cot_all,
        lse,
        middle,
        two_all,
    ) = refs[12:19]
    kept, rest = refs[19:29], refs[29:]
    (normed_all, wqkv_all, wout_all, query, query_t, kv_all, kt, bias, mixed_t, mixed_low) = rest[:10]
    table, normed, own_kv, vt, part, total, two, local_sem = rest[10:18]
    scratch, (send, recv) = rest[18:23], rest[23:]
    moves = Moves(local_sem)
    stores = []

    def keep(*names):
        for i in names:
            stores.append(moves.start(rest[i], kept[i]))

    sems = Sems(send, recv)
    pc, near = Place(chain), Place(1)
    rows, width = tok.shape
    wrows = wqkv.shape[0]
    local = query.shape[0]
    wide = query.shape[1]
    greet(pc)

    def head():
        yield from share_gains(pc, sems, own_gain, table)
        lay_gains(pc, table, gains)

        def norm(r):
            v = tok[r, :].astype(F32)
            normed[r, :] = (v * unit(v) * gains[0:1, :]).astype(BF)

        each_rows(rows, norm)
        yield from plane_gather(near, sems, normed, normed_all)

    first = dp_gather(pc, sems, wqkv, rows_of(wqkv_all, wrows), 2)
    outw = dp_gather(pc, sems, wout, rows_of(wout_all, wrows), 2)
    half = wgu_all.shape[1] // 2
    gatew = spread(pc, sems, lambda d: wgate.at[d], rows_of(wgu_all.at[:, pl.ds(0, half)], wrows))
    upw = spread(pc, sems, lambda d: wup.at[d], rows_of(wgu_all.at[:, pl.ds(half, half)], wrows))
    downw = spread(pc, sems, lambda d: wdown.at[d], rows_of(wdown_all, wrows))
    cots = plane_gather(pc, sems, cot, cot_all, 2)
    beside = head()
    go(first, 2)
    go(beside, 1)
    go(cots, 1)
    go(first, 2)
    go(beside, 1)
    go(first, 2)
    go(cots, 1)
    go(beside, 2)
    go(first, 3)
    go(outw, 2)
    run(beside)
    run(first)
    go(outw, 2)
    go(cots, 2)

    here = jnp.concatenate([normed_all[0, s] for s in range(normed_all.shape[1])], axis=0)
    size = 256
    for at in range(0, wide, size):
        pre = jnp.dot(here, wqkv_all[:, at : at + size], preferred_element_type=F32)
        for lanes in range(0, size, 128):
            turned = turn(pre[:, lanes : lanes + 128], cosine[...], sine[...])
            turned = turned * 0.125
            query[:, at + lanes : at + lanes + 128] = turned.astype(BF)
            query_t[at + lanes : at + lanes + 128, :] = turned.T.astype(BF)
    pre = jnp.dot(here, wqkv_all[:, wide : wide + 128], preferred_element_type=F32)
    own_kv[...] = jnp.where(halves(), turn(pre, cosine[...], sine[...]), pre).astype(BF)
    go(outw, 2)
    run(dp_gather(pc, sems, own_kv, rows_of(kv_all, local)))
    keep(0, 1, 3, 4, 5)
    go(gatew, 2)
    go(outw, 3)
    go(cots, 2)
    turn_values(kv_all, vt)
    size = gcd_of(kv_all.shape[0], 640)
    low, high = key_range(pc.d * local, local, kv_all.shape[0], size)
    fill_bias(bias, pc.d * local, low, high, size, qinfo, kinfo)
    go(upw, 2)
    stops = Points([], [lambda: go(cots, 2)], [lambda: go(downw, 2)], [lambda: run(outw)])
    attend(pc, query_t, kv_all, vt, bias, mixed_t, mixed_low, lse, stops)
    stops.drain()


    def put(cols, value):
        for s in range(part.shape[1]):
            part[0, s, :, cols] = value[s * rows : (s + 1) * rows].astype(BF)

    tiled_nt(mixed_low[...], wout_all, put)
    totals = plane_reduce(near, sems, part, scratch, total)
    go(totals, 1)
    keep(2, 7, 8, 9)
    go(gatew, 3)
    turn_keys(kv_all, kt)
    keep(6)
    run(totals)

    def norm(r):
        v = tok[r, :].astype(F32) + total[r, :]
        middle[r, :] = v
        two[r, :] = (v * unit(v) * gains[1:2, :]).astype(BF)

    each_rows(rows, norm)
    twos = plane_gather(pc, sems, two, two_all, 2)
    go(twos, 2)
    go(upw, 3)
    go(twos, 2)
    go(cots, 3)
    go(twos, 2)
    go(downw, 3)
    run(twos)
    run(cots, gatew, upw, downw)
    for store in stores:
        store.wait()


def dot_nt(a, b):
    return lax.dot_general(a, b, (((1,), (1,)), ((), ())), preferred_element_type=F32)


def dot_tn(a, b):
    return lax.dot_general(a, b, (((0,), (0,)), ((), ())), preferred_element_type=F32)


def grads_into(left, right, out, size=256):
    def body(j, carry):
        at = pl.ds(pl.multiple_of(j * size, size), size)
        out[at, :] = dot_tn(left[:, at], right[...]).astype(BF)
        return carry

    lax.fori_loop(0, out.shape[0] // size, body, 0)


def norm_back(r, v, grad, gain, extra, gain_acc):
    root = unit(v)
    xhat = v * root
    e = grad * gain
    gain_acc[...] += grad * xhat
    return extra + root * (e - xhat * jnp.mean(e * xhat, axis=-1, keepdims=True))


def feed_kernel(chain, *refs):
    (two_all, cot_all, wgu_all, wdn_all, middle, cot, gains) = refs[:7]
    (opart_all, middle_grad, branch_all, gain_out, cgu, cdn) = refs[7:13]
    rest = refs[13:]
    two, cotan, wgu, wdn, opart, gu, h, both, hidden, npart, ggu, gdn = rest[:12]
    s_part = rest[12:17]
    s_gu, s_dn = rest[17:19], rest[19:21]
    branch, gain_acc, local_sem, send, recv = rest[21:]
    sems = Sems(send, recv)
    pc, near = Place(chain), Place(1)
    fetches = []
    for i, (src, dst) in enumerate(((wgu_all, wgu), (two_all, two), (wdn_all, wdn), (cot_all, cotan))):
        fetches.append(pltpu.make_async_copy(src, dst, local_sem.at[i]))
        fetches[-1].start()
    greet(pc)
    rows, width = middle.shape
    n_t = npart.shape[1]
    units = hidden.shape[1]
    reduce = PlaneReduce(pc, sems, npart, s_part, middle_grad)
    fetches[0].wait()
    fetches[1].wait()
    for at in range(0, 2 * units, 256):
        gu[:, at : at + 256] = jnp.dot(two[...], wgu[:, at : at + 256], preferred_element_type=F32)
    fetches[2].wait()
    fetches[3].wait()
    for at in range(0, units, 128):
        h[:, at : at + 128] = jnp.dot(cotan[...], wdn[:, at : at + 128], preferred_element_type=F32)

    def gates(r):
        for at in range(0, units, 128):
            left, right = pl.ds(at, 128), pl.ds(units + at, 128)
            g, u, k = gu[r, left], gu[r, right], h[r, left]
            sigma = 1.0 / (1.0 + jnp.exp(-g))
            silu = g * sigma
            hidden[r, left] = (silu * u).astype(BF)
            both[r, left] = (k * u * sigma * (1.0 + g * (1.0 - sigma))).astype(BF)
            both[r, right] = (k * silu).astype(BF)

    each_rows(two.shape[0], gates, 32)

    def tiled_out(left, right, out):
        def body(i, carry):
            cols = pl.ds(pl.multiple_of(i * 256, 256), 256)
            value = dot_nt(left[...], right[cols, :]).astype(BF)
            out[:, :, :, cols] = value.reshape(chain, n_t, rows, 256)
            return carry

        lax.fori_loop(0, width // 256, body, 0)

    tiled_out(both, wgu, npart)
    steps = reduce.steps()
    go(steps, 4)
    gus = Collect(pc, sems, ggu, s_gu, cgu, False)
    dns = Collect(pc, sems, gdn, s_dn, cdn, False)
    grads_into(two, both, ggu)
    gus.send(0, 1)
    go(steps, 1)
    grads_into(cotan, hidden, gdn)
    go(steps, 1)
    gus.turn(0, 1)
    gus.send(2, 3)
    go(steps, 1)
    dns.send()
    run(steps)
    gus.turn(2, 3)
    gain_acc[...] = jnp.zeros_like(gain_acc)

    def back(r):
        grad = norm_back(r, middle[r, :], middle_grad[r, :], gains[1:2, :], cot[r, :].astype(F32), gain_acc)
        middle_grad[r, :] = grad
        branch[r, :] = grad.astype(BF)

    each_rows(rows, back)
    spreading = plane_gather(near, sems, branch, branch_all)
    go(spreading, 2)
    tiled_out(hidden, wdn, opart)
    store = pltpu.make_async_copy(opart, opart_all, local_sem.at[0])
    store.start()
    run(spreading)
    gain_out[...] = jnp.broadcast_to(jnp.sum(gain_acc[...], axis=0, keepdims=True), gain_out.shape)
    dns.turn()
    gus.finish()
    dns.finish()
    store.wait()


def attend_back(pc, query, query_t, dmix, mixed_t, lse, kv, kt, bias, dsum, put, step):
    local, total = query.shape[0], kv.shape[0]
    size = gcd_of(total, 640)
    low, high = key_range(pc.d * local, local, total, size)
    even = jnp.where(halves(), 1.0, 0.0).astype(BF)
    odd = jnp.where(halves(), 0.0, 1.0).astype(BF)
    none = jnp.zeros((64, local), BF)
    for chunk in range(query.shape[1] // 128):
        first = chunk * 128
        lanes = slice(first, first + 128)
        q, dm = query[:, lanes], dmix[:, lanes]
        turned = dm.astype(F32).T
        product = turned * mixed_t[lanes, :]
        turned = turned.astype(BF)
        heads = []
        for k, pick in enumerate((even, odd)):
            at = slice(k * 64, k * 64 + 64)
            heads.append(
                (
                    query_t[first + k * 64 : first + k * 64 + 64, :],
                    jnp.concatenate([none, turned[at, :]], axis=0),
                    q * pick,
                    dm * pick,
                    lse[2 * chunk + k : 2 * chunk + k + 1, :],
                    jnp.sum(product[at, :], axis=0, keepdims=True),
                )
            )

        def body(j, carry):
            rows = pl.ds(pl.multiple_of(j * size, size), size)
            both, key, key_t, mask = kv[rows, :], kv[rows, 0:64], kt[:, rows], bias[rows, :].astype(F32)
            out = []
            dk = jnp.zeros((size, 128), F32)
            dv = jnp.zeros((size, 128), F32)
            for (qt, dmt, qh, dh, top, delta), acc in zip(heads, carry):
                p = jnp.exp(jnp.dot(key, qt, preferred_element_type=F32) + mask - top)
                dp = jnp.dot(both, dmt, preferred_element_type=F32)
                ds = (p * (dp - delta)).astype(BF)
                dk = dk + jnp.dot(ds, qh, preferred_element_type=F32)
                dv = dv + jnp.dot(p.astype(BF), dh, preferred_element_type=F32)
                out.append(acc + jnp.dot(key_t, ds, preferred_element_type=F32))
            dsum[rows, :] += jnp.where(halves(), dk + pltpu.roll(dk, 64, 1), dv + pltpu.roll(dv, 64, 1))
            return tuple(out)

        zero = jnp.zeros((64, local), F32)
        done = lax.fori_loop(low, high, body, (zero, zero))
        put(lanes, jnp.concatenate(done, axis=0).T)
        step()


def low_rows(full, low):
    size = gcd_of(full.shape[0], 256)

    def body(j, carry):
        r = pl.ds(pl.multiple_of(j * size, size), size)
        low[r, :] = full[r, :].astype(BF)
        return carry

    lax.fori_loop(0, full.shape[0] // size, body, 0)


def zero_rows(*refs):
    size = gcd_of(refs[0].shape[0], 256)

    def body(j, carry):
        r = pl.ds(pl.multiple_of(j * size, size), size)
        for ref in refs:
            ref[r, :] = jnp.zeros((size, ref.shape[1]), ref.dtype)
        return carry

    lax.fori_loop(0, refs[0].shape[0] // size, body, 0)


def backward_kernel(chain, *refs):
    kept, branch_all, opart = refs[:10], refs[10], refs[11]
    (lse, tok, middle_grad, gains, gain_two, middle, cosine, sine) = refs[12:20]
    (layer_out, input_grad, qkv_out, kv_out, wout_out, gain_out) = refs[20:26]
    rest = refs[26:]
    (normed, wqkv, wout, query, query_t, kv, kt, bias, mixed_t, mixed_low) = rest[:10]
    (branch_in, held, local_sem) = rest[10:13]
    (dmix, dsum, dkv, dkv_own, dqkv, gwo, gkv, part, osum, gain_acc) = rest[13:23]
    gq = gwo
    rest = rest[23:]
    s_out, s_near = rest[:5], rest[5:10]
    s_gwo, s_gq, s_gkv, s_keys = rest[10:13], rest[13:16], rest[16:19], rest[19:22]
    by_group, stage, mid, second, send, recv = rest[22:]
    sems = Sems(send, recv)
    pc, near = Place(chain), Place(1)
    rows, width = tok.shape
    local, wide = query.shape
    moves = Moves(local_sem)
    inner = (normed, wqkv, wout, query, query_t, kv, kt, bias, mixed_t, mixed_low)
    fetches = {}
    fetches[10] = moves.start(branch_all, branch_in)
    for i in (9, 2):
        fetches[i] = moves.start(kept[i], inner[i])
    halves_of = [
        moves.start(opart.at[:, col], held.at[i]) for i, col in enumerate((pc.sy, pc.s))
    ]
    for i in (7, 5, 6, 3, 4, 8, 0, 1):
        fetches[i] = moves.start(kept[i], inner[i])
    greet(pc)

    def finish():
        yield from PlaneReduce(pc, sems, opart, s_out, osum, held).steps()

        def add(r):
            layer_out[r, :] = (middle[r, :] + osum[r, :]).astype(BF)

        each_rows(rows, add)

    fetches[10].wait()
    fetches[9].wait()
    branch = branch_in
    whole = branch[...]
    grads_into(branch, mixed_low, gwo)
    out_sum = Collect(pc, sems, gwo, s_gwo, wout_out, True)
    out_sum.send()
    laying = finish()
    go(laying, 1)
    for fetch in halves_of:
        fetch.wait()
    fetches[2].wait()
    for at in range(0, wide, 256):
        dmix[:, at : at + 256] = jnp.dot(whole, wout[:, at : at + 256], preferred_element_type=F32).astype(BF)
    zero_rows(dsum)
    for i in (7, 5, 6, 3, 4, 8):
        fetches[i].wait()
    stops = Points(
        [lambda: go(laying, 3)],
        [lambda: go(laying, 1)],
        [out_sum.turn, lambda: go(laying, 1)],
        [lambda: go(laying, 1)],
    )

    def put_query(lanes, value):
        dqkv[:, lanes] = turn(value * 0.125, cosine[...], -sine[...]).astype(BF)

    attend_back(pc, query, query_t, dmix, mixed_t, lse, kv, kt, bias, dsum, put_query, stops)
    stops.drain()
    low_rows(dsum, dkv)
    keys = Collect(pc, sems, dkv, s_keys, dkv_own, True)
    keys.send()
    out_sum.finish()
    fetches[0].wait()
    fetches[1].wait()

    def query_grads(j, carry):
        at = pl.ds(pl.multiple_of(j * 256, 256), 256)
        left = jnp.concatenate([normed[0, s, :, at] for s in range(normed.shape[1])], axis=0)
        gq[at, :] = dot_tn(left, dqkv[:, :wide]).astype(BF)
        return carry

    lax.fori_loop(0, width // 256, query_grads, 0)
    query_sum = Collect(pc, sems, gq, s_gq, qkv_out, True)
    kv_sum = Collect(pc, sems, gkv, s_gkv, kv_out, True)
    keys.turn()
    query_sum.send()
    keys.finish()
    pre = dkv_own[...]
    dqkv[:, wide : wide + 128] = jnp.where(halves(), turn(pre, cosine[...], -sine[...]), pre).astype(BF)

    def put(cols, value):
        for s in range(part.shape[1]):
            part[0, s, :, cols] = value[s * rows : (s + 1) * rows].astype(BF)

    tiled_nt(dqkv[...], wqkv, put)

    def ending():
        yield from plane_reduce(near, sems, part, s_near, input_grad)
        gain_acc[...] = jnp.zeros_like(gain_acc)

        def back(r):
            v = tok[r, :].astype(F32)
            input_grad[r, :] = norm_back(r, v, input_grad[r, :], gains[0:1, :], middle_grad[r, :], gain_acc)

        each_rows(rows, back)
        own = jnp.sum(gain_acc[...], axis=0, keepdims=True)
        row = lax.broadcasted_iota(jnp.int32, (8, 128), 0)
        for j in range(by_group.shape[0]):
            cols = slice(j * 128, (j + 1) * 128)
            by_group[j] = jnp.where(row == 0, jnp.broadcast_to(own[:, cols], (8, 128)), gain_two[:, cols])
        yield from sum_gains(pc, sems, by_group, stage, mid, second, gain_out)

    end = ending()
    go(end, 1)

    def key_grads(j, carry):
        at = pl.ds(pl.multiple_of(j * 256, 256), 256)
        left = jnp.concatenate([normed[0, s, :, at] for s in range(normed.shape[1])], axis=0)
        gkv[at, :] = dot_tn(left, dqkv[:, wide : wide + 128]).astype(BF)
        return carry

    lax.fori_loop(0, width // 256, key_grads, 0)
    kv_sum.send()
    query_sum.turn(0, 1)
    go(end, 5)
    query_sum.turn(2, 3)
    kv_sum.turn()
    run(end)
    run(laying)
    query_sum.finish()
    kv_sum.finish()


def shards(
    tokens,
    segment_ids,
    key_mask,
    attn_gain,
    w_query,
    w_key,
    w_value,
    w_out,
    mlp_gain,
    w_gate,
    w_up,
    w_down,
    cotangent,
):
    n_dp, n_t = lax.axis_size("dp"), lax.axis_size("tensor")
    chain = 4
    groups = n_dp // chain
    rows, width = tokens.shape
    local = rows * n_t
    total = local * n_dp
    dim = w_key.shape[1]
    heads = w_query.shape[1] // dim
    wrows = w_query.shape[0]
    units = w_gate.shape[1] // chain
    qkv = w_query.shape[1] + 2 * dim
    me = lax.axis_index("dp")
    share = attn_gain.shape[0]
    tile = 128 // share

    first_row = me * local
    own_gain = jnp.concatenate(
        [
            jnp.tile(attn_gain, tile)[None],
            jnp.tile(mlp_gain, tile)[None],
            jnp.zeros((6, 128), F32),
        ],
        axis=0,
    )
    wqkv = jnp.concatenate([w_query, w_key, w_value], axis=1)
    wout = w_out.T

    held = (units + 127) // 128 * 128

    def by_chain(w):
        w = jnp.pad(w.reshape(wrows, chain, units), ((0, 0), (0, 0), (0, held - units)))
        return w.transpose(1, 0, 2)

    plane = chain * n_t * rows
    nbytes = 60 << 20
    positions = first_row + jnp.arange(local, dtype=jnp.int32)
    lane = jnp.arange(128, dtype=jnp.int32)
    frequency = THETA ** (-(lane % (dim // 2)).astype(F32) / (dim // 2))
    turned = positions.astype(F32)[:, None] * frequency[None, :]
    cosine = jnp.cos(turned)
    sine = jnp.sin(turned) * jnp.where(lane % dim < dim // 2, -1.0, 1.0)
    own_segments = lax.dynamic_slice(segment_ids, (first_row,), (local,))
    wide = heads * dim
    saved = [
        ((1, n_t, rows, width), BF),
        ((width, qkv), BF),
        ((width, wide), BF),
        ((local, wide), BF),
        ((wide, local), BF),
        ((total, 128), BF),
        ((64, total), BF),
        ((total, local), BF),
        ((wide, local), F32),
        ((local, wide), BF),
    ]
    (gains, wgu, wdn, cot, lse, middle, two, *kept) = call(
        functools.partial(forward_kernel, chain),
        "forward",
        0,
        [VM, VM] + [ANY] * 6 + [VM] * 4,
        [
            ((8, width), F32, VM),
            ((width, 2 * held), BF, ANY),
            ((width, held), BF, ANY),
            ((chain, n_t, rows, width), BF, ANY),
            ((heads, local), F32, VM),
            ((rows, width), F32, VM),
            ((chain, n_t, rows, width), BF, ANY),
        ]
        + [(shape, kind, ANY) for shape, kind in saved],
        [pltpu.VMEM(shape, kind) for shape, kind in saved]
        + [
            pltpu.VMEM((n_dp, n_t, 8, 128), F32),
            pltpu.VMEM((rows, width), BF),
            pltpu.VMEM((local, 2 * dim), BF),
            pltpu.VMEM((80, total), BF),
            pltpu.VMEM((1, n_t, rows, width), BF),
            pltpu.VMEM((rows, width), F32),
            pltpu.VMEM((rows, width), BF),
            pltpu.SemaphoreType.DMA((10,)),
        ]
        + plane_scratch(1, rows, width),
        (
            tokens,
            own_gain,
            wqkv,
            wout,
            by_chain(w_gate),
            by_chain(w_up),
            by_chain(w_down.T),
            cotangent,
            cosine,
            sine,
            own_segments[:, None] * 2 + 1,
            (segment_ids * 2 + key_mask)[None],
        ),
        nbytes,
    )
    (opart, middle_grad, branch, gain_two, ggu, gdn) = call(
        functools.partial(feed_kernel, chain),
        "feed",
        1,
        [ANY] * 4 + [VM] * 3,
        [
            ((chain, n_t, rows, width), BF, ANY),
            ((rows, width), F32, VM),
            ((1, n_t, rows, width), BF, ANY),
            ((8, width), F32, VM),
            ((chain, wrows, 2 * held), BF, ANY),
            ((chain, wrows, held), BF, ANY),
        ],
        [
            pltpu.VMEM((plane, width), BF),
            pltpu.VMEM((plane, width), BF),
            pltpu.VMEM((width, 2 * held), BF),
            pltpu.VMEM((width, held), BF),
            pltpu.VMEM((chain, n_t, rows, width), BF),
            pltpu.VMEM((plane, 2 * held), F32),
            pltpu.VMEM((plane, held), F32),
            pltpu.VMEM((plane, 2 * held), BF),
            pltpu.VMEM((plane, held), BF),
            pltpu.VMEM((chain, n_t, rows, width), BF),
            pltpu.VMEM((width, 2 * held), BF),
            pltpu.VMEM((width, held), BF),
        ]
        + plane_scratch(chain, rows, width)
        + collect_scratch(chain, groups, wrows, 2 * held)
        + collect_scratch(chain, groups, wrows, held)
        + [
            pltpu.VMEM((rows, width), BF),
            pltpu.VMEM((16, width), F32),
            pltpu.SemaphoreType.DMA((4,)),
        ],
        (two.reshape(plane, width), cot.reshape(plane, width), wgu, wdn, middle, cotangent, gains),
        nbytes,
    )

    def shard_of(g):
        return jnp.concatenate([g[z, :, :units].astype(F32) for z in range(chain)], axis=1)

    grad_gate, grad_up, grad_down = shard_of(ggu), shard_of(ggu[:, :, held:]), shard_of(gdn).T

    count = max(1, n_t * share // 128)
    layer_out, input_grad, gq, gkv, gwout, gain_sum = call(
        functools.partial(backward_kernel, chain),
        "backward",
        2,
        [ANY] * 12 + [VM] * 8,
        [
            ((rows, width), BF, VM),
            ((rows, width), F32, VM),
            ((wrows, wide), F32, VM),
            ((wrows, 2 * dim), F32, VM),
            ((wrows, wide), F32, VM),
            ((8, 128), F32, VM),
        ],
        [pltpu.VMEM(shape, kind) for shape, kind in saved]
        + [
            pltpu.VMEM((local, width), BF),
            pltpu.VMEM((2, chain, rows, width), BF),
            pltpu.SemaphoreType.DMA((13,)),
            pltpu.VMEM((local, wide), BF),
            pltpu.VMEM((total, 128), F32),
            pltpu.VMEM((total, 128), BF),
            pltpu.VMEM((local, 128), F32),
            pltpu.VMEM((local, qkv), BF),
            pltpu.VMEM((width, wide), BF),
            pltpu.VMEM((width, 128), BF),
            pltpu.VMEM((1, n_t, rows, width), BF),
            pltpu.VMEM((rows, width), F32),
            pltpu.VMEM((16, width), F32),
        ]
        + plane_scratch(chain, rows, width)
        + plane_scratch(1, rows, width)
        + dp_scratch(chain, groups, wrows, wide)
        + dp_scratch(chain, groups, wrows, wide)
        + dp_scratch(chain, groups, wrows, 128)
        + dp_scratch(chain, groups, local, 128)
        + [
            pltpu.VMEM((width // 128, 8, 128), F32),
            pltpu.VMEM((n_dp, count, 8, 128), F32),
            pltpu.VMEM((count, 8, 128), F32),
            pltpu.VMEM((n_t, 8, 128), F32),
        ],
        (
            *kept,
            branch.reshape(local, width),
            opart,
            lse,
            tokens,
            middle_grad,
            gains,
            gain_two,
            middle,
            cosine,
            sine,
        ),
        nbytes,
    )
    lane = (me * n_t + lax.axis_index("tensor")) * share % 128
    gain_grads = lax.dynamic_slice(gain_sum, (0, lane), (2, share))
    return (
        layer_out,
        input_grad,
        gain_grads[0],
        gq,
        gkv[:, :dim],
        gkv[:, dim:],
        gwout.T,
        gain_grads[1],
        grad_gate,
        grad_up,
        grad_down,
    )


def solution(mesh):
    in_specs = (
        P(("dp", "tensor"), None),
        P(),
        P(),
        P(("dp", "tensor")),
        P("dp", "tensor"),
        P("dp", "tensor"),
        P("dp", "tensor"),
        P("tensor", "dp"),
        P(("dp", "tensor")),
        P("dp", "tensor"),
        P("dp", "tensor"),
        P("tensor", "dp"),
        P(("dp", "tensor"), None),
    )
    out_specs = (
        P(("dp", "tensor"), None),
        P(("dp", "tensor"), None),
        P(("dp", "tensor")),
        P("dp", "tensor"),
        P("dp", "tensor"),
        P("dp", "tensor"),
        P("tensor", "dp"),
        P(("dp", "tensor")),
        P("dp", "tensor"),
        P("dp", "tensor"),
        P("tensor", "dp"),
    )
    return jax.shard_map(shards, mesh=mesh, in_specs=in_specs, out_specs=out_specs, check_vma=False)
```

```python
import functools

import jax
import jax.numpy as jnp
from jax import lax
from jax.experimental import pallas as pl
from jax.experimental.pallas import tpu as pltpu
from jax.sharding import PartitionSpec as P

EPS = 1e-05
NEG = -1e30
THETA = 10000.0
BF = jnp.bfloat16
F32 = jnp.float32
MESH = pl.DeviceIdType.MESH
ANY = pl.BlockSpec(memory_space=pl.ANY)
VM = pl.BlockSpec(memory_space=pltpu.VMEM)


def sem_count():
    return 200 + 18 * lax.axis_size("dp")


class Sems:
    def __init__(self, send, recv):
        self.send, self.recv, self.used = send, recv, 0

    def take(self, count):
        base = self.used
        self.used += count
        assert self.used <= sem_count()
        return base


class Place:
    def __init__(self, chain):
        self.n_dp = lax.axis_size("dp")
        self.n_t = lax.axis_size("tensor")
        self.chain = chain
        self.groups = self.n_dp // chain
        self.d = lax.axis_index("dp")
        self.s = lax.axis_index("tensor")
        self.z = self.d // self.groups
        self.t = self.d % self.groups
        self.y = self.s // 2
        self.c = self.s % 2
        self.sy = (1 - self.y) * 2 + self.c
        self.sc = self.y * 2 + 1 - self.c
        self.so = (1 - self.y) * 2 + 1 - self.c
        self.above = self.at(z=jnp.minimum(self.z + 1, chain - 1))
        self.below = self.at(z=jnp.maximum(self.z - 1, 0))

    def at(self, z=None, t=None, s=None):
        z = self.z if z is None else z
        t = self.t if t is None else t
        s = self.s if s is None else s
        return {"dp": z * self.groups + t, "tensor": s}


def when(pred, act):
    if pred is None:
        act()
    else:
        pl.when(pred)(act)


class Copies:
    def __init__(self, sems):
        self.sems = sems
        self.sent = []

    def go(self, i, src, dst, where, pred=None):
        copy = pltpu.make_async_remote_copy(
            src_ref=src,
            dst_ref=dst,
            send_sem=self.sems.send.at[i],
            recv_sem=self.sems.recv.at[i],
            device_id=where,
            device_id_type=MESH,
        )
        when(pred, copy.start)
        self.sent.append((copy, pred))

    def keep(self, i, src, dst):
        copy = pltpu.make_async_copy(src, dst, self.sems.send.at[i])
        copy.start()
        return copy

    def arrive(self, i, dst, where, pred=None):
        copy = pltpu.make_async_remote_copy(
            src_ref=dst,
            dst_ref=dst,
            send_sem=self.sems.send.at[i],
            recv_sem=self.sems.recv.at[i],
            device_id=where,
            device_id_type=MESH,
        )
        when(pred, copy.wait_recv)

    def describe(self, i, src):
        return pltpu.make_async_remote_copy(
            src_ref=src,
            dst_ref=src,
            send_sem=self.sems.send.at[i],
            recv_sem=self.sems.recv.at[i],
            device_id={"dp": lax.axis_index("dp"), "tensor": lax.axis_index("tensor")},
            device_id_type=MESH,
        )

    def finish(self):
        for copy, pred in self.sent:
            when(pred, copy.wait_send)


def greet(pc):
    barrier = pltpu.get_barrier_semaphore()
    for k in range(1, pc.n_dp):
        pl.semaphore_signal(
            barrier, inc=1, device_id={"dp": (pc.d + k) % pc.n_dp, "tensor": pc.s}, device_id_type=MESH
        )
    for k in range(1, pc.n_t):
        pl.semaphore_signal(
            barrier, inc=1, device_id={"dp": pc.d, "tensor": (pc.s + k) % pc.n_t}, device_id_type=MESH
        )
    pl.semaphore_wait(barrier, pc.n_dp + pc.n_t - 2)


def run(*tasks):
    live = list(tasks)
    while live:
        live = [task for task in live if next(task, "end") != "end"]


def go(task, steps):
    for _ in range(steps):
        next(task, None)


class Points:
    def __init__(self, *acts):
        self.acts = list(acts)

    def __call__(self):
        if self.acts:
            for act in self.acts.pop(0):
                act()

    def drain(self):
        while self.acts:
            self()


def chain_steps(pc):
    chain, z = pc.chain, pc.z
    for k in range(chain - 1):
        for side in (0, 1):
            if side == 0:
                got = z - 1 - k >= 0
                yield k, side, jnp.maximum(z - 1 - k, 0), got, pc.above, jnp.logical_and(got, z + 1 < chain)
            else:
                got = z + 1 + k <= chain - 1
                yield k, side, jnp.minimum(z + 1 + k, chain - 1), got, pc.below, jnp.logical_and(got, z > 0)


def plane_gather(pc, sems, own, out, parts=1):
    chain, z, s = pc.chain, pc.z, pc.s
    width = own.shape[1] // parts
    cp = Copies(sems)
    base = sems.take(1 + 8 * chain * parts)

    def sem(kind, i, p):
        return base + 1 + (kind * chain + i) * parts + p

    def view(b, col, p):
        return out.at[b, col, :, pl.ds(p * width, width)]

    keep = cp.keep(base, own, out.at[z, s])
    for p in range(parts):
        src = own.at[:, pl.ds(p * width, width)]
        cp.go(sem(2, 0, p), src, view(z, s, p), pc.at(s=pc.sy))
        cp.go(sem(4, 0, p), src, view(z, s, p), pc.at(s=pc.sc))
    yield "own"
    for p in range(parts):
        src = own.at[:, pl.ds(p * width, width)]
        if chain > 1:
            cp.go(sem(0, 0, p), src, view(z, s, p), pc.above, z + 1 < chain)
            cp.go(sem(1, 0, p), src, view(z, s, p), pc.below, z > 0)
    yield "start"
    crossing = [(z, None, 0, p) for p in range(parts)]
    landed = []

    def cross(count):
        for _ in range(min(count, len(crossing))):
            b, got, i, p = crossing.pop(0)
            cp.arrive(sem(2, i, p), view(b, pc.sy, p), pc.at(), got)
            cp.go(sem(6, i, p), view(b, pc.sy, p), view(b, pc.sy, p), pc.at(s=pc.sc), got)
            landed.append((b, got, i, p))

    steps = list(chain_steps(pc))
    for k in range(chain - 1):
        for p in range(parts):
            for step, side, b, got, onward, more in steps:
                if step != k:
                    continue
                i = 1 + k if side == 0 else chain + k
                cp.arrive(sem(side, k, p), view(b, s, p), pc.at(), got)
                if k < chain - 2:
                    cp.go(sem(side, k + 1, p), view(b, s, p), view(b, s, p), onward, more)
                cp.go(sem(2, i, p), view(b, s, p), view(b, s, p), pc.at(s=pc.sy), got)
                cp.go(sem(4, i, p), view(b, s, p), view(b, s, p), pc.at(s=pc.sc), got)
                crossing.append((b, got, i, p))
            cross(1 if k == 0 else 2)
            yield "more"
    yield "tail"
    while crossing:
        cross(2)
        yield "more"
    for b, got, i, p in landed:
        cp.arrive(sem(4, i, p), view(b, pc.sc, p), pc.at(), got)
        cp.arrive(sem(6, i, p), view(b, pc.so, p), pc.at(), got)
    keep.wait()
    cp.finish()
    yield


def far_first(chain, z, j):
    if isinstance(j, int) and j == chain - 1:
        return z
    up = jnp.where(j < chain - 1 - z, chain - 1 - j, j - (chain - 1 - z))
    down = jnp.where(j < z, j, chain - 1 - (j - z))
    return jnp.where(j == chain - 1, z, jnp.where(2 * z < chain, up, down))


def each_rows(count, fn, rows=16):
    def body(i, carry):
        fn(pl.ds(pl.multiple_of(i * rows, rows), rows))
        return carry

    lax.fori_loop(0, count // rows, body, 0)


def chain_reduce(pc, cp, right, left, b, last, value, zsend, came, store, rows, cols):
    chain, z = pc.chain, pc.z
    if not last:
        fromleft = jnp.logical_and(b > z, z > 0)
        fromright = jnp.logical_and(b < z, z < chain - 1)
        cp.arrive(right, came.at[b, :, cols], pc.at(), fromleft)
        cp.arrive(left, came.at[b, :, cols], pc.at(), fromright)
        some = jnp.logical_or(fromleft, fromright)

        @pl.when(some)
        def _():
            def add(r):
                zsend[b, r, cols] = (value(r) + came[b, r, cols].astype(F32)).astype(BF)

            each_rows(rows, add)

        @pl.when(jnp.logical_not(some))
        def _():
            def add(r):
                zsend[b, r, cols] = value(r).astype(BF)

            each_rows(rows, add)

        cp.go(right, zsend.at[b, :, cols], came.at[b, :, cols], pc.above, b > z)
        slot = jnp.where(b == z - 1, chain, b)
        cp.go(left, zsend.at[b, :, cols], came.at[slot, :, cols], pc.below, b < z)
        return

    def first(r):
        store(r, value(r), False)

    each_rows(rows, first)
    if chain > 1:

        @pl.when(z > 0)
        def _():
            cp.arrive(right, came.at[b, :, cols], pc.at())

            def add(r):
                store(r, came[b, r, cols].astype(F32), True)

            each_rows(rows, add)

        @pl.when(z < chain - 1)
        def _():
            cp.arrive(left, came.at[chain, :, cols], pc.at())

            def add(r):
                store(r, came[chain, r, cols].astype(F32), True)

            each_rows(rows, add)


def plane_scratch(chain, rows, width):
    return [
        pltpu.VMEM((chain, 2, rows, width), BF),
        pltpu.VMEM((chain, rows, width), BF),
        pltpu.VMEM((chain, rows, width), BF),
        pltpu.VMEM((chain if chain > 1 else 1, rows, width) if chain > 1 else (1, 16, 128), BF),
        pltpu.VMEM((chain + 1, rows, width) if chain > 1 else (1, 16, 128), BF),
    ]


class PlaneReduce:
    def __init__(self, pc, sems, part, scratch, out, held=None):
        self.pc, self.part, self.out, self.held = pc, part, out, held
        self.crecv, self.csum, self.yrecv, self.zsend, self.came = scratch
        self.cp = Copies(sems)
        self.base = sems.take(5 * pc.chain)
        self.rows, self.width = out.shape

    def sem(self, kind, i):
        return self.base + kind * self.pc.chain + i

    def block(self, j):
        return far_first(self.pc.chain, self.pc.z, j)

    def pass_core(self, over, j, b, cp=None):
        pc = self.pc
        (cp or self.cp).go(
            self.sem(over, j),
            self.part.at[b, pc.so if over else pc.sc],
            self.crecv.at[b, over],
            pc.at(s=pc.sc),
        )

    def cross(self, j, b, cp=None):
        pc, crecv, csum = self.pc, self.crecv, self.csum
        cp = cp or self.cp
        cp.arrive(self.sem(1, j), crecv.at[b, 1], pc.at())

        def add(r):
            csum[b, r, :] = (self.own(0, b, r).astype(F32) + crecv[b, 1, r, :].astype(F32)).astype(BF)

        each_rows(self.rows, add)
        cp.go(self.sem(2, j), csum.at[b], self.yrecv.at[b], pc.at(s=pc.sy))

    def own(self, here, b, r):
        if self.held is not None:
            return self.held[here, b, r, :]
        return self.part[b, self.pc.s if here else self.pc.sy, r, :]

    def steps(self):
        pc = self.pc
        chain, z = pc.chain, pc.z
        crecv, yrecv, out = self.crecv, self.yrecv, self.out
        cp = self.cp
        todo = [(j, self.block(j)) for j in range(chain)]
        for j, b in todo:
            self.pass_core(1, j, b)
        yield
        ahead = list(todo)
        for _ in range(min(2, chain)):
            self.cross(*ahead.pop(0))
            yield
        for j, b in todo:
            self.pass_core(0, j, b)
        yield
        for j, b in todo:
            cp.arrive(self.sem(0, j), crecv.at[b, 0], pc.at())
            cp.arrive(self.sem(2, j), yrecv.at[b], pc.at())
            if ahead:
                self.cross(*ahead.pop(0))

            def value(r):
                return (
                    self.own(1, b, r).astype(F32)
                    + crecv[b, 0, r, :].astype(F32)
                    + yrecv[b, r, :].astype(F32)
                )

            def store(r, term, more):
                out[r, :] = out[r, :] + term if more else term

            chain_reduce(
                pc,
                cp,
                self.sem(3, b),
                self.sem(4, b),
                b,
                j == chain - 1,
                value,
                self.zsend,
                self.came,
                store,
                self.rows,
                pl.ds(0, self.width),
            )
            yield
        cp.finish()
        yield


def plane_reduce(pc, sems, part, scratch, out):
    return PlaneReduce(pc, sems, part, scratch, out).steps()


def dp_gather(pc, sems, own, out, parts=1):
    chain, groups, z, t = pc.chain, pc.groups, pc.z, pc.t
    cp = Copies(sems)
    base = sems.take(1 + (2 * chain + 2 * chain * groups) * parts)
    rows = own.shape[0] // parts

    def cut(ref, p):
        return ref.at[pl.ds(p * rows, rows)]

    def along(side, k, p):
        return base + 1 + (side * chain + k) * parts + p

    def across(i, g, p):
        return base + 1 + (2 * chain + i * groups + g) * parts + p

    keep = cp.keep(base, own, out(pc.d))
    for p in range(parts):
        for g in range(1, groups):
            cp.go(across(0, g, p), cut(own, p), cut(out(pc.d), p), pc.at(t=(t + g) % groups))
    yield "own"
    if chain > 1:
        for p in range(parts):
            cp.go(along(0, 0, p), cut(own, p), cut(out(pc.d), p), pc.above, z + 1 < chain)
            cp.go(along(1, 0, p), cut(own, p), cut(out(pc.d), p), pc.below, z > 0)
    yield "start"
    landed = [(z, None, 0)]
    for k in range(chain - 1):
        for p in range(parts):
            for step, side, b, got, onward, more in chain_steps(pc):
                if step != k:
                    continue
                i = 1 + k if side == 0 else chain + k
                block = cut(out(b * groups + t), p)
                cp.arrive(along(side, k, p), block, pc.at(), got)
                if k < chain - 2:
                    cp.go(along(side, k + 1, p), block, block, onward, more)
                for g in range(1, groups):
                    cp.go(across(i, g, p), block, block, pc.at(t=(t + g) % groups), got)
                if p == 0:
                    landed.append((b, got, i))
            yield "more"
    yield "tail"
    for b, got, i in landed:
        for p in range(parts):
            for g in range(1, groups):
                cp.arrive(across(i, g, p), cut(out(b * groups + (t - g + groups) % groups), p), pc.at(), got)
    keep.wait()
    cp.finish()
    yield "end"


def plane_direct(pc, sems, own, out):
    chain, z, s = pc.chain, pc.z, pc.s
    cp = Copies(sems)
    base = sems.take(1 + 4 * chain)

    def sem(kind, k):
        return base + 1 + kind * chain + k

    keep = cp.keep(base, own, out.at[z, s])
    cp.go(sem(1, 0), own, out.at[z, s], pc.at(s=pc.sy))
    cp.go(sem(2, 0), own, out.at[z, s], pc.at(s=pc.sc))
    yield "own"
    for k in range(1, chain):
        to = (z + k) % chain
        cp.go(sem(0, k), own, out.at[z, s], pc.at(z=to))
    yield "start"
    for k in range(1, chain):
        b = (z - k + chain) % chain
        cp.arrive(sem(0, k), out.at[b, s], pc.at())
        cp.go(sem(1, k), out.at[b, s], out.at[b, s], pc.at(s=pc.sy))
        cp.go(sem(2, k), out.at[b, s], out.at[b, s], pc.at(s=pc.sc))
    yield "turned"
    for k in range(chain):
        b = (z - k + chain) % chain
        cp.arrive(sem(1, k), out.at[b, pc.sy], pc.at())
        cp.go(sem(3, k), out.at[b, pc.sy], out.at[b, pc.sy], pc.at(s=pc.sc))
    yield "crossed"
    for k in range(chain):
        b = (z - k + chain) % chain
        cp.arrive(sem(2, k), out.at[b, pc.sc], pc.at())
        cp.arrive(sem(3, k), out.at[b, pc.so], pc.at())
    keep.wait()
    cp.finish()
    yield "end"


def spread(pc, sems, blocks, out):
    chain, groups, z, t = pc.chain, pc.groups, pc.z, pc.t
    cp = Copies(sems)
    base = sems.take(1 + chain + chain * groups)
    along, across = base + 1, base + 1 + chain
    keep = cp.keep(base, blocks(z), out(pc.d))
    for g in range(1, groups):
        cp.go(across + g, blocks(z), out(pc.d), pc.at(t=(t + g) % groups))
    yield "own"
    for k in range(1, chain):
        to = (z + k) % chain
        cp.go(along + k, blocks(to), out(pc.d), pc.at(z=to))
    yield "start"
    for k in range(1, chain):
        block = out((z - k + chain) % chain * groups + t)
        cp.arrive(along + k, block, pc.at())
        for g in range(1, groups):
            cp.go(across + k * groups + g, block, block, pc.at(t=(t + g) % groups))
        yield "more"
    yield "tail"
    for k in range(chain):
        for g in range(1, groups):
            block = out((z - k + chain) % chain * groups + (t - g + groups) % groups)
            cp.arrive(across + k * groups + g, block, pc.at())
    keep.wait()
    cp.finish()
    yield "end"


class Side:
    def __init__(self, pc, sems, part, recv):
        self.pc, self.part, self.recv = pc, part, recv
        self.rows, self.width = recv.shape[2], recv.shape[3]
        self.base = sems.take(pc.chain * pc.groups)

    def start(self, i):
        return pl.multiple_of(i * self.rows, self.rows)

    def send(self, cp, j, b):
        pc = self.pc
        for g in range(1, pc.groups):
            to = (pc.t + g) % pc.groups
            cp.go(
                self.base + j * pc.groups + g,
                self.part.at[pl.ds(self.start(b * pc.groups + to), self.rows)],
                self.recv.at[g - 1, b],
                pc.at(t=to),
            )

    def arrive(self, cp, j, b):
        for g in range(1, self.pc.groups):
            cp.arrive(self.base + j * self.pc.groups + g, self.recv.at[g - 1, b], self.pc.at())

    def value(self, b, r):
        at = self.start(b * self.pc.groups + self.pc.t)
        total = self.part[pl.ds(pl.multiple_of(at + r.start, 16), r.size), :].astype(F32)
        for g in range(1, self.pc.groups):
            total = total + self.recv[g - 1, b, r, :].astype(F32)
        return total


def dp_scratch(chain, groups, rows, width):
    return [
        pltpu.VMEM((max(groups - 1, 1), chain, rows, width), BF),
        pltpu.VMEM((chain, rows, width), BF),
        pltpu.VMEM((chain, rows, width), BF),
    ]


class Moves:
    def __init__(self, sem):
        self.sem, self.count = sem, 0

    def start(self, src, dst):
        copy = pltpu.make_async_copy(src, dst, self.sem.at[self.count])
        self.count += 1
        copy.start()
        return copy


class Collect:
    def __init__(self, pc, sems, part, scratch, out, summed):
        self.pc, self.out, self.summed = pc, out, summed
        self.side = Side(pc, sems, part, scratch[0])
        self.sums = scratch[1]
        self.came = scratch[2] if summed else out
        self.cp = Copies(sems)
        self.along = sems.take(pc.chain)
        self.kept = None

    def block(self, k):
        return (self.pc.z + self.pc.chain - 1 - k) % self.pc.chain

    def send(self, *which):
        for k in which or range(self.pc.chain):
            self.side.send(self.cp, k, self.block(k))

    def turn(self, *which):
        pc, chain, z, side = self.pc, self.pc.chain, self.pc.z, self.side
        for k in which or range(chain):
            b = self.block(k)
            side.arrive(self.cp, k, b)
            if k == chain - 1 and self.summed:

                def first(r):
                    self.out[r, :] = side.value(b, r)

                each_rows(side.rows, first)
                continue

            def add(r):
                self.sums[b, r, :] = side.value(b, r).astype(BF)

            each_rows(side.rows, add)
            if k < chain - 1:
                self.cp.go(self.along + k, self.sums.at[b], self.came.at[z], pc.at(z=b))
            else:
                self.kept = self.cp.keep(self.along + k, self.sums.at[b], self.out.at[z])

    def finish(self):
        pc, chain, z, side = self.pc, self.pc.chain, self.pc.z, self.side
        for k in range(chain - 1):
            b = (z - (chain - 1 - k) + chain) % chain
            self.cp.arrive(self.along + k, self.came.at[b], pc.at())
            if self.summed:

                def add(r):
                    self.out[r, :] = self.out[r, :] + self.came[b, r, :].astype(F32)

                each_rows(side.rows, add)
        if self.kept is not None:
            self.kept.wait()
        self.cp.finish()


def collect_scratch(chain, groups, rows, width):
    return dp_scratch(chain, groups, rows, width)[:2]


def share_gains(pc, sems, own, table):
    cp = Copies(sems)
    base = sems.take(pc.n_dp + pc.n_t)
    table[pc.d, pc.s] = own[...]
    for k in range(1, pc.n_t):
        cp.go(base + k, table.at[pc.d, pc.s], table.at[pc.d, pc.s], {"dp": pc.d, "tensor": (pc.s + k) % pc.n_t})
    yield
    for k in range(1, pc.n_t):
        cp.arrive(base + k, table.at[pc.d, (pc.s - k + pc.n_t) % pc.n_t], pc.at())
    second = base + pc.n_t
    for k in range(1, pc.n_dp):
        cp.go(second + k, table.at[pc.d], table.at[pc.d], {"dp": (pc.d + k) % pc.n_dp, "tensor": pc.s})
    yield
    for k in range(1, pc.n_dp):
        cp.arrive(second + k, table.at[(pc.d - k + pc.n_dp) % pc.n_dp], pc.at())
    cp.finish()
    yield


def lay_gains(pc, table, gains):
    lanes = 128
    devices = pc.n_dp * pc.n_t
    each = gains.shape[1] // devices
    per = lanes // each
    lane = lax.broadcasted_iota(jnp.int32, (8, lanes), 1)
    for j in range(gains.shape[1] // lanes):
        row = table[(j * per) // pc.n_t, (j * per) % pc.n_t]
        for k in range(1, per):
            o = j * per + k
            row = jnp.where(lane >= k * each, table[o // pc.n_t, o % pc.n_t], row)
        gains[:, j * lanes : (j + 1) * lanes] = row


def sum_gains(pc, sems, groups_of, stage, mid, second, out):
    count = stage.shape[1]
    n_dp, n_t = pc.n_dp, pc.n_t
    cp = Copies(sems)
    base = sems.take(n_dp + n_t)

    def start_of(d):
        return d * groups_of.shape[0] // n_dp

    for k in range(1, n_dp):
        to = (pc.d + k) % n_dp
        cp.go(
            base + k,
            groups_of.at[pl.ds(start_of(to), count)],
            stage.at[pc.d],
            {"dp": to, "tensor": pc.s},
        )
    stage[pc.d] = groups_of[pl.ds(start_of(pc.d), count)]
    yield
    for k in range(1, n_dp):
        cp.arrive(base + k, stage.at[(pc.d - k + n_dp) % n_dp], pc.at())
    total = stage[0]
    for k in range(1, n_dp):
        total = total + stage[k]
    mid[...] = total
    yield
    last = base + n_dp
    for k in range(1, n_t):
        to = (pc.s + k) % n_t
        cp.go(last + k, mid.at[to * count // n_t], second.at[pc.s], {"dp": pc.d, "tensor": to})
    second[pc.s] = mid[pc.s * count // n_t]
    yield
    for k in range(1, n_t):
        cp.arrive(last + k, second.at[(pc.s - k + n_t) % n_t], pc.at())
    total = second[0]
    for k in range(1, n_t):
        total = total + second[k]
    out[...] = total
    cp.finish()
    yield


def call(kernel, name, number, ins, outs, scratch, operands, cost):
    sems = [pltpu.SemaphoreType.DMA((sem_count(),))] * 2
    return pl.pallas_call(
        kernel,
        out_shape=[jax.ShapeDtypeStruct(shape, kind) for shape, kind, _ in outs],
        in_specs=ins,
        out_specs=[space for _, _, space in outs],
        scratch_shapes=list(scratch) + sems,
        name=name,
        cost_estimate=pl.CostEstimate(flops=0, bytes_accessed=cost, transcendentals=0),
        compiler_params=pltpu.CompilerParams(
            collective_id=number, has_side_effects=True, vmem_limit_bytes=63 << 20
        ),
    )(*operands)


def unit(v):
    return lax.rsqrt(jnp.mean(v * v, axis=-1, keepdims=True) + EPS)


def gcd_of(n, size):
    while n % size:
        size //= 2
    return size


def rows_of(ref, count):
    return lambda d: ref.at[pl.ds(pl.multiple_of(d * count, count), count)]


def halves():
    lane = lax.broadcasted_iota(jnp.int32, (1, 128), 1)
    return lane < 64


def turn(x, cosine, sine):
    lane = lax.broadcasted_iota(jnp.int32, x.shape, 1)
    swapped = jnp.where(lane % 64 < 32, pltpu.roll(x, 96, 1), pltpu.roll(x, 32, 1))
    return x * cosine + swapped * sine


def key_range(first, count, total, size):
    long_end = 5 * total // 8
    low = jnp.where(first >= long_end + total // 32 - 16, long_end, 0)
    return low // size, (first + count + size - 1) // size


def fill_bias(bias, first, low, high, size, qinfo, kinfo):
    qpos = first + lax.broadcasted_iota(jnp.int32, qinfo.shape, 0)

    def fill(j, carry):
        at = pl.multiple_of(j * size, size)
        cols = pl.ds(at, size)
        kpos = at + lax.broadcasted_iota(jnp.int32, (1, size), 1)
        allowed = (kpos == qpos) | ((kinfo[:, cols] == qinfo[...]) & (kpos < qpos))
        bias[cols, :] = jnp.where(allowed, 0.0, NEG).T.astype(BF)
        return carry

    lax.fori_loop(low, high, fill, 0)


def turn_values(kv, vt):
    size = gcd_of(kv.shape[0], 256)
    vt[64:80, :] = jnp.ones((16, kv.shape[0]), BF)

    def body(j, carry):
        r = pl.ds(pl.multiple_of(j * size, size), size)
        vt[0:64, r] = kv[r, :].astype(F32).T[64:128, :].astype(BF)
        return carry

    lax.fori_loop(0, kv.shape[0] // size, body, 0)


def turn_keys(kv, kt):
    size = gcd_of(kv.shape[0], 256)

    def body(j, carry):
        r = pl.ds(pl.multiple_of(j * size, size), size)
        kt[:, r] = kv[r, :].astype(F32).T[0:64, :].astype(BF)
        return carry

    lax.fori_loop(0, kv.shape[0] // size, body, 0)


def attend(pc, query_t, kv, vt, bias, mixed_t, mixed_low, lse, step):
    local, total = query_t.shape[1], kv.shape[0]
    size = gcd_of(total, 640)
    low, high = key_range(pc.d * local, local, total, size)

    def one(chunk, carry):
        first = pl.multiple_of(chunk * 128, 128)
        queries = tuple(query_t[pl.ds(pl.multiple_of(first + k * 64, 64), 64), :] for k in range(2))

        def body(j, carry):
            rows = pl.ds(pl.multiple_of(j * size, size), size)
            key, value, mask = kv[rows, 0:64], vt[:, rows], bias[rows, :].astype(F32)
            out = []
            for q, (top, acc) in zip(queries, carry):
                s = jnp.dot(key, q, preferred_element_type=F32) + mask
                new = jnp.maximum(top, jnp.max(s, axis=0, keepdims=True))
                p = jnp.exp(s - new).astype(BF)
                acc = acc * jnp.exp(top - new) + jnp.dot(value, p, preferred_element_type=F32)
                out.append((new, acc))
            return tuple(out)

        start = (jnp.full((1, local), NEG, F32), jnp.zeros((80, local), F32))
        done = lax.fori_loop(low, high, body, (start, start))
        pair = []
        for k, (top, acc) in enumerate(done):
            tot = acc[64:65, :]
            pair.append(acc[0:64, :] / tot)
            lse[pl.ds(2 * chunk + k, 1), :] = top + jnp.log(tot)
        both = jnp.concatenate(pair, axis=0)
        mixed_t[pl.ds(first, 128), :] = both
        mixed_low[:, pl.ds(first, 128)] = both.T.astype(BF)
        return carry

    chunks = query_t.shape[0] // 128
    for half in range(2):
        lax.fori_loop(half * chunks // 2, (half + 1) * chunks // 2, one, 0)
        step()


def tiled_nt(left, right, put, size=256):
    size = gcd_of(right.shape[0], size)

    def body(j, carry):
        cols = pl.ds(pl.multiple_of(j * size, size), size)
        put(
            cols,
            lax.dot_general(left, right[cols, :], (((1,), (1,)), ((), ())), preferred_element_type=F32),
        )
        return carry

    lax.fori_loop(0, right.shape[0] // size, body, 0)


def forward_kernel(chain, *refs):
    (tok, own_gain, wqkv, wout, wgate, wup, wdown, cot, cosine, sine, qinfo, kinfo) = refs[:12]
    (
        gains,
        wgu_all,
        wdown_all,
        cot_all,
        lse,
        middle,
        two_all,
    ) = refs[12:19]
    kept, rest = refs[19:29], refs[29:]
    (normed_all, wqkv_all, wout_all, query, query_t, kv_all, kt, bias, mixed_t, mixed_low) = rest[:10]
    table, normed, own_kv, vt, part, total, two, local_sem = rest[10:18]
    scratch, (send, recv) = rest[18:23], rest[23:]
    moves = Moves(local_sem)
    stores = []

    def keep(*names):
        for i in names:
            stores.append(moves.start(rest[i], kept[i]))

    sems = Sems(send, recv)
    pc, near = Place(chain), Place(1)
    rows, width = tok.shape
    wrows = wqkv.shape[0]
    local = query.shape[0]
    wide = query.shape[1]
    greet(pc)

    def head():
        yield from share_gains(pc, sems, own_gain, table)
        lay_gains(pc, table, gains)

        def norm(r):
            v = tok[r, :].astype(F32)
            normed[r, :] = (v * unit(v) * gains[0:1, :]).astype(BF)

        each_rows(rows, norm)
        yield from plane_gather(near, sems, normed, normed_all)

    first = dp_gather(pc, sems, wqkv, rows_of(wqkv_all, wrows), 2)
    outw = dp_gather(pc, sems, wout, rows_of(wout_all, wrows), 2)
    half = wgu_all.shape[1] // 2
    gatew = spread(pc, sems, lambda d: wgate.at[d], rows_of(wgu_all.at[:, pl.ds(0, half)], wrows))
    upw = spread(pc, sems, lambda d: wup.at[d], rows_of(wgu_all.at[:, pl.ds(half, half)], wrows))
    downw = spread(pc, sems, lambda d: wdown.at[d], rows_of(wdown_all, wrows))
    cots = plane_gather(pc, sems, cot, cot_all, 2)
    beside = head()
    go(first, 2)
    go(beside, 1)
    go(cots, 1)
    go(first, 2)
    go(beside, 1)
    go(first, 2)
    go(cots, 1)
    go(beside, 2)
    go(first, 3)
    go(outw, 2)
    run(beside)
    run(first)
    go(outw, 2)
    go(cots, 2)

    here = jnp.concatenate([normed_all[0, s] for s in range(normed_all.shape[1])], axis=0)
    size = 256
    for at in range(0, wide, size):
        pre = jnp.dot(here, wqkv_all[:, at : at + size], preferred_element_type=F32)
        for lanes in range(0, size, 128):
            turned = turn(pre[:, lanes : lanes + 128], cosine[...], sine[...])
            turned = turned * 0.125
            query[:, at + lanes : at + lanes + 128] = turned.astype(BF)
            query_t[at + lanes : at + lanes + 128, :] = turned.T.astype(BF)
    pre = jnp.dot(here, wqkv_all[:, wide : wide + 128], preferred_element_type=F32)
    own_kv[...] = jnp.where(halves(), turn(pre, cosine[...], sine[...]), pre).astype(BF)
    go(outw, 2)
    run(dp_gather(pc, sems, own_kv, rows_of(kv_all, local)))
    keep(0, 1, 3, 4, 5)
    go(gatew, 2)
    go(outw, 3)
    go(cots, 2)
    turn_values(kv_all, vt)
    size = gcd_of(kv_all.shape[0], 640)
    low, high = key_range(pc.d * local, local, kv_all.shape[0], size)
    fill_bias(bias, pc.d * local, low, high, size, qinfo, kinfo)
    go(upw, 2)
    stops = Points([lambda: go(cots, 2), lambda: go(downw, 2)], [lambda: run(outw)])
    attend(pc, query_t, kv_all, vt, bias, mixed_t, mixed_low, lse, stops)
    stops.drain()


    def put(cols, value):
        for s in range(part.shape[1]):
            part[0, s, :, cols] = value[s * rows : (s + 1) * rows].astype(BF)

    tiled_nt(mixed_low[...], wout_all, put)
    totals = plane_reduce(near, sems, part, scratch, total)
    go(totals, 1)
    keep(2, 7, 8, 9)
    go(gatew, 3)
    turn_keys(kv_all, kt)
    keep(6)
    run(totals)

    def norm(r):
        v = tok[r, :].astype(F32) + total[r, :]
        middle[r, :] = v
        two[r, :] = (v * unit(v) * gains[1:2, :]).astype(BF)

    each_rows(rows, norm)
    twos = plane_gather(pc, sems, two, two_all, 2)
    go(twos, 2)
    go(upw, 3)
    go(twos, 2)
    go(cots, 3)
    go(twos, 2)
    go(downw, 3)
    run(twos)
    run(cots, gatew, upw, downw)
    for store in stores:
        store.wait()


def dot_nt(a, b):
    return lax.dot_general(a, b, (((1,), (1,)), ((), ())), preferred_element_type=F32)


def dot_tn(a, b):
    return lax.dot_general(a, b, (((0,), (0,)), ((), ())), preferred_element_type=F32)


def grads_into(left, right, out, size=256):
    def body(j, carry):
        at = pl.ds(pl.multiple_of(j * size, size), size)
        out[at, :] = dot_tn(left[:, at], right[...]).astype(BF)
        return carry

    lax.fori_loop(0, out.shape[0] // size, body, 0)


def norm_back(r, v, grad, gain, extra, gain_acc):
    root = unit(v)
    xhat = v * root
    e = grad * gain
    gain_acc[...] += grad * xhat
    return extra + root * (e - xhat * jnp.mean(e * xhat, axis=-1, keepdims=True))


def tiled_in(left, right, out, size):
    def body(j, carry):
        at = pl.ds(pl.multiple_of(j * size, size), size)
        out[:, at] = jnp.dot(left[...], right[:, at], preferred_element_type=F32)
        return carry

    lax.fori_loop(0, out.shape[1] // size, body, 0)


def feed_kernel(chain, *refs):
    (two_all, cot_all, wgu_all, wdn_all, middle, cot, gains) = refs[:7]
    (opart_all, middle_grad, branch_all, gain_out, cgu, cdn) = refs[7:13]
    rest = refs[13:]
    two, cotan, wgu, wdn, opart, gu, h, both, hidden, npart, ggu, gdn = rest[:12]
    s_part = rest[12:17]
    s_gu, s_dn = rest[17:19], rest[19:21]
    branch, gain_acc, local_sem, send, recv = rest[21:]
    sems = Sems(send, recv)
    pc, near = Place(chain), Place(1)
    fetches = []
    for i, (src, dst) in enumerate(((wgu_all, wgu), (two_all, two), (wdn_all, wdn), (cot_all, cotan))):
        fetches.append(pltpu.make_async_copy(src, dst, local_sem.at[i]))
        fetches[-1].start()
    greet(pc)
    rows, width = middle.shape
    n_t = npart.shape[1]
    units = hidden.shape[1]
    reduce = PlaneReduce(pc, sems, npart, s_part, middle_grad)
    fetches[0].wait()
    fetches[1].wait()
    tiled_in(two, wgu, gu, 256)
    fetches[2].wait()
    fetches[3].wait()
    tiled_in(cotan, wdn, h, 128)

    def gates(r):
        for at in range(0, units, 128):
            left, right = pl.ds(at, 128), pl.ds(units + at, 128)
            g, u, k = gu[r, left], gu[r, right], h[r, left]
            sigma = 1.0 / (1.0 + jnp.exp(-g))
            silu = g * sigma
            hidden[r, left] = (silu * u).astype(BF)
            both[r, left] = (k * u * sigma * (1.0 + g * (1.0 - sigma))).astype(BF)
            both[r, right] = (k * silu).astype(BF)

    each_rows(two.shape[0], gates, 32)

    def tiled_out(left, right, out):
        def body(i, carry):
            cols = pl.ds(pl.multiple_of(i * 256, 256), 256)
            value = dot_nt(left[...], right[cols, :]).astype(BF)
            out[:, :, :, cols] = value.reshape(chain, n_t, rows, 256)
            return carry

        lax.fori_loop(0, width // 256, body, 0)

    tiled_out(both, wgu, npart)
    steps = reduce.steps()
    go(steps, 4)
    gus = Collect(pc, sems, ggu, s_gu, cgu, False)
    dns = Collect(pc, sems, gdn, s_dn, cdn, False)
    grads_into(two, both, ggu)
    gus.send(0, 1)
    go(steps, 1)
    grads_into(cotan, hidden, gdn)
    go(steps, 1)
    gus.turn(0, 1)
    gus.send(2, 3)
    go(steps, 1)
    dns.send()
    run(steps)
    gus.turn(2, 3)
    gain_acc[...] = jnp.zeros_like(gain_acc)

    def back(r):
        grad = norm_back(r, middle[r, :], middle_grad[r, :], gains[1:2, :], cot[r, :].astype(F32), gain_acc)
        middle_grad[r, :] = grad
        branch[r, :] = grad.astype(BF)

    each_rows(rows, back)
    spreading = plane_gather(near, sems, branch, branch_all)
    go(spreading, 2)
    tiled_out(hidden, wdn, opart)
    store = pltpu.make_async_copy(opart, opart_all, local_sem.at[0])
    store.start()
    run(spreading)
    gain_out[...] = jnp.broadcast_to(jnp.sum(gain_acc[...], axis=0, keepdims=True), gain_out.shape)
    dns.turn()
    gus.finish()
    dns.finish()
    store.wait()


def attend_back(pc, query, query_t, dmix, mixed_t, lse, kv, kt, bias, dsum, put, step):
    local, total = query.shape[0], kv.shape[0]
    size = gcd_of(total, 640)
    low, high = key_range(pc.d * local, local, total, size)
    even = jnp.where(halves(), 1.0, 0.0).astype(BF)
    odd = jnp.where(halves(), 0.0, 1.0).astype(BF)
    none = jnp.zeros((64, local), BF)
    for chunk in range(query.shape[1] // 128):
        first = chunk * 128
        lanes = slice(first, first + 128)
        q, dm = query[:, lanes], dmix[:, lanes]
        turned = dm.astype(F32).T
        product = turned * mixed_t[lanes, :]
        turned = turned.astype(BF)
        heads = []
        for k, pick in enumerate((even, odd)):
            at = slice(k * 64, k * 64 + 64)
            heads.append(
                (
                    query_t[first + k * 64 : first + k * 64 + 64, :],
                    jnp.concatenate([none, turned[at, :]], axis=0),
                    q * pick,
                    dm * pick,
                    lse[2 * chunk + k : 2 * chunk + k + 1, :],
                    jnp.sum(product[at, :], axis=0, keepdims=True),
                )
            )

        def body(j, carry):
            rows = pl.ds(pl.multiple_of(j * size, size), size)
            both, key, key_t, mask = kv[rows, :], kv[rows, 0:64], kt[:, rows], bias[rows, :].astype(F32)
            out = []
            dk = jnp.zeros((size, 128), F32)
            dv = jnp.zeros((size, 128), F32)
            for (qt, dmt, qh, dh, top, delta), acc in zip(heads, carry):
                p = jnp.exp(jnp.dot(key, qt, preferred_element_type=F32) + mask - top)
                dp = jnp.dot(both, dmt, preferred_element_type=F32)
                ds = (p * (dp - delta)).astype(BF)
                dk = dk + jnp.dot(ds, qh, preferred_element_type=F32)
                dv = dv + jnp.dot(p.astype(BF), dh, preferred_element_type=F32)
                out.append(acc + jnp.dot(key_t, ds, preferred_element_type=F32))
            dsum[rows, :] += jnp.where(halves(), dk + pltpu.roll(dk, 64, 1), dv + pltpu.roll(dv, 64, 1))
            return tuple(out)

        zero = jnp.zeros((64, local), F32)
        done = lax.fori_loop(low, high, body, (zero, zero))
        put(lanes, jnp.concatenate(done, axis=0).T)
        step()


def low_rows(full, low):
    size = gcd_of(full.shape[0], 256)

    def body(j, carry):
        r = pl.ds(pl.multiple_of(j * size, size), size)
        low[r, :] = full[r, :].astype(BF)
        return carry

    lax.fori_loop(0, full.shape[0] // size, body, 0)


def zero_rows(*refs):
    size = gcd_of(refs[0].shape[0], 256)

    def body(j, carry):
        r = pl.ds(pl.multiple_of(j * size, size), size)
        for ref in refs:
            ref[r, :] = jnp.zeros((size, ref.shape[1]), ref.dtype)
        return carry

    lax.fori_loop(0, refs[0].shape[0] // size, body, 0)


def backward_kernel(chain, *refs):
    kept, branch_all, opart = refs[:10], refs[10], refs[11]
    (lse, tok, middle_grad, gains, gain_two, middle, cosine, sine) = refs[12:20]
    (layer_out, input_grad, qkv_out, kv_out, wout_out, gain_out) = refs[20:26]
    rest = refs[26:]
    (normed, wqkv, wout, query, query_t, kv, kt, bias, mixed_t, mixed_low) = rest[:10]
    (branch_in, held, local_sem) = rest[10:13]
    (dmix, dsum, dkv, dkv_own, dqkv, gwo, gkv, part, osum, gain_acc) = rest[13:23]
    gq = gwo
    rest = rest[23:]
    s_out, s_near = rest[:5], rest[5:10]
    s_gwo, s_gq, s_gkv, s_keys = rest[10:13], rest[13:16], rest[16:19], rest[19:22]
    by_group, stage, mid, second, send, recv = rest[22:]
    sems = Sems(send, recv)
    pc, near = Place(chain), Place(1)
    rows, width = tok.shape
    local, wide = query.shape
    moves = Moves(local_sem)
    inner = (normed, wqkv, wout, query, query_t, kv, kt, bias, mixed_t, mixed_low)
    fetches = {}
    fetches[10] = moves.start(branch_all, branch_in)
    for i in (9, 2):
        fetches[i] = moves.start(kept[i], inner[i])
    halves_of = [
        moves.start(opart.at[:, col], held.at[i]) for i, col in enumerate((pc.sy, pc.s))
    ]
    for i in (7, 5, 6, 3, 4, 8, 0, 1):
        fetches[i] = moves.start(kept[i], inner[i])
    greet(pc)

    def finish():
        yield from PlaneReduce(pc, sems, opart, s_out, osum, held).steps()

        def add(r):
            layer_out[r, :] = (middle[r, :] + osum[r, :]).astype(BF)

        each_rows(rows, add)

    fetches[10].wait()
    fetches[9].wait()
    branch = branch_in
    whole = branch[...]
    grads_into(branch, mixed_low, gwo)
    out_sum = Collect(pc, sems, gwo, s_gwo, wout_out, True)
    out_sum.send()
    laying = finish()
    go(laying, 1)
    for fetch in halves_of:
        fetch.wait()
    fetches[2].wait()
    for at in range(0, wide, 256):
        dmix[:, at : at + 256] = jnp.dot(whole, wout[:, at : at + 256], preferred_element_type=F32).astype(BF)
    zero_rows(dsum)
    for i in (7, 5, 6, 3, 4, 8):
        fetches[i].wait()
    stops = Points(
        [lambda: go(laying, 3)],
        [lambda: go(laying, 1)],
        [out_sum.turn, lambda: go(laying, 1)],
        [lambda: go(laying, 1)],
    )

    def put_query(lanes, value):
        dqkv[:, lanes] = turn(value * 0.125, cosine[...], -sine[...]).astype(BF)

    attend_back(pc, query, query_t, dmix, mixed_t, lse, kv, kt, bias, dsum, put_query, stops)
    stops.drain()
    low_rows(dsum, dkv)
    keys = Collect(pc, sems, dkv, s_keys, dkv_own, True)
    keys.send()
    out_sum.finish()
    fetches[0].wait()
    fetches[1].wait()

    def query_grads(j, carry):
        at = pl.ds(pl.multiple_of(j * 256, 256), 256)
        left = jnp.concatenate([normed[0, s, :, at] for s in range(normed.shape[1])], axis=0)
        gq[at, :] = dot_tn(left, dqkv[:, :wide]).astype(BF)
        return carry

    lax.fori_loop(0, width // 256, query_grads, 0)
    query_sum = Collect(pc, sems, gq, s_gq, qkv_out, True)
    kv_sum = Collect(pc, sems, gkv, s_gkv, kv_out, True)
    keys.turn()
    query_sum.send()
    keys.finish()
    pre = dkv_own[...]
    dqkv[:, wide : wide + 128] = jnp.where(halves(), turn(pre, cosine[...], -sine[...]), pre).astype(BF)

    def put(cols, value):
        for s in range(part.shape[1]):
            part[0, s, :, cols] = value[s * rows : (s + 1) * rows].astype(BF)

    tiled_nt(dqkv[...], wqkv, put)

    def ending():
        yield from plane_reduce(near, sems, part, s_near, input_grad)
        gain_acc[...] = jnp.zeros_like(gain_acc)

        def back(r):
            v = tok[r, :].astype(F32)
            input_grad[r, :] = norm_back(r, v, input_grad[r, :], gains[0:1, :], middle_grad[r, :], gain_acc)

        each_rows(rows, back)
        own = jnp.sum(gain_acc[...], axis=0, keepdims=True)
        row = lax.broadcasted_iota(jnp.int32, (8, 128), 0)
        for j in range(by_group.shape[0]):
            cols = slice(j * 128, (j + 1) * 128)
            by_group[j] = jnp.where(row == 0, jnp.broadcast_to(own[:, cols], (8, 128)), gain_two[:, cols])
        yield from sum_gains(pc, sems, by_group, stage, mid, second, gain_out)

    end = ending()
    go(end, 1)

    def key_grads(j, carry):
        at = pl.ds(pl.multiple_of(j * 256, 256), 256)
        left = jnp.concatenate([normed[0, s, :, at] for s in range(normed.shape[1])], axis=0)
        gkv[at, :] = dot_tn(left, dqkv[:, wide : wide + 128]).astype(BF)
        return carry

    lax.fori_loop(0, width // 256, key_grads, 0)
    kv_sum.send()
    query_sum.turn(0, 1)
    go(end, 5)
    query_sum.turn(2, 3)
    kv_sum.turn()
    run(end)
    run(laying)
    query_sum.finish()
    kv_sum.finish()


def shards(
    tokens,
    segment_ids,
    key_mask,
    attn_gain,
    w_query,
    w_key,
    w_value,
    w_out,
    mlp_gain,
    w_gate,
    w_up,
    w_down,
    cotangent,
):
    n_dp, n_t = lax.axis_size("dp"), lax.axis_size("tensor")
    chain = 4
    groups = n_dp // chain
    rows, width = tokens.shape
    local = rows * n_t
    total = local * n_dp
    dim = w_key.shape[1]
    heads = w_query.shape[1] // dim
    wrows = w_query.shape[0]
    units = w_gate.shape[1] // chain
    qkv = w_query.shape[1] + 2 * dim
    me = lax.axis_index("dp")
    share = attn_gain.shape[0]
    tile = 128 // share

    first_row = me * local
    own_gain = jnp.concatenate(
        [
            jnp.tile(attn_gain, tile)[None],
            jnp.tile(mlp_gain, tile)[None],
            jnp.zeros((6, 128), F32),
        ],
        axis=0,
    )
    wqkv = jnp.concatenate([w_query, w_key, w_value], axis=1)
    wout = w_out.T

    held = (units + 127) // 128 * 128

    def by_chain(w):
        w = jnp.pad(w.reshape(wrows, chain, units), ((0, 0), (0, 0), (0, held - units)))
        return w.transpose(1, 0, 2)

    plane = chain * n_t * rows
    nbytes = 60 << 20
    positions = first_row + jnp.arange(local, dtype=jnp.int32)
    lane = jnp.arange(128, dtype=jnp.int32)
    frequency = THETA ** (-(lane % (dim // 2)).astype(F32) / (dim // 2))
    turned = positions.astype(F32)[:, None] * frequency[None, :]
    cosine = jnp.cos(turned)
    sine = jnp.sin(turned) * jnp.where(lane % dim < dim // 2, -1.0, 1.0)
    own_segments = lax.dynamic_slice(segment_ids, (first_row,), (local,))
    wide = heads * dim
    saved = [
        ((1, n_t, rows, width), BF),
        ((width, qkv), BF),
        ((width, wide), BF),
        ((local, wide), BF),
        ((wide, local), BF),
        ((total, 128), BF),
        ((64, total), BF),
        ((total, local), BF),
        ((wide, local), F32),
        ((local, wide), BF),
    ]
    (gains, wgu, wdn, cot, lse, middle, two, *kept) = call(
        functools.partial(forward_kernel, chain),
        "forward",
        0,
        [VM, VM] + [ANY] * 6 + [VM] * 4,
        [
            ((8, width), F32, VM),
            ((width, 2 * held), BF, ANY),
            ((width, held), BF, ANY),
            ((chain, n_t, rows, width), BF, ANY),
            ((heads, local), F32, VM),
            ((rows, width), F32, VM),
            ((chain, n_t, rows, width), BF, ANY),
        ]
        + [(shape, kind, ANY) for shape, kind in saved],
        [pltpu.VMEM(shape, kind) for shape, kind in saved]
        + [
            pltpu.VMEM((n_dp, n_t, 8, 128), F32),
            pltpu.VMEM((rows, width), BF),
            pltpu.VMEM((local, 2 * dim), BF),
            pltpu.VMEM((80, total), BF),
            pltpu.VMEM((1, n_t, rows, width), BF),
            pltpu.VMEM((rows, width), F32),
            pltpu.VMEM((rows, width), BF),
            pltpu.SemaphoreType.DMA((10,)),
        ]
        + plane_scratch(1, rows, width),
        (
            tokens,
            own_gain,
            wqkv,
            wout,
            by_chain(w_gate),
            by_chain(w_up),
            by_chain(w_down.T),
            cotangent,
            cosine,
            sine,
            own_segments[:, None] * 2 + 1,
            (segment_ids * 2 + key_mask)[None],
        ),
        nbytes,
    )
    (opart, middle_grad, branch, gain_two, ggu, gdn) = call(
        functools.partial(feed_kernel, chain),
        "feed",
        1,
        [ANY] * 4 + [VM] * 3,
        [
            ((chain, n_t, rows, width), BF, ANY),
            ((rows, width), F32, VM),
            ((1, n_t, rows, width), BF, ANY),
            ((8, width), F32, VM),
            ((chain, wrows, 2 * held), BF, ANY),
            ((chain, wrows, held), BF, ANY),
        ],
        [
            pltpu.VMEM((plane, width), BF),
            pltpu.VMEM((plane, width), BF),
            pltpu.VMEM((width, 2 * held), BF),
            pltpu.VMEM((width, held), BF),
            pltpu.VMEM((chain, n_t, rows, width), BF),
            pltpu.VMEM((plane, 2 * held), F32),
            pltpu.VMEM((plane, held), F32),
            pltpu.VMEM((plane, 2 * held), BF),
            pltpu.VMEM((plane, held), BF),
            pltpu.VMEM((chain, n_t, rows, width), BF),
            pltpu.VMEM((width, 2 * held), BF),
            pltpu.VMEM((width, held), BF),
        ]
        + plane_scratch(chain, rows, width)
        + collect_scratch(chain, groups, wrows, 2 * held)
        + collect_scratch(chain, groups, wrows, held)
        + [
            pltpu.VMEM((rows, width), BF),
            pltpu.VMEM((16, width), F32),
            pltpu.SemaphoreType.DMA((4,)),
        ],
        (two.reshape(plane, width), cot.reshape(plane, width), wgu, wdn, middle, cotangent, gains),
        nbytes,
    )

    def shard_of(g):
        return jnp.concatenate([g[z, :, :units].astype(F32) for z in range(chain)], axis=1)

    grad_gate, grad_up, grad_down = shard_of(ggu), shard_of(ggu[:, :, held:]), shard_of(gdn).T

    count = max(1, n_t * share // 128)
    layer_out, input_grad, gq, gkv, gwout, gain_sum = call(
        functools.partial(backward_kernel, chain),
        "backward",
        2,
        [ANY] * 12 + [VM] * 8,
        [
            ((rows, width), BF, VM),
            ((rows, width), F32, VM),
            ((wrows, wide), F32, VM),
            ((wrows, 2 * dim), F32, VM),
            ((wrows, wide), F32, VM),
            ((8, 128), F32, VM),
        ],
        [pltpu.VMEM(shape, kind) for shape, kind in saved]
        + [
            pltpu.VMEM((local, width), BF),
            pltpu.VMEM((2, chain, rows, width), BF),
            pltpu.SemaphoreType.DMA((13,)),
            pltpu.VMEM((local, wide), BF),
            pltpu.VMEM((total, 128), F32),
            pltpu.VMEM((total, 128), BF),
            pltpu.VMEM((local, 128), F32),
            pltpu.VMEM((local, qkv), BF),
            pltpu.VMEM((width, wide), BF),
            pltpu.VMEM((width, 128), BF),
            pltpu.VMEM((1, n_t, rows, width), BF),
            pltpu.VMEM((rows, width), F32),
            pltpu.VMEM((16, width), F32),
        ]
        + plane_scratch(chain, rows, width)
        + plane_scratch(1, rows, width)
        + dp_scratch(chain, groups, wrows, wide)
        + dp_scratch(chain, groups, wrows, wide)
        + dp_scratch(chain, groups, wrows, 128)
        + dp_scratch(chain, groups, local, 128)
        + [
            pltpu.VMEM((width // 128, 8, 128), F32),
            pltpu.VMEM((n_dp, count, 8, 128), F32),
            pltpu.VMEM((count, 8, 128), F32),
            pltpu.VMEM((n_t, 8, 128), F32),
        ],
        (
            *kept,
            branch.reshape(local, width),
            opart,
            lse,
            tokens,
            middle_grad,
            gains,
            gain_two,
            middle,
            cosine,
            sine,
        ),
        nbytes,
    )
    lane = (me * n_t + lax.axis_index("tensor")) * share % 128
    gain_grads = lax.dynamic_slice(gain_sum, (0, lane), (2, share))
    return (
        layer_out,
        input_grad,
        gain_grads[0],
        gq,
        gkv[:, :dim],
        gkv[:, dim:],
        gwout.T,
        gain_grads[1],
        grad_gate,
        grad_up,
        grad_down,
    )


def solution(mesh):
    in_specs = (
        P(("dp", "tensor"), None),
        P(),
        P(),
        P(("dp", "tensor")),
        P("dp", "tensor"),
        P("dp", "tensor"),
        P("dp", "tensor"),
        P("tensor", "dp"),
        P(("dp", "tensor")),
        P("dp", "tensor"),
        P("dp", "tensor"),
        P("tensor", "dp"),
        P(("dp", "tensor"), None),
    )
    out_specs = (
        P(("dp", "tensor"), None),
        P(("dp", "tensor"), None),
        P(("dp", "tensor")),
        P("dp", "tensor"),
        P("dp", "tensor"),
        P("dp", "tensor"),
        P("tensor", "dp"),
        P(("dp", "tensor")),
        P("dp", "tensor"),
        P("dp", "tensor"),
        P("tensor", "dp"),
    )
    return jax.shard_map(shards, mesh=mesh, in_specs=in_specs, out_specs=out_specs, check_vma=False)
```

```python
import functools

import jax
import jax.numpy as jnp
from jax import lax
from jax.experimental import pallas as pl
from jax.experimental.pallas import tpu as pltpu
from jax.sharding import PartitionSpec as P

EPS = 1e-05
NEG = -1e30
THETA = 10000.0
BF = jnp.bfloat16
F32 = jnp.float32
MESH = pl.DeviceIdType.MESH
ANY = pl.BlockSpec(memory_space=pl.ANY)
VM = pl.BlockSpec(memory_space=pltpu.VMEM)


def sem_count():
    return 200 + 18 * lax.axis_size("dp")


class Sems:
    def __init__(self, send, recv):
        self.send, self.recv, self.used = send, recv, 0

    def take(self, count):
        base = self.used
        self.used += count
        assert self.used <= sem_count()
        return base


class Place:
    def __init__(self, chain):
        self.n_dp = lax.axis_size("dp")
        self.n_t = lax.axis_size("tensor")
        self.chain = chain
        self.groups = self.n_dp // chain
        self.d = lax.axis_index("dp")
        self.s = lax.axis_index("tensor")
        self.z = self.d // self.groups
        self.t = self.d % self.groups
        self.y = self.s // 2
        self.c = self.s % 2
        self.sy = (1 - self.y) * 2 + self.c
        self.sc = self.y * 2 + 1 - self.c
        self.so = (1 - self.y) * 2 + 1 - self.c
        self.above = self.at(z=jnp.minimum(self.z + 1, chain - 1))
        self.below = self.at(z=jnp.maximum(self.z - 1, 0))

    def at(self, z=None, t=None, s=None):
        z = self.z if z is None else z
        t = self.t if t is None else t
        s = self.s if s is None else s
        return {"dp": z * self.groups + t, "tensor": s}


def when(pred, act):
    if pred is None:
        act()
    else:
        pl.when(pred)(act)


class Copies:
    def __init__(self, sems):
        self.sems = sems
        self.sent = []

    def go(self, i, src, dst, where, pred=None):
        copy = pltpu.make_async_remote_copy(
            src_ref=src,
            dst_ref=dst,
            send_sem=self.sems.send.at[i],
            recv_sem=self.sems.recv.at[i],
            device_id=where,
            device_id_type=MESH,
        )
        when(pred, copy.start)
        self.sent.append((copy, pred))

    def keep(self, i, src, dst):
        copy = pltpu.make_async_copy(src, dst, self.sems.send.at[i])
        copy.start()
        return copy

    def arrive(self, i, dst, where, pred=None):
        copy = pltpu.make_async_remote_copy(
            src_ref=dst,
            dst_ref=dst,
            send_sem=self.sems.send.at[i],
            recv_sem=self.sems.recv.at[i],
            device_id=where,
            device_id_type=MESH,
        )
        when(pred, copy.wait_recv)

    def describe(self, i, src):
        return pltpu.make_async_remote_copy(
            src_ref=src,
            dst_ref=src,
            send_sem=self.sems.send.at[i],
            recv_sem=self.sems.recv.at[i],
            device_id={"dp": lax.axis_index("dp"), "tensor": lax.axis_index("tensor")},
            device_id_type=MESH,
        )

    def finish(self):
        for copy, pred in self.sent:
            when(pred, copy.wait_send)


def greet(pc):
    barrier = pltpu.get_barrier_semaphore()
    for k in range(1, pc.n_dp):
        pl.semaphore_signal(
            barrier, inc=1, device_id={"dp": (pc.d + k) % pc.n_dp, "tensor": pc.s}, device_id_type=MESH
        )
    for k in range(1, pc.n_t):
        pl.semaphore_signal(
            barrier, inc=1, device_id={"dp": pc.d, "tensor": (pc.s + k) % pc.n_t}, device_id_type=MESH
        )
    pl.semaphore_wait(barrier, pc.n_dp + pc.n_t - 2)


def run(*tasks):
    live = list(tasks)
    while live:
        live = [task for task in live if next(task, "end") != "end"]


def go(task, steps):
    for _ in range(steps):
        next(task, None)


class Points:
    def __init__(self, *acts):
        self.acts = list(acts)

    def __call__(self):
        if self.acts:
            for act in self.acts.pop(0):
                act()

    def drain(self):
        while self.acts:
            self()


def chain_steps(pc):
    chain, z = pc.chain, pc.z
    for k in range(chain - 1):
        for side in (0, 1):
            if side == 0:
                got = z - 1 - k >= 0
                yield k, side, jnp.maximum(z - 1 - k, 0), got, pc.above, jnp.logical_and(got, z + 1 < chain)
            else:
                got = z + 1 + k <= chain - 1
                yield k, side, jnp.minimum(z + 1 + k, chain - 1), got, pc.below, jnp.logical_and(got, z > 0)


def plane_gather(pc, sems, own, out, parts=1):
    chain, z, s = pc.chain, pc.z, pc.s
    width = own.shape[1] // parts
    cp = Copies(sems)
    base = sems.take(1 + 8 * chain * parts)

    def sem(kind, i, p):
        return base + 1 + (kind * chain + i) * parts + p

    def view(b, col, p):
        return out.at[b, col, :, pl.ds(p * width, width)]

    keep = cp.keep(base, own, out.at[z, s])
    for p in range(parts):
        src = own.at[:, pl.ds(p * width, width)]
        cp.go(sem(2, 0, p), src, view(z, s, p), pc.at(s=pc.sy))
        cp.go(sem(4, 0, p), src, view(z, s, p), pc.at(s=pc.sc))
    yield "own"
    for p in range(parts):
        src = own.at[:, pl.ds(p * width, width)]
        if chain > 1:
            cp.go(sem(0, 0, p), src, view(z, s, p), pc.above, z + 1 < chain)
            cp.go(sem(1, 0, p), src, view(z, s, p), pc.below, z > 0)
    yield "start"
    crossing = [(z, None, 0, p) for p in range(parts)]
    landed = []

    def cross(count):
        for _ in range(min(count, len(crossing))):
            b, got, i, p = crossing.pop(0)
            cp.arrive(sem(2, i, p), view(b, pc.sy, p), pc.at(), got)
            cp.go(sem(6, i, p), view(b, pc.sy, p), view(b, pc.sy, p), pc.at(s=pc.sc), got)
            landed.append((b, got, i, p))

    steps = list(chain_steps(pc))
    for k in range(chain - 1):
        for p in range(parts):
            for step, side, b, got, onward, more in steps:
                if step != k:
                    continue
                i = 1 + k if side == 0 else chain + k
                cp.arrive(sem(side, k, p), view(b, s, p), pc.at(), got)
                if k < chain - 2:
                    cp.go(sem(side, k + 1, p), view(b, s, p), view(b, s, p), onward, more)
                cp.go(sem(2, i, p), view(b, s, p), view(b, s, p), pc.at(s=pc.sy), got)
                cp.go(sem(4, i, p), view(b, s, p), view(b, s, p), pc.at(s=pc.sc), got)
                crossing.append((b, got, i, p))
            cross(1 if k == 0 else 2)
            yield "more"
    yield "tail"
    while crossing:
        cross(2)
        yield "more"
    for b, got, i, p in landed:
        cp.arrive(sem(4, i, p), view(b, pc.sc, p), pc.at(), got)
        cp.arrive(sem(6, i, p), view(b, pc.so, p), pc.at(), got)
    keep.wait()
    cp.finish()
    yield


def far_first(chain, z, j):
    if isinstance(j, int) and j == chain - 1:
        return z
    up = jnp.where(j < chain - 1 - z, chain - 1 - j, j - (chain - 1 - z))
    down = jnp.where(j < z, j, chain - 1 - (j - z))
    return jnp.where(j == chain - 1, z, jnp.where(2 * z < chain, up, down))


def each_rows(count, fn, rows=16):
    def body(i, carry):
        fn(pl.ds(pl.multiple_of(i * rows, rows), rows))
        return carry

    lax.fori_loop(0, count // rows, body, 0)


def chain_reduce(pc, cp, right, left, b, last, value, zsend, came, store, rows, cols):
    chain, z = pc.chain, pc.z
    if not last:
        fromleft = jnp.logical_and(b > z, z > 0)
        fromright = jnp.logical_and(b < z, z < chain - 1)
        cp.arrive(right, came.at[b, :, cols], pc.at(), fromleft)
        cp.arrive(left, came.at[b, :, cols], pc.at(), fromright)
        some = jnp.logical_or(fromleft, fromright)

        @pl.when(some)
        def _():
            def add(r):
                zsend[b, r, cols] = (value(r) + came[b, r, cols].astype(F32)).astype(BF)

            each_rows(rows, add)

        @pl.when(jnp.logical_not(some))
        def _():
            def add(r):
                zsend[b, r, cols] = value(r).astype(BF)

            each_rows(rows, add)

        cp.go(right, zsend.at[b, :, cols], came.at[b, :, cols], pc.above, b > z)
        slot = jnp.where(b == z - 1, chain, b)
        cp.go(left, zsend.at[b, :, cols], came.at[slot, :, cols], pc.below, b < z)
        return

    def first(r):
        store(r, value(r), False)

    each_rows(rows, first)
    if chain > 1:

        @pl.when(z > 0)
        def _():
            cp.arrive(right, came.at[b, :, cols], pc.at())

            def add(r):
                store(r, came[b, r, cols].astype(F32), True)

            each_rows(rows, add)

        @pl.when(z < chain - 1)
        def _():
            cp.arrive(left, came.at[chain, :, cols], pc.at())

            def add(r):
                store(r, came[chain, r, cols].astype(F32), True)

            each_rows(rows, add)


def plane_scratch(chain, rows, width):
    return [
        pltpu.VMEM((chain, 2, rows, width), BF),
        pltpu.VMEM((chain, rows, width), BF),
        pltpu.VMEM((chain, rows, width), BF),
        pltpu.VMEM((chain if chain > 1 else 1, rows, width) if chain > 1 else (1, 16, 128), BF),
        pltpu.VMEM((chain + 1, rows, width) if chain > 1 else (1, 16, 128), BF),
    ]


class PlaneReduce:
    def __init__(self, pc, sems, part, scratch, out, held=None):
        self.pc, self.part, self.out, self.held = pc, part, out, held
        self.crecv, self.csum, self.yrecv, self.zsend, self.came = scratch
        self.cp = Copies(sems)
        self.base = sems.take(5 * pc.chain)
        self.rows, self.width = out.shape

    def sem(self, kind, i):
        return self.base + kind * self.pc.chain + i

    def block(self, j):
        return far_first(self.pc.chain, self.pc.z, j)

    def pass_core(self, over, j, b, cp=None):
        pc = self.pc
        (cp or self.cp).go(
            self.sem(over, j),
            self.part.at[b, pc.so if over else pc.sc],
            self.crecv.at[b, over],
            pc.at(s=pc.sc),
        )

    def cross(self, j, b, cp=None):
        pc, crecv, csum = self.pc, self.crecv, self.csum
        cp = cp or self.cp
        cp.arrive(self.sem(1, j), crecv.at[b, 1], pc.at())

        def add(r):
            csum[b, r, :] = (self.own(0, b, r).astype(F32) + crecv[b, 1, r, :].astype(F32)).astype(BF)

        each_rows(self.rows, add)
        cp.go(self.sem(2, j), csum.at[b], self.yrecv.at[b], pc.at(s=pc.sy))

    def own(self, here, b, r):
        if self.held is not None:
            return self.held[here, b, r, :]
        return self.part[b, self.pc.s if here else self.pc.sy, r, :]

    def steps(self):
        pc = self.pc
        chain, z = pc.chain, pc.z
        crecv, yrecv, out = self.crecv, self.yrecv, self.out
        cp = self.cp
        todo = [(j, self.block(j)) for j in range(chain)]
        for j, b in todo:
            self.pass_core(1, j, b)
        yield
        ahead = list(todo)
        for _ in range(min(2, chain)):
            self.cross(*ahead.pop(0))
            yield
        for j, b in todo:
            self.pass_core(0, j, b)
        yield
        for j, b in todo:
            cp.arrive(self.sem(0, j), crecv.at[b, 0], pc.at())
            cp.arrive(self.sem(2, j), yrecv.at[b], pc.at())
            if ahead:
                self.cross(*ahead.pop(0))

            def value(r):
                return (
                    self.own(1, b, r).astype(F32)
                    + crecv[b, 0, r, :].astype(F32)
                    + yrecv[b, r, :].astype(F32)
                )

            def store(r, term, more):
                out[r, :] = out[r, :] + term if more else term

            chain_reduce(
                pc,
                cp,
                self.sem(3, b),
                self.sem(4, b),
                b,
                j == chain - 1,
                value,
                self.zsend,
                self.came,
                store,
                self.rows,
                pl.ds(0, self.width),
            )
            yield
        cp.finish()
        yield


def plane_reduce(pc, sems, part, scratch, out):
    return PlaneReduce(pc, sems, part, scratch, out).steps()


def dp_gather(pc, sems, own, out, parts=1):
    chain, groups, z, t = pc.chain, pc.groups, pc.z, pc.t
    cp = Copies(sems)
    base = sems.take(1 + (2 * chain + 2 * chain * groups) * parts)
    rows = own.shape[0] // parts

    def cut(ref, p):
        return ref.at[pl.ds(p * rows, rows)]

    def along(side, k, p):
        return base + 1 + (side * chain + k) * parts + p

    def across(i, g, p):
        return base + 1 + (2 * chain + i * groups + g) * parts + p

    keep = cp.keep(base, own, out(pc.d))
    for p in range(parts):
        for g in range(1, groups):
            cp.go(across(0, g, p), cut(own, p), cut(out(pc.d), p), pc.at(t=(t + g) % groups))
    yield "own"
    if chain > 1:
        for p in range(parts):
            cp.go(along(0, 0, p), cut(own, p), cut(out(pc.d), p), pc.above, z + 1 < chain)
            cp.go(along(1, 0, p), cut(own, p), cut(out(pc.d), p), pc.below, z > 0)
    yield "start"
    landed = [(z, None, 0)]
    for k in range(chain - 1):
        for p in range(parts):
            for step, side, b, got, onward, more in chain_steps(pc):
                if step != k:
                    continue
                i = 1 + k if side == 0 else chain + k
                block = cut(out(b * groups + t), p)
                cp.arrive(along(side, k, p), block, pc.at(), got)
                if k < chain - 2:
                    cp.go(along(side, k + 1, p), block, block, onward, more)
                for g in range(1, groups):
                    cp.go(across(i, g, p), block, block, pc.at(t=(t + g) % groups), got)
                if p == 0:
                    landed.append((b, got, i))
            yield "more"
    yield "tail"
    for b, got, i in landed:
        for p in range(parts):
            for g in range(1, groups):
                cp.arrive(across(i, g, p), cut(out(b * groups + (t - g + groups) % groups), p), pc.at(), got)
    keep.wait()
    cp.finish()
    yield "end"


def plane_direct(pc, sems, own, out):
    chain, z, s = pc.chain, pc.z, pc.s
    cp = Copies(sems)
    base = sems.take(1 + 4 * chain)

    def sem(kind, k):
        return base + 1 + kind * chain + k

    keep = cp.keep(base, own, out.at[z, s])
    cp.go(sem(1, 0), own, out.at[z, s], pc.at(s=pc.sy))
    cp.go(sem(2, 0), own, out.at[z, s], pc.at(s=pc.sc))
    yield "own"
    for k in range(1, chain):
        to = (z + k) % chain
        cp.go(sem(0, k), own, out.at[z, s], pc.at(z=to))
    yield "start"
    for k in range(1, chain):
        b = (z - k + chain) % chain
        cp.arrive(sem(0, k), out.at[b, s], pc.at())
        cp.go(sem(1, k), out.at[b, s], out.at[b, s], pc.at(s=pc.sy))
        cp.go(sem(2, k), out.at[b, s], out.at[b, s], pc.at(s=pc.sc))
    yield "turned"
    for k in range(chain):
        b = (z - k + chain) % chain
        cp.arrive(sem(1, k), out.at[b, pc.sy], pc.at())
        cp.go(sem(3, k), out.at[b, pc.sy], out.at[b, pc.sy], pc.at(s=pc.sc))
    yield "crossed"
    for k in range(chain):
        b = (z - k + chain) % chain
        cp.arrive(sem(2, k), out.at[b, pc.sc], pc.at())
        cp.arrive(sem(3, k), out.at[b, pc.so], pc.at())
    keep.wait()
    cp.finish()
    yield "end"


def spread(pc, sems, blocks, out):
    chain, groups, z, t = pc.chain, pc.groups, pc.z, pc.t
    cp = Copies(sems)
    base = sems.take(1 + chain + chain * groups)
    along, across = base + 1, base + 1 + chain
    keep = cp.keep(base, blocks(z), out(pc.d))
    for g in range(1, groups):
        cp.go(across + g, blocks(z), out(pc.d), pc.at(t=(t + g) % groups))
    yield "own"
    for k in range(1, chain):
        to = (z + k) % chain
        cp.go(along + k, blocks(to), out(pc.d), pc.at(z=to))
    yield "start"
    for k in range(1, chain):
        block = out((z - k + chain) % chain * groups + t)
        cp.arrive(along + k, block, pc.at())
        for g in range(1, groups):
            cp.go(across + k * groups + g, block, block, pc.at(t=(t + g) % groups))
        yield "more"
    yield "tail"
    for k in range(chain):
        for g in range(1, groups):
            block = out((z - k + chain) % chain * groups + (t - g + groups) % groups)
            cp.arrive(across + k * groups + g, block, pc.at())
    keep.wait()
    cp.finish()
    yield "end"


class Side:
    def __init__(self, pc, sems, part, recv):
        self.pc, self.part, self.recv = pc, part, recv
        self.rows, self.width = recv.shape[2], recv.shape[3]
        self.base = sems.take(pc.chain * pc.groups)

    def start(self, i):
        return pl.multiple_of(i * self.rows, self.rows)

    def send(self, cp, j, b):
        pc = self.pc
        for g in range(1, pc.groups):
            to = (pc.t + g) % pc.groups
            cp.go(
                self.base + j * pc.groups + g,
                self.part.at[pl.ds(self.start(b * pc.groups + to), self.rows)],
                self.recv.at[g - 1, b],
                pc.at(t=to),
            )

    def arrive(self, cp, j, b):
        for g in range(1, self.pc.groups):
            cp.arrive(self.base + j * self.pc.groups + g, self.recv.at[g - 1, b], self.pc.at())

    def value(self, b, r):
        at = self.start(b * self.pc.groups + self.pc.t)
        total = self.part[pl.ds(pl.multiple_of(at + r.start, 16), r.size), :].astype(F32)
        for g in range(1, self.pc.groups):
            total = total + self.recv[g - 1, b, r, :].astype(F32)
        return total


def dp_scratch(chain, groups, rows, width):
    return [
        pltpu.VMEM((max(groups - 1, 1), chain, rows, width), BF),
        pltpu.VMEM((chain, rows, width), BF),
        pltpu.VMEM((chain, rows, width), BF),
    ]


class Moves:
    def __init__(self, sem):
        self.sem, self.count = sem, 0

    def start(self, src, dst):
        copy = pltpu.make_async_copy(src, dst, self.sem.at[self.count])
        self.count += 1
        copy.start()
        return copy


class Collect:
    def __init__(self, pc, sems, part, scratch, out, summed):
        self.pc, self.out, self.summed = pc, out, summed
        self.side = Side(pc, sems, part, scratch[0])
        self.sums = scratch[1]
        self.came = scratch[2] if summed else out
        self.cp = Copies(sems)
        self.along = sems.take(pc.chain)
        self.kept = None

    def block(self, k):
        return (self.pc.z + self.pc.chain - 1 - k) % self.pc.chain

    def send(self, *which):
        for k in which or range(self.pc.chain):
            self.side.send(self.cp, k, self.block(k))

    def turn(self, *which):
        pc, chain, z, side = self.pc, self.pc.chain, self.pc.z, self.side
        for k in which or range(chain):
            b = self.block(k)
            side.arrive(self.cp, k, b)
            if k == chain - 1 and self.summed:

                def first(r):
                    self.out[r, :] = side.value(b, r)

                each_rows(side.rows, first)
                continue

            def add(r):
                self.sums[b, r, :] = side.value(b, r).astype(BF)

            each_rows(side.rows, add)
            if k < chain - 1:
                self.cp.go(self.along + k, self.sums.at[b], self.came.at[z], pc.at(z=b))
            else:
                self.kept = self.cp.keep(self.along + k, self.sums.at[b], self.out.at[z])

    def finish(self):
        pc, chain, z, side = self.pc, self.pc.chain, self.pc.z, self.side
        for k in range(chain - 1):
            b = (z - (chain - 1 - k) + chain) % chain
            self.cp.arrive(self.along + k, self.came.at[b], pc.at())
            if self.summed:

                def add(r):
                    self.out[r, :] = self.out[r, :] + self.came[b, r, :].astype(F32)

                each_rows(side.rows, add)
        if self.kept is not None:
            self.kept.wait()
        self.cp.finish()


def collect_scratch(chain, groups, rows, width):
    return dp_scratch(chain, groups, rows, width)[:2]


def share_gains(pc, sems, own, table):
    cp = Copies(sems)
    base = sems.take(pc.n_dp + pc.n_t)
    table[pc.d, pc.s] = own[...]
    for k in range(1, pc.n_t):
        cp.go(base + k, table.at[pc.d, pc.s], table.at[pc.d, pc.s], {"dp": pc.d, "tensor": (pc.s + k) % pc.n_t})
    yield
    for k in range(1, pc.n_t):
        cp.arrive(base + k, table.at[pc.d, (pc.s - k + pc.n_t) % pc.n_t], pc.at())
    second = base + pc.n_t
    for k in range(1, pc.n_dp):
        cp.go(second + k, table.at[pc.d], table.at[pc.d], {"dp": (pc.d + k) % pc.n_dp, "tensor": pc.s})
    yield
    for k in range(1, pc.n_dp):
        cp.arrive(second + k, table.at[(pc.d - k + pc.n_dp) % pc.n_dp], pc.at())
    cp.finish()
    yield


def lay_gains(pc, table, gains):
    lanes = 128
    devices = pc.n_dp * pc.n_t
    each = gains.shape[1] // devices
    per = lanes // each
    lane = lax.broadcasted_iota(jnp.int32, (8, lanes), 1)
    for j in range(gains.shape[1] // lanes):
        row = table[(j * per) // pc.n_t, (j * per) % pc.n_t]
        for k in range(1, per):
            o = j * per + k
            row = jnp.where(lane >= k * each, table[o // pc.n_t, o % pc.n_t], row)
        gains[:, j * lanes : (j + 1) * lanes] = row


def sum_gains(pc, sems, groups_of, stage, mid, second, out):
    count = stage.shape[1]
    n_dp, n_t = pc.n_dp, pc.n_t
    cp = Copies(sems)
    base = sems.take(n_dp + n_t)

    def start_of(d):
        return d * groups_of.shape[0] // n_dp

    for k in range(1, n_dp):
        to = (pc.d + k) % n_dp
        cp.go(
            base + k,
            groups_of.at[pl.ds(start_of(to), count)],
            stage.at[pc.d],
            {"dp": to, "tensor": pc.s},
        )
    stage[pc.d] = groups_of[pl.ds(start_of(pc.d), count)]
    yield
    for k in range(1, n_dp):
        cp.arrive(base + k, stage.at[(pc.d - k + n_dp) % n_dp], pc.at())
    total = stage[0]
    for k in range(1, n_dp):
        total = total + stage[k]
    mid[...] = total
    yield
    last = base + n_dp
    for k in range(1, n_t):
        to = (pc.s + k) % n_t
        cp.go(last + k, mid.at[to * count // n_t], second.at[pc.s], {"dp": pc.d, "tensor": to})
    second[pc.s] = mid[pc.s * count // n_t]
    yield
    for k in range(1, n_t):
        cp.arrive(last + k, second.at[(pc.s - k + n_t) % n_t], pc.at())
    total = second[0]
    for k in range(1, n_t):
        total = total + second[k]
    out[...] = total
    cp.finish()
    yield


def call(kernel, name, number, ins, outs, scratch, operands, cost):
    sems = [pltpu.SemaphoreType.DMA((sem_count(),))] * 2
    return pl.pallas_call(
        kernel,
        out_shape=[jax.ShapeDtypeStruct(shape, kind) for shape, kind, _ in outs],
        in_specs=ins,
        out_specs=[space for _, _, space in outs],
        scratch_shapes=list(scratch) + sems,
        name=name,
        cost_estimate=pl.CostEstimate(flops=0, bytes_accessed=cost, transcendentals=0),
        compiler_params=pltpu.CompilerParams(
            collective_id=number, has_side_effects=True, vmem_limit_bytes=63 << 20
        ),
    )(*operands)


def unit(v):
    return lax.rsqrt(jnp.mean(v * v, axis=-1, keepdims=True) + EPS)


def gcd_of(n, size):
    while n % size:
        size //= 2
    return size


def rows_of(ref, count):
    return lambda d: ref.at[pl.ds(pl.multiple_of(d * count, count), count)]


def halves():
    lane = lax.broadcasted_iota(jnp.int32, (1, 128), 1)
    return lane < 64


def turn(x, cosine, sine):
    lane = lax.broadcasted_iota(jnp.int32, x.shape, 1)
    swapped = jnp.where(lane % 64 < 32, pltpu.roll(x, 96, 1), pltpu.roll(x, 32, 1))
    return x * cosine + swapped * sine


def key_range(first, count, total, size):
    long_end = 5 * total // 8
    low = jnp.where(first >= long_end + total // 32 - 16, long_end, 0)
    return low // size, (first + count + size - 1) // size


def fill_bias(bias, first, low, high, size, qinfo, kinfo):
    qpos = first + lax.broadcasted_iota(jnp.int32, qinfo.shape, 0)

    def fill(j, carry):
        at = pl.multiple_of(j * size, size)
        cols = pl.ds(at, size)
        kpos = at + lax.broadcasted_iota(jnp.int32, (1, size), 1)
        allowed = (kpos == qpos) | ((kinfo[:, cols] == qinfo[...]) & (kpos < qpos))
        bias[cols, :] = jnp.where(allowed, 0.0, NEG).T.astype(BF)
        return carry

    lax.fori_loop(low, high, fill, 0)


def turn_values(kv, vt):
    size = gcd_of(kv.shape[0], 256)
    vt[64:80, :] = jnp.ones((16, kv.shape[0]), BF)

    def body(j, carry):
        r = pl.ds(pl.multiple_of(j * size, size), size)
        vt[0:64, r] = kv[r, :].astype(F32).T[64:128, :].astype(BF)
        return carry

    lax.fori_loop(0, kv.shape[0] // size, body, 0)


def turn_keys(kv, kt):
    size = gcd_of(kv.shape[0], 256)

    def body(j, carry):
        r = pl.ds(pl.multiple_of(j * size, size), size)
        kt[:, r] = kv[r, :].astype(F32).T[0:64, :].astype(BF)
        return carry

    lax.fori_loop(0, kv.shape[0] // size, body, 0)


def attend(pc, query_t, kv, vt, bias, mixed_t, mixed_low, lse, step):
    local, total = query_t.shape[1], kv.shape[0]
    size = gcd_of(total, 640)
    low, high = key_range(pc.d * local, local, total, size)

    def one(chunk, carry):
        first = pl.multiple_of(chunk * 128, 128)
        queries = tuple(query_t[pl.ds(pl.multiple_of(first + k * 64, 64), 64), :] for k in range(2))

        def body(j, carry):
            rows = pl.ds(pl.multiple_of(j * size, size), size)
            key, value, mask = kv[rows, 0:64], vt[:, rows], bias[rows, :].astype(F32)
            out = []
            for q, (top, acc) in zip(queries, carry):
                s = jnp.dot(key, q, preferred_element_type=F32) + mask
                new = jnp.maximum(top, jnp.max(s, axis=0, keepdims=True))
                p = jnp.exp(s - new).astype(BF)
                acc = acc * jnp.exp(top - new) + jnp.dot(value, p, preferred_element_type=F32)
                out.append((new, acc))
            return tuple(out)

        start = (jnp.full((1, local), NEG, F32), jnp.zeros((80, local), F32))
        done = lax.fori_loop(low, high, body, (start, start))
        pair = []
        for k, (top, acc) in enumerate(done):
            tot = acc[64:65, :]
            pair.append(acc[0:64, :] / tot)
            lse[pl.ds(2 * chunk + k, 1), :] = top + jnp.log(tot)
        both = jnp.concatenate(pair, axis=0)
        mixed_t[pl.ds(first, 128), :] = both
        mixed_low[:, pl.ds(first, 128)] = both.T.astype(BF)
        return carry

    chunks = query_t.shape[0] // 128
    for half in range(2):
        lax.fori_loop(half * chunks // 2, (half + 1) * chunks // 2, one, 0)
        step()


def tiled_nt(left, right, put, size=256):
    size = gcd_of(right.shape[0], size)

    def body(j, carry):
        cols = pl.ds(pl.multiple_of(j * size, size), size)
        put(
            cols,
            lax.dot_general(left, right[cols, :], (((1,), (1,)), ((), ())), preferred_element_type=F32),
        )
        return carry

    lax.fori_loop(0, right.shape[0] // size, body, 0)


def forward_kernel(chain, *refs):
    (tok, own_gain, wqkv, wout, wgate, wup, wdown, cot, cosine, sine, qinfo, kinfo) = refs[:12]
    (
        gains,
        wgu_all,
        wdown_all,
        cot_all,
        lse,
        middle,
        two_all,
    ) = refs[12:19]
    kept, rest = refs[19:29], refs[29:]
    (normed_all, wqkv_all, wout_all, query, query_t, kv_all, kt, bias, mixed_t, mixed_low) = rest[:10]
    table, normed, own_kv, vt, part, total, two, local_sem = rest[10:18]
    scratch, (send, recv) = rest[18:23], rest[23:]
    moves = Moves(local_sem)
    stores = []

    def keep(*names):
        for i in names:
            stores.append(moves.start(rest[i], kept[i]))

    sems = Sems(send, recv)
    pc, near = Place(chain), Place(1)
    rows, width = tok.shape
    wrows = wqkv.shape[0]
    local = query.shape[0]
    wide = query.shape[1]
    greet(pc)

    def head():
        yield from share_gains(pc, sems, own_gain, table)
        lay_gains(pc, table, gains)

        def norm(r):
            v = tok[r, :].astype(F32)
            normed[r, :] = (v * unit(v) * gains[0:1, :]).astype(BF)

        each_rows(rows, norm)
        yield from plane_gather(near, sems, normed, normed_all)

    first = dp_gather(pc, sems, wqkv, rows_of(wqkv_all, wrows), 2)
    outw = dp_gather(pc, sems, wout, rows_of(wout_all, wrows), 2)
    half = wgu_all.shape[1] // 2
    gatew = spread(pc, sems, lambda d: wgate.at[d], rows_of(wgu_all.at[:, pl.ds(0, half)], wrows))
    upw = spread(pc, sems, lambda d: wup.at[d], rows_of(wgu_all.at[:, pl.ds(half, half)], wrows))
    downw = spread(pc, sems, lambda d: wdown.at[d], rows_of(wdown_all, wrows))
    cots = plane_gather(pc, sems, cot, cot_all, 2)
    beside = head()
    go(first, 2)
    go(beside, 1)
    go(cots, 1)
    go(first, 2)
    go(beside, 1)
    go(first, 2)
    go(cots, 1)
    go(beside, 2)
    go(first, 3)
    go(outw, 2)
    run(beside)
    run(first)
    go(outw, 2)
    go(cots, 2)

    here = jnp.concatenate([normed_all[0, s] for s in range(normed_all.shape[1])], axis=0)
    size = 256
    for at in range(0, wide, size):
        pre = jnp.dot(here, wqkv_all[:, at : at + size], preferred_element_type=F32)
        for lanes in range(0, size, 128):
            turned = turn(pre[:, lanes : lanes + 128], cosine[...], sine[...])
            turned = turned * 0.125
            query[:, at + lanes : at + lanes + 128] = turned.astype(BF)
            query_t[at + lanes : at + lanes + 128, :] = turned.T.astype(BF)
    pre = jnp.dot(here, wqkv_all[:, wide : wide + 128], preferred_element_type=F32)
    own_kv[...] = jnp.where(halves(), turn(pre, cosine[...], sine[...]), pre).astype(BF)
    go(outw, 2)
    run(dp_gather(pc, sems, own_kv, rows_of(kv_all, local)))
    keep(0, 1, 3, 4, 5)
    go(gatew, 2)
    go(outw, 3)
    go(cots, 2)
    turn_values(kv_all, vt)
    size = gcd_of(kv_all.shape[0], 640)
    low, high = key_range(pc.d * local, local, kv_all.shape[0], size)
    fill_bias(bias, pc.d * local, low, high, size, qinfo, kinfo)
    go(upw, 2)
    stops = Points([lambda: go(cots, 2), lambda: go(downw, 2)], [lambda: run(outw)])
    attend(pc, query_t, kv_all, vt, bias, mixed_t, mixed_low, lse, stops)
    stops.drain()


    def put(cols, value):
        for s in range(part.shape[1]):
            part[0, s, :, cols] = value[s * rows : (s + 1) * rows].astype(BF)

    tiled_nt(mixed_low[...], wout_all, put)
    totals = plane_reduce(near, sems, part, scratch, total)
    go(totals, 1)
    keep(2, 7, 8, 9)
    go(gatew, 3)
    turn_keys(kv_all, kt)
    keep(6)
    run(totals)

    def norm(r):
        v = tok[r, :].astype(F32) + total[r, :]
        middle[r, :] = v
        two[r, :] = (v * unit(v) * gains[1:2, :]).astype(BF)

    each_rows(rows, norm)
    twos = plane_gather(pc, sems, two, two_all, 2)
    go(twos, 2)
    go(upw, 3)
    go(twos, 2)
    go(cots, 3)
    go(twos, 2)
    go(downw, 3)
    run(twos)
    run(cots, gatew, upw, downw)
    for store in stores:
        store.wait()


def dot_nt(a, b):
    return lax.dot_general(a, b, (((1,), (1,)), ((), ())), preferred_element_type=F32)


def dot_tn(a, b):
    return lax.dot_general(a, b, (((0,), (0,)), ((), ())), preferred_element_type=F32)


def grads_into(left, right, out, size=256):
    def body(j, carry):
        at = pl.ds(pl.multiple_of(j * size, size), size)
        out[at, :] = dot_tn(left[:, at], right[...]).astype(BF)
        return carry

    lax.fori_loop(0, out.shape[0] // size, body, 0)


def norm_back(r, v, grad, gain, extra, gain_acc):
    root = unit(v)
    xhat = v * root
    e = grad * gain
    gain_acc[...] += grad * xhat
    return extra + root * (e - xhat * jnp.mean(e * xhat, axis=-1, keepdims=True))


def tiled_in(left, right, out, size):
    def body(j, carry):
        at = pl.ds(pl.multiple_of(j * size, size), size)
        out[:, at] = jnp.dot(left[...], right[:, at], preferred_element_type=F32)
        return carry

    lax.fori_loop(0, out.shape[1] // size, body, 0)


def feed_kernel(chain, *refs):
    (two_all, cot_all, wgu_all, wdn_all, middle, cot, gains) = refs[:7]
    (opart_all, middle_grad, branch_all, gain_out, cgu, cdn) = refs[7:13]
    rest = refs[13:]
    two, cotan, wgu, wdn, opart, gu, h, both, hidden, npart, ggu, gdn = rest[:12]
    s_part = rest[12:17]
    s_gu, s_dn = rest[17:19], rest[19:21]
    branch, gain_acc, local_sem, send, recv = rest[21:]
    sems = Sems(send, recv)
    pc, near = Place(chain), Place(1)
    fetches = []
    for i, (src, dst) in enumerate(((wgu_all, wgu), (two_all, two), (wdn_all, wdn), (cot_all, cotan))):
        fetches.append(pltpu.make_async_copy(src, dst, local_sem.at[i]))
        fetches[-1].start()
    greet(pc)
    rows, width = middle.shape
    n_t = npart.shape[1]
    units = hidden.shape[1]
    reduce = PlaneReduce(pc, sems, npart, s_part, middle_grad)
    fetches[0].wait()
    fetches[1].wait()
    tiled_in(two, wgu, gu, 256)
    fetches[2].wait()
    fetches[3].wait()
    tiled_in(cotan, wdn, h, 128)

    def gates(r):
        for at in range(0, units, 128):
            left, right = pl.ds(at, 128), pl.ds(units + at, 128)
            g, u, k = gu[r, left], gu[r, right], h[r, left]
            sigma = 1.0 / (1.0 + jnp.exp(-g))
            silu = g * sigma
            hidden[r, left] = (silu * u).astype(BF)
            both[r, left] = (k * u * sigma * (1.0 + g * (1.0 - sigma))).astype(BF)
            both[r, right] = (k * silu).astype(BF)

    each_rows(two.shape[0], gates, 32)

    def tiled_out(left, right, out):
        def body(i, carry):
            cols = pl.ds(pl.multiple_of(i * 256, 256), 256)
            value = dot_nt(left[...], right[cols, :]).astype(BF)
            out[:, :, :, cols] = value.reshape(chain, n_t, rows, 256)
            return carry

        lax.fori_loop(0, width // 256, body, 0)

    tiled_out(both, wgu, npart)
    steps = reduce.steps()
    go(steps, 4)
    gus = Collect(pc, sems, ggu, s_gu, cgu, False)
    dns = Collect(pc, sems, gdn, s_dn, cdn, False)
    grads_into(two, both, ggu)
    gus.send(0, 1)
    go(steps, 1)
    grads_into(cotan, hidden, gdn)
    go(steps, 1)
    gus.send(2)
    go(steps, 1)
    gus.turn(0, 1)
    gus.send(3)
    dns.send()
    run(steps)
    gus.turn(2, 3)
    gain_acc[...] = jnp.zeros_like(gain_acc)

    def back(r):
        grad = norm_back(r, middle[r, :], middle_grad[r, :], gains[1:2, :], cot[r, :].astype(F32), gain_acc)
        middle_grad[r, :] = grad
        branch[r, :] = grad.astype(BF)

    each_rows(rows, back)
    spreading = plane_gather(near, sems, branch, branch_all)
    go(spreading, 2)
    tiled_out(hidden, wdn, opart)
    store = pltpu.make_async_copy(opart, opart_all, local_sem.at[0])
    store.start()
    run(spreading)
    gain_out[...] = jnp.broadcast_to(jnp.sum(gain_acc[...], axis=0, keepdims=True), gain_out.shape)
    dns.turn()
    gus.finish()
    dns.finish()
    store.wait()


def attend_back(pc, query, query_t, dmix, mixed_t, lse, kv, kt, bias, dsum, put, step):
    local, total = query.shape[0], kv.shape[0]
    size = gcd_of(total, 640)
    low, high = key_range(pc.d * local, local, total, size)
    even = jnp.where(halves(), 1.0, 0.0).astype(BF)
    odd = jnp.where(halves(), 0.0, 1.0).astype(BF)
    none = jnp.zeros((64, local), BF)
    for chunk in range(query.shape[1] // 128):
        first = chunk * 128
        lanes = slice(first, first + 128)
        q, dm = query[:, lanes], dmix[:, lanes]
        turned = dm.astype(F32).T
        product = turned * mixed_t[lanes, :]
        turned = turned.astype(BF)
        heads = []
        for k, pick in enumerate((even, odd)):
            at = slice(k * 64, k * 64 + 64)
            heads.append(
                (
                    query_t[first + k * 64 : first + k * 64 + 64, :],
                    jnp.concatenate([none, turned[at, :]], axis=0),
                    q * pick,
                    dm * pick,
                    lse[2 * chunk + k : 2 * chunk + k + 1, :],
                    jnp.sum(product[at, :], axis=0, keepdims=True),
                )
            )

        def body(j, carry):
            rows = pl.ds(pl.multiple_of(j * size, size), size)
            both, key, key_t, mask = kv[rows, :], kv[rows, 0:64], kt[:, rows], bias[rows, :].astype(F32)
            out = []
            dk = jnp.zeros((size, 128), F32)
            dv = jnp.zeros((size, 128), F32)
            for (qt, dmt, qh, dh, top, delta), acc in zip(heads, carry):
                p = jnp.exp(jnp.dot(key, qt, preferred_element_type=F32) + mask - top)
                dp = jnp.dot(both, dmt, preferred_element_type=F32)
                ds = (p * (dp - delta)).astype(BF)
                dk = dk + jnp.dot(ds, qh, preferred_element_type=F32)
                dv = dv + jnp.dot(p.astype(BF), dh, preferred_element_type=F32)
                out.append(acc + jnp.dot(key_t, ds, preferred_element_type=F32))
            dsum[rows, :] += jnp.where(halves(), dk + pltpu.roll(dk, 64, 1), dv + pltpu.roll(dv, 64, 1))
            return tuple(out)

        zero = jnp.zeros((64, local), F32)
        done = lax.fori_loop(low, high, body, (zero, zero))
        put(lanes, jnp.concatenate(done, axis=0).T)
        step()


def low_rows(full, low):
    size = gcd_of(full.shape[0], 256)

    def body(j, carry):
        r = pl.ds(pl.multiple_of(j * size, size), size)
        low[r, :] = full[r, :].astype(BF)
        return carry

    lax.fori_loop(0, full.shape[0] // size, body, 0)


def zero_rows(*refs):
    size = gcd_of(refs[0].shape[0], 256)

    def body(j, carry):
        r = pl.ds(pl.multiple_of(j * size, size), size)
        for ref in refs:
            ref[r, :] = jnp.zeros((size, ref.shape[1]), ref.dtype)
        return carry

    lax.fori_loop(0, refs[0].shape[0] // size, body, 0)


def backward_kernel(chain, *refs):
    kept, branch_all, opart = refs[:10], refs[10], refs[11]
    (lse, tok, middle_grad, gains, gain_two, middle, cosine, sine) = refs[12:20]
    (layer_out, input_grad, qkv_out, kv_out, wout_out, gain_out) = refs[20:26]
    rest = refs[26:]
    (normed, wqkv, wout, query, query_t, kv, kt, bias, mixed_t, mixed_low) = rest[:10]
    (branch_in, held, local_sem) = rest[10:13]
    (dmix, dsum, dkv, dkv_own, dqkv, gwo, gkv, part, osum, gain_acc) = rest[13:23]
    gq = gwo
    rest = rest[23:]
    s_out, s_near = rest[:5], rest[5:10]
    s_gwo, s_gq, s_gkv, s_keys = rest[10:13], rest[13:16], rest[16:19], rest[19:22]
    by_group, stage, mid, second, send, recv = rest[22:]
    sems = Sems(send, recv)
    pc, near = Place(chain), Place(1)
    rows, width = tok.shape
    local, wide = query.shape
    moves = Moves(local_sem)
    inner = (normed, wqkv, wout, query, query_t, kv, kt, bias, mixed_t, mixed_low)
    fetches = {}
    fetches[10] = moves.start(branch_all, branch_in)
    for i in (9, 2):
        fetches[i] = moves.start(kept[i], inner[i])
    halves_of = [
        moves.start(opart.at[:, col], held.at[i]) for i, col in enumerate((pc.sy, pc.s))
    ]
    for i in (7, 5, 6, 3, 4, 8, 0, 1):
        fetches[i] = moves.start(kept[i], inner[i])
    greet(pc)

    def finish():
        yield from PlaneReduce(pc, sems, opart, s_out, osum, held).steps()

        def add(r):
            layer_out[r, :] = (middle[r, :] + osum[r, :]).astype(BF)

        each_rows(rows, add)

    fetches[10].wait()
    fetches[9].wait()
    branch = branch_in
    whole = branch[...]
    grads_into(branch, mixed_low, gwo)
    out_sum = Collect(pc, sems, gwo, s_gwo, wout_out, True)
    out_sum.send()
    laying = finish()
    go(laying, 1)
    for fetch in halves_of:
        fetch.wait()
    fetches[2].wait()
    for at in range(0, wide, 256):
        dmix[:, at : at + 256] = jnp.dot(whole, wout[:, at : at + 256], preferred_element_type=F32).astype(BF)
    zero_rows(dsum)
    for i in (7, 5, 6, 3, 4, 8):
        fetches[i].wait()
    stops = Points(
        [lambda: go(laying, 3)],
        [lambda: go(laying, 1)],
        [out_sum.turn, lambda: go(laying, 1)],
        [lambda: go(laying, 1)],
    )

    def put_query(lanes, value):
        dqkv[:, lanes] = turn(value * 0.125, cosine[...], -sine[...]).astype(BF)

    attend_back(pc, query, query_t, dmix, mixed_t, lse, kv, kt, bias, dsum, put_query, stops)
    stops.drain()
    low_rows(dsum, dkv)
    keys = Collect(pc, sems, dkv, s_keys, dkv_own, True)
    keys.send()
    out_sum.finish()
    fetches[0].wait()
    fetches[1].wait()

    def query_grads(j, carry):
        at = pl.ds(pl.multiple_of(j * 256, 256), 256)
        left = jnp.concatenate([normed[0, s, :, at] for s in range(normed.shape[1])], axis=0)
        gq[at, :] = dot_tn(left, dqkv[:, :wide]).astype(BF)
        return carry

    lax.fori_loop(0, width // 256, query_grads, 0)
    query_sum = Collect(pc, sems, gq, s_gq, qkv_out, True)
    kv_sum = Collect(pc, sems, gkv, s_gkv, kv_out, True)
    keys.turn()
    query_sum.send()
    keys.finish()
    pre = dkv_own[...]
    dqkv[:, wide : wide + 128] = jnp.where(halves(), turn(pre, cosine[...], -sine[...]), pre).astype(BF)

    def put(cols, value):
        for s in range(part.shape[1]):
            part[0, s, :, cols] = value[s * rows : (s + 1) * rows].astype(BF)

    tiled_nt(dqkv[...], wqkv, put)

    def ending():
        yield from plane_reduce(near, sems, part, s_near, input_grad)
        gain_acc[...] = jnp.zeros_like(gain_acc)

        def back(r):
            v = tok[r, :].astype(F32)
            input_grad[r, :] = norm_back(r, v, input_grad[r, :], gains[0:1, :], middle_grad[r, :], gain_acc)

        each_rows(rows, back)
        own = jnp.sum(gain_acc[...], axis=0, keepdims=True)
        row = lax.broadcasted_iota(jnp.int32, (8, 128), 0)
        for j in range(by_group.shape[0]):
            cols = slice(j * 128, (j + 1) * 128)
            by_group[j] = jnp.where(row == 0, jnp.broadcast_to(own[:, cols], (8, 128)), gain_two[:, cols])
        yield from sum_gains(pc, sems, by_group, stage, mid, second, gain_out)

    end = ending()
    go(end, 1)

    def key_grads(j, carry):
        at = pl.ds(pl.multiple_of(j * 256, 256), 256)
        left = jnp.concatenate([normed[0, s, :, at] for s in range(normed.shape[1])], axis=0)
        gkv[at, :] = dot_tn(left, dqkv[:, wide : wide + 128]).astype(BF)
        return carry

    lax.fori_loop(0, width // 256, key_grads, 0)
    kv_sum.send()
    query_sum.turn(0, 1)
    go(end, 5)
    query_sum.turn(2, 3)
    kv_sum.turn()
    run(end)
    run(laying)
    query_sum.finish()
    kv_sum.finish()


def shards(
    tokens,
    segment_ids,
    key_mask,
    attn_gain,
    w_query,
    w_key,
    w_value,
    w_out,
    mlp_gain,
    w_gate,
    w_up,
    w_down,
    cotangent,
):
    n_dp, n_t = lax.axis_size("dp"), lax.axis_size("tensor")
    chain = 4
    groups = n_dp // chain
    rows, width = tokens.shape
    local = rows * n_t
    total = local * n_dp
    dim = w_key.shape[1]
    heads = w_query.shape[1] // dim
    wrows = w_query.shape[0]
    units = w_gate.shape[1] // chain
    qkv = w_query.shape[1] + 2 * dim
    me = lax.axis_index("dp")
    share = attn_gain.shape[0]
    tile = 128 // share

    first_row = me * local
    own_gain = jnp.concatenate(
        [
            jnp.tile(attn_gain, tile)[None],
            jnp.tile(mlp_gain, tile)[None],
            jnp.zeros((6, 128), F32),
        ],
        axis=0,
    )
    wqkv = jnp.concatenate([w_query, w_key, w_value], axis=1)
    wout = w_out.T

    held = (units + 127) // 128 * 128

    def by_chain(w):
        w = jnp.pad(w.reshape(wrows, chain, units), ((0, 0), (0, 0), (0, held - units)))
        return w.transpose(1, 0, 2)

    plane = chain * n_t * rows
    nbytes = 60 << 20
    positions = first_row + jnp.arange(local, dtype=jnp.int32)
    lane = jnp.arange(128, dtype=jnp.int32)
    frequency = THETA ** (-(lane % (dim // 2)).astype(F32) / (dim // 2))
    turned = positions.astype(F32)[:, None] * frequency[None, :]
    cosine = jnp.cos(turned)
    sine = jnp.sin(turned) * jnp.where(lane % dim < dim // 2, -1.0, 1.0)
    own_segments = lax.dynamic_slice(segment_ids, (first_row,), (local,))
    wide = heads * dim
    saved = [
        ((1, n_t, rows, width), BF),
        ((width, qkv), BF),
        ((width, wide), BF),
        ((local, wide), BF),
        ((wide, local), BF),
        ((total, 128), BF),
        ((64, total), BF),
        ((total, local), BF),
        ((wide, local), F32),
        ((local, wide), BF),
    ]
    (gains, wgu, wdn, cot, lse, middle, two, *kept) = call(
        functools.partial(forward_kernel, chain),
        "forward",
        0,
        [VM, VM] + [ANY] * 6 + [VM] * 4,
        [
            ((8, width), F32, VM),
            ((width, 2 * held), BF, ANY),
            ((width, held), BF, ANY),
            ((chain, n_t, rows, width), BF, ANY),
            ((heads, local), F32, VM),
            ((rows, width), F32, VM),
            ((chain, n_t, rows, width), BF, ANY),
        ]
        + [(shape, kind, ANY) for shape, kind in saved],
        [pltpu.VMEM(shape, kind) for shape, kind in saved]
        + [
            pltpu.VMEM((n_dp, n_t, 8, 128), F32),
            pltpu.VMEM((rows, width), BF),
            pltpu.VMEM((local, 2 * dim), BF),
            pltpu.VMEM((80, total), BF),
            pltpu.VMEM((1, n_t, rows, width), BF),
            pltpu.VMEM((rows, width), F32),
            pltpu.VMEM((rows, width), BF),
            pltpu.SemaphoreType.DMA((10,)),
        ]
        + plane_scratch(1, rows, width),
        (
            tokens,
            own_gain,
            wqkv,
            wout,
            by_chain(w_gate),
            by_chain(w_up),
            by_chain(w_down.T),
            cotangent,
            cosine,
            sine,
            own_segments[:, None] * 2 + 1,
            (segment_ids * 2 + key_mask)[None],
        ),
        nbytes,
    )
    (opart, middle_grad, branch, gain_two, ggu, gdn) = call(
        functools.partial(feed_kernel, chain),
        "feed",
        1,
        [ANY] * 4 + [VM] * 3,
        [
            ((chain, n_t, rows, width), BF, ANY),
            ((rows, width), F32, VM),
            ((1, n_t, rows, width), BF, ANY),
            ((8, width), F32, VM),
            ((chain, wrows, 2 * held), BF, ANY),
            ((chain, wrows, held), BF, ANY),
        ],
        [
            pltpu.VMEM((plane, width), BF),
            pltpu.VMEM((plane, width), BF),
            pltpu.VMEM((width, 2 * held), BF),
            pltpu.VMEM((width, held), BF),
            pltpu.VMEM((chain, n_t, rows, width), BF),
            pltpu.VMEM((plane, 2 * held), F32),
            pltpu.VMEM((plane, held), F32),
            pltpu.VMEM((plane, 2 * held), BF),
            pltpu.VMEM((plane, held), BF),
            pltpu.VMEM((chain, n_t, rows, width), BF),
            pltpu.VMEM((width, 2 * held), BF),
            pltpu.VMEM((width, held), BF),
        ]
        + plane_scratch(chain, rows, width)
        + collect_scratch(chain, groups, wrows, 2 * held)
        + collect_scratch(chain, groups, wrows, held)
        + [
            pltpu.VMEM((rows, width), BF),
            pltpu.VMEM((16, width), F32),
            pltpu.SemaphoreType.DMA((4,)),
        ],
        (two.reshape(plane, width), cot.reshape(plane, width), wgu, wdn, middle, cotangent, gains),
        nbytes,
    )

    def shard_of(g):
        return jnp.concatenate([g[z, :, :units].astype(F32) for z in range(chain)], axis=1)

    grad_gate, grad_up, grad_down = shard_of(ggu), shard_of(ggu[:, :, held:]), shard_of(gdn).T

    count = max(1, n_t * share // 128)
    layer_out, input_grad, gq, gkv, gwout, gain_sum = call(
        functools.partial(backward_kernel, chain),
        "backward",
        2,
        [ANY] * 12 + [VM] * 8,
        [
            ((rows, width), BF, VM),
            ((rows, width), F32, VM),
            ((wrows, wide), F32, VM),
            ((wrows, 2 * dim), F32, VM),
            ((wrows, wide), F32, VM),
            ((8, 128), F32, VM),
        ],
        [pltpu.VMEM(shape, kind) for shape, kind in saved]
        + [
            pltpu.VMEM((local, width), BF),
            pltpu.VMEM((2, chain, rows, width), BF),
            pltpu.SemaphoreType.DMA((13,)),
            pltpu.VMEM((local, wide), BF),
            pltpu.VMEM((total, 128), F32),
            pltpu.VMEM((total, 128), BF),
            pltpu.VMEM((local, 128), F32),
            pltpu.VMEM((local, qkv), BF),
            pltpu.VMEM((width, wide), BF),
            pltpu.VMEM((width, 128), BF),
            pltpu.VMEM((1, n_t, rows, width), BF),
            pltpu.VMEM((rows, width), F32),
            pltpu.VMEM((16, width), F32),
        ]
        + plane_scratch(chain, rows, width)
        + plane_scratch(1, rows, width)
        + dp_scratch(chain, groups, wrows, wide)
        + dp_scratch(chain, groups, wrows, wide)
        + dp_scratch(chain, groups, wrows, 128)
        + dp_scratch(chain, groups, local, 128)
        + [
            pltpu.VMEM((width // 128, 8, 128), F32),
            pltpu.VMEM((n_dp, count, 8, 128), F32),
            pltpu.VMEM((count, 8, 128), F32),
            pltpu.VMEM((n_t, 8, 128), F32),
        ],
        (
            *kept,
            branch.reshape(local, width),
            opart,
            lse,
            tokens,
            middle_grad,
            gains,
            gain_two,
            middle,
            cosine,
            sine,
        ),
        nbytes,
    )
    lane = (me * n_t + lax.axis_index("tensor")) * share % 128
    gain_grads = lax.dynamic_slice(gain_sum, (0, lane), (2, share))
    return (
        layer_out,
        input_grad,
        gain_grads[0],
        gq,
        gkv[:, :dim],
        gkv[:, dim:],
        gwout.T,
        gain_grads[1],
        grad_gate,
        grad_up,
        grad_down,
    )


def solution(mesh):
    in_specs = (
        P(("dp", "tensor"), None),
        P(),
        P(),
        P(("dp", "tensor")),
        P("dp", "tensor"),
        P("dp", "tensor"),
        P("dp", "tensor"),
        P("tensor", "dp"),
        P(("dp", "tensor")),
        P("dp", "tensor"),
        P("dp", "tensor"),
        P("tensor", "dp"),
        P(("dp", "tensor"), None),
    )
    out_specs = (
        P(("dp", "tensor"), None),
        P(("dp", "tensor"), None),
        P(("dp", "tensor")),
        P("dp", "tensor"),
        P("dp", "tensor"),
        P("dp", "tensor"),
        P("tensor", "dp"),
        P(("dp", "tensor")),
        P("dp", "tensor"),
        P("dp", "tensor"),
        P("tensor", "dp"),
    )
    return jax.shard_map(shards, mesh=mesh, in_specs=in_specs, out_specs=out_specs, check_vma=False)
```
